32 devices in a mesh: gx: 16 (over z, y, core), gy: 2 (over x).
Axes of the slice: x: 2, y: 2, z: 4, core: 2. Of those that a mesh axis runs over, the one named last changes fastest.
Arguments:
- loads: float32 [8, 2, 16384], P(None, 'gy', 'gx'), may hold values from -6 to 6
- dual_op: bfloat16 [2, 16384, 1024], P('gy', 'gx')
- iface: int32 [2, 16, 1024], P('gy', 'gx'), may hold values from 0 to 1023, each once within a row
- precond: float32 [2, 16384], P('gy', 'gx'), may hold values from 0.3 to 3
- corner_map: float32 [2, 128, 16384], P('gy', None, 'gx'), may hold values from -0.25 to 0.25
- coarse_inv: float32 [128, 128], replicated
- elem_stiff: float32 [8, 8], replicated
- elem_dofs: int32 [8, 1024, 256], P(None, 'gx', 'gy'), may hold values from 0 to 1023
- density: float32 [1024, 256], P('gx', 'gy'), may hold values from 0.1 to 1
- passive: int32 [1024, 256], P('gx', 'gy'), may hold values 0 or 1
Outputs:
- adjoint: float32 [8, 2, 16384], P(None, 'gy', 'gx')
- sens: float32 [1024, 256], P('gx', 'gy')
The draws below stay inside these ranges and needn't reach their ends.
All inputs are finite; a program needn't handle non-finite values. No bound on the sum of `passive` on one device may be relied on, other than what follows from the above.
Results may differ from the reference program's by a relative error of at most 0.00052.
Values sent between devices are 32-bit elements; how exact they have to be, the bound alone decides.
No kernel may reach another device: no remote copies, remote signals or barrier semaphores. Data moves between devices by JAX's collectives and lax.ppermute only.
A program may use at most 128 MiB of HBM per device.

```python
import math
import jax
import jax.numpy as jnp
from jax import lax

M = 1024
R = 128
NCG = 128
CASES = 8
ITERS = 2
SWEEPS = 3
EX = 64
EY = 128
EXG = 1024
EYG = 256
MX = 16384
N_GX = 16
N_GY = 2


def draw_dual_op(key, part):
    first, second = jax.random.split(jax.random.fold_in(key, 11))
    width = 0.4 * 6.0 ** 0.5 / M ** 0.5
    raw = jax.random.uniform(first, (N_GY, N_GX, M, M), jnp.float32, -width, width)
    sym = 0.5 * (raw + jnp.swapaxes(raw, -1, -2))
    diag = jax.random.uniform(second, (N_GY, N_GX, M), jnp.float32, 1.6, 3.0)
    eye = jnp.eye(M, dtype=jnp.float32)
    full = sym * (1.0 - eye) + diag[..., None] * eye
    return full.reshape(N_GY, N_GX * M, M).astype(jnp.bfloat16)


def draw_coarse_inv(key, part):
    first, second = jax.random.split(jax.random.fold_in(key, 23))
    width = 0.4 * 6.0 ** 0.5 / NCG ** 0.5
    raw = jax.random.uniform(first, (NCG, NCG), jnp.float32, -width, width)
    sym = 0.5 * (raw + raw.T)
    diag = jax.random.uniform(second, (NCG,), jnp.float32, 1.0, 2.0)
    eye = jnp.eye(NCG, dtype=jnp.float32)
    return sym * (1.0 - eye) + diag[:, None] * eye


def draw_elem_stiff(key, part):
    first, second = jax.random.split(jax.random.fold_in(key, 37))
    raw = jax.random.uniform(first, (8, 8), jnp.float32, -0.2, 0.2)
    sym = 0.5 * (raw + raw.T)
    diag = jax.random.uniform(second, (8,), jnp.float32, 1.5, 2.5)
    eye = jnp.eye(8, dtype=jnp.float32)
    return sym * (1.0 - eye) + diag[:, None] * eye


def touch_ends(entries, rng, least, high):
    longest = entries.shape.index(max(entries.shape))
    spots = []
    for shift in (0, 1):
        where = [jax.random.randint(jax.random.fold_in(rng, axis), (), 0, length) for axis, length in enumerate(entries.shape)]
        where[longest] = (where[longest] + shift) % entries.shape[longest]
        spots.append(tuple(where))
    return entries.at[spots[0]].set(least).at[spots[1]].set(high)


def shard_levels(rng, shape, cuts, low, largest):
    loudness = 1.0
    for dim, blocks in cuts:
        draws = jax.random.uniform(jax.random.fold_in(jax.random.fold_in(rng, 6), dim), (blocks,), jnp.float32, low / len(cuts), largest / len(cuts))
        loudness = loudness * jnp.repeat(jnp.exp(draws), shape[dim] // blocks).reshape((-1,) + (1,) * (len(shape) - 1 - dim))
    return loudness


def noise(rng, dims, scale, limit, cuts=(), held_as=jnp.bfloat16):
    array = jax.random.normal(rng, dims, jnp.float32) * scale
    if len(cuts) > 0:
        array = shard_levels(rng, dims, cuts, -0.22, 0.18) * array
    return jnp.clip(array, min=-limit, max=limit).astype(held_as)


def setup_inputs(seed: int = 0) -> dict:
    arg_keys = jax.random.split(jax.random.key(seed), 11)
    return {
        "loads": noise(arg_keys[0], (CASES, N_GY, MX), 1.0, 6.0, ((1, 2), (2, 16)), jnp.float32),
        "dual_op": draw_dual_op(jax.random.fold_in(arg_keys[10], 71), 0),
        "iface": jax.vmap(lambda own: jax.random.permutation(own, M))(jax.random.split(arg_keys[2], N_GY * N_GX)).reshape((N_GY, N_GX, M)).astype(jnp.int32),
        "precond": jnp.clip(jnp.exp(math.log(3.0) - 2.3025851 * jax.random.uniform(arg_keys[3], (N_GY, MX), jnp.float32) ** shard_levels(arg_keys[3], (N_GY, MX), ((0, 2), (1, 16)), -0.2, 0.2)), 0.3, 3.0),
        "corner_map": noise(arg_keys[4], (N_GY, NCG, MX), (0.8 * (M * N_GX * N_GY * NCG) ** -0.25), 0.25, ((0, 2), (2, 16)), jnp.float32),
        "coarse_inv": draw_coarse_inv(jax.random.fold_in(arg_keys[10], 71), 0),
        "elem_stiff": draw_elem_stiff(jax.random.fold_in(arg_keys[10], 71), 0),
        "elem_dofs": touch_ends(jax.random.randint(arg_keys[7], (8, EXG, EYG), 0, M), jax.random.fold_in(arg_keys[7], 1), 0, M - 1).astype(jnp.int32),
        "density": jnp.clip(0.1 + 0.9 * jax.random.uniform(arg_keys[8], (EXG, EYG), jnp.float32) ** shard_levels(arg_keys[8], (EXG, EYG), ((0, 16), (1, 2)), -0.2, 0.2), 0.1, 1.0),
        "passive": touch_ends((jax.random.randint(arg_keys[9], (EXG, EYG), 0, 8) < 1).astype(jnp.int32), jax.random.fold_in(arg_keys[9], 1), 0, 1),
    }


coupling = 0.3
radius_sq = 2.0
penalty = 3.0


def scatter_rows(vals, idx):
    return jnp.zeros((M,), jnp.float32).at[idx].add(vals)


def reference(loads, dual_op, iface, precond, corner_map, coarse_inv, elem_stiff, elem_dofs, density, passive):
    hi = lax.Precision.HIGHEST
    ops = dual_op.reshape(N_GY, N_GX, M, M)
    left_idx = iface[:, :, :R]
    right_idx = iface[:, :, R:2 * R]
    left_b = jnp.broadcast_to(left_idx[None], (CASES, N_GY, N_GX, R))
    right_b = jnp.broadcast_to(right_idx[None], (CASES, N_GY, N_GX, R))
    corners = corner_map.reshape(N_GY, NCG, N_GX, M)
    pre = precond.reshape(N_GY, N_GX, M)[None]
    scat = jax.vmap(jax.vmap(jax.vmap(scatter_rows)))

    def apply_dual(vec):
        vb = vec.astype(jnp.bfloat16)
        local = lax.map(lambda a: jnp.einsum('xmk,cxk->cxm', a[0].astype(jnp.float32), a[1].astype(jnp.float32), precision=hi), (ops, jnp.moveaxis(vb, 1, 0)))
        local = jnp.moveaxis(local, 0, 1)
        right_vals = jnp.take_along_axis(vec, right_b, axis=-1)
        left_vals = jnp.take_along_axis(vec, left_b, axis=-1)
        from_lower = jnp.pad(right_vals, ((0, 0), (0, 0), (1, 0), (0, 0)))[:, :, :-1]
        from_upper = jnp.pad(left_vals, ((0, 0), (0, 0), (0, 1), (0, 0)))[:, :, 1:]
        out = local + scat(-coupling * from_lower, left_b) + scat(-coupling * from_upper, right_b)
        csum = jnp.einsum('yjxm,cyxm->cj', corners, vec, precision=hi)
        zc = jnp.dot(csum, coarse_inv.T, precision=hi)
        return out + jnp.einsum('cj,yjxm->cyxm', zc, corners, precision=hi)

    def inner(a, b):
        return jnp.sum(a * b, axis=(1, 2, 3))[:, None, None, None]

    resid = loads.reshape(CASES, N_GY, N_GX, M)
    adjoint = jnp.zeros_like(resid)
    z = pre * resid
    p = z
    rz = inner(resid, z)
    for step in range(ITERS):
        q = apply_dual(p)
        alpha = rz / inner(p, q)
        adjoint = adjoint + alpha * p
        resid = resid - alpha * q
        if step + 1 < ITERS:
            z = pre * resid
            rz_new = inner(resid, z)
            p = z + (rz_new / rz) * p
            rz = rz_new

    lam_t = jnp.transpose(adjoint, (2, 1, 0, 3))
    idx_blocks = jnp.transpose(elem_dofs.reshape(8, N_GX, EX, N_GY, EY), (1, 3, 0, 2, 4))

    def energy_one(lv, ib):
        u = lv[:, ib]
        v = jnp.einsum('ab,cbxy->caxy', elem_stiff, u, precision=hi)
        return jnp.sum(u * v, axis=(0, 1))

    energy = lax.map(lambda a: jax.vmap(energy_one)(a[0], a[1]), (lam_t, idx_blocks))
    energy = jnp.transpose(energy, (0, 2, 1, 3)).reshape(EXG, EYG)
    grad = jnp.where(passive == 1, 0.0, -penalty * density * density * energy)
    diag = 1.0 + 4.0 * radius_sq
    smooth = grad / diag
    for sweep in range(SWEEPS - 1):
        padded = jnp.pad(smooth, 1)
        beside = padded[2:, 1:-1] + padded[:-2, 1:-1] + padded[1:-1, 2:] + padded[1:-1, :-2]
        smooth = (grad + radius_sq * beside) / diag
    return adjoint.reshape(CASES, N_GY, MX), smooth
```

```python
import jax
import jax.numpy as jnp
from jax import lax
from jax.experimental import pallas as pl
from jax.experimental.pallas import tpu as pltpu
from jax.sharding import PartitionSpec as P

R = 128
LANES = 128
CASES = 8
CORNERS = 4

coupling = 0.3
radius_sq = 2.0
penalty = 3.0
diag = 1.0 + 4.0 * radius_sq

HI = lax.Precision.HIGHEST
F32 = jnp.float32
BF16 = jnp.bfloat16
VMEM = pl.BlockSpec(memory_space=pltpu.VMEM)
SMEM = pl.BlockSpec(memory_space=pltpu.SMEM)

SIDE_P, SIDE_Y, SIDE_M, SIDE_C = 0, 8, 16, 24
RZ, PQ, QMQ, TLT, PE, TE = range(6)


def rows_dot(a, b):
    return lax.dot_general(a, b, (((1,), (1,)), ((), ())), precision=HI, preferred_element_type=F32)


def plain_dot(a, b):
    return lax.dot_general(a, b, (((1,), (0,)), ((), ())), precision=HI, preferred_element_type=F32)


def halves(x):
    high = x.astype(BF16)
    low = (x - high.astype(F32)).astype(BF16)
    return jnp.concatenate([high, low], axis=0)


def lane_sum(x):
    return jnp.sum(x, axis=1, keepdims=True)


def pattern(idx):
    return idx & (LANES - 1), (idx & 128) != 0, (idx & 256) != 0, (idx & 512) != 0


def pick(blocks, where):
    lane, bit0, bit1, bit2 = where
    got = [jnp.take_along_axis(b, lane, axis=1, mode="promise_in_bounds") for b in blocks]
    got = [jnp.where(bit0, got[2 * i + 1], got[2 * i]) for i in range(4)]
    got = [jnp.where(bit1, got[2 * i + 1], got[2 * i]) for i in range(2)]
    return jnp.where(bit2, got[1], got[0])


def blocks_of(row8):
    return [row8[:, LANES * h : LANES * (h + 1)] for h in range(8)]


def first_kernel(loads_ref, pre_ref, corner_ref, send_ref, p_ref):
    p = pre_ref[...] * loads_ref[:, 0, :]
    p_ref[...] = p
    part = rows_dot(p, corner_ref[0])
    for d in range(send_ref.shape[0]):
        send_ref[d] = part


def side_kernel(odd_ref, p_ref, op_ref, iface_ref, pre_ref, corner_ref,
                y_ref, rest_ref, even_ref, oddp_ref, hot_ref):
    p = p_ref[...]
    both = lax.dot_general(halves(p), op_ref[0], (((1,), (1,)), ((), ())), preferred_element_type=F32)
    y = both[:CASES]
    y_ref[...] = y
    rest_ref[...] = both[CASES:]
    pre = jnp.broadcast_to(pre_ref[...], (8, pre_ref.shape[1]))
    left = iface_ref[0, :, :R]
    right = iface_ref[0, :, R : 2 * R]
    odd = jnp.broadcast_to(odd_ref[0] != 0, (1, R))
    for side, (idx, out) in enumerate(((jnp.where(odd, left, right), even_ref),
                                       (jnp.where(odd, right, left), oddp_ref))):
        where = pattern(jnp.broadcast_to(idx, (8, R)))
        scale = pick(blocks_of(pre), where)
        out[SIDE_P : SIDE_P + 8] = pick(blocks_of(p), where)
        out[SIDE_Y : SIDE_Y + 8] = scale * pick(blocks_of(y), where)
        out[SIDE_M : SIDE_M + 8] = scale
        for j in range(corner_ref.shape[1] // 8):
            rows = corner_ref[0, 8 * j : 8 * j + 8]
            out[SIDE_C + 8 * j : SIDE_C + 8 * j + 8] = scale * pick(blocks_of(rows), where)
        column = jnp.transpose(jnp.broadcast_to(idx, (R, R)))
        for h in range(8):
            at = lax.broadcasted_iota(jnp.int32, (R, LANES), 1) + LANES * h
            hot_ref[side, :, LANES * h : LANES * (h + 1)] = jnp.where(column == at, 1.0, 0.0).astype(BF16)


def spread(values, hot):
    high = values.astype(BF16)
    rest = values - high.astype(F32)
    mid = rest.astype(BF16)
    low = (rest - mid.astype(F32)).astype(BF16)
    parts = jnp.concatenate([high, mid, low, jnp.zeros_like(low)], axis=0)
    got = lax.dot_general(parts, hot, (((1,), (0,)), ((), ())), preferred_element_type=F32)
    return got[:8] + got[8:16] + got[16:24]


def second_kernel(got_ref, coarse_ref, loads_ref, p_ref, y_ref, rest_ref, pre_ref, corner_ref, op_ref,
                  mine_e_ref, mine_o_ref, theirs_e_ref, theirs_o_ref, hot_ref,
                  send_ref, t_ref):
    total = got_ref[0]
    for d in range(1, got_ref.shape[0]):
        total = total + got_ref[d]
    w = rows_dot(total, coarse_ref[...])
    p = p_ref[...]
    q = y_ref[...] + plain_dot(w, corner_ref[0])
    tlt = None
    for side, (mine, theirs) in enumerate(((mine_e_ref, theirs_e_ref), (mine_o_ref, theirs_o_ref))):
        p_mine, p_theirs = mine[SIDE_P : SIDE_P + 8], theirs[SIDE_P : SIDE_P + 8]
        q = q + spread(-coupling * p_theirs, hot_ref[side])
        t_mine = mine[SIDE_Y : SIDE_Y + 8] - coupling * mine[SIDE_M : SIDE_M + 8] * p_theirs
        t_mine = t_mine + plain_dot(w, mine[SIDE_C:])
        t_theirs = theirs[SIDE_Y : SIDE_Y + 8] - coupling * theirs[SIDE_M : SIDE_M + 8] * p_mine
        t_theirs = t_theirs + plain_dot(w, theirs[SIDE_C:])
        term = -coupling * lane_sum(t_mine * t_theirs)
        tlt = term if tlt is None else tlt + term
    t = pre_ref[...] * q
    t_ref[...] = t
    both = lax.dot_general(halves(t), op_ref[0], (((1,), (1,)), ((), ())), preferred_element_type=F32)
    tlt = tlt + lane_sum(t * (both[:CASES] + both[CASES:]))
    g = rows_dot(t, corner_ref[0])
    rest = rest_ref[...]
    scalars = (lane_sum(loads_ref[:, 0, :] * p), lane_sum(p * q), lane_sum(q * t), tlt,
               lane_sum(p * rest), lane_sum(t * rest))
    lane = lax.broadcasted_iota(jnp.int32, (CASES, LANES), 1)
    block = jnp.zeros((CASES, LANES), F32)
    for j, s in enumerate(scalars):
        block = jnp.where(lane == j, s, block)
    for d in range(send_ref.shape[0]):
        send_ref[d, :CASES] = g
        send_ref[d, CASES:] = block


def make_table(table_ref, adj):
    for c in range(CASES):
        for h in range(8):
            table_ref[c, h] = jnp.broadcast_to(adj[c : c + 1, LANES * h : LANES * (h + 1)], (8, LANES))


def tile_energy(dofs, stiff_ref, table_ref, u_ref):
    for a in range(8):
        where = pattern(dofs(a))
        for c in range(CASES):
            u_ref[a, c] = pick([table_ref[c, h] for h in range(8)], where)
    total = None
    for c in range(CASES):
        u = [u_ref[a, c] for a in range(8)]
        for a in range(8):
            v = stiff_ref[a, 0] * u[0]
            for b in range(1, 8):
                v = v + stiff_ref[a, b] * u[b]
            total = u[a] * v if total is None else total + u[a] * v
    return total


def adjoint_kernel(stiff_ref, got_ref, coarse_ref, p_ref, t_ref, pack_ref, wpack_ref,
                   out_ref, adj_ref, edge_ref, table_ref, u_ref):
    total = got_ref[0]
    for d in range(1, got_ref.shape[0]):
        total = total + got_ref[d]
    g, s = total[:CASES], total[CASES:]
    rz, pq, qmq, tlt, pe, te = (s[:, j : j + 1] for j in (RZ, PQ, QMQ, TLT, PE, TE))
    tat = tlt + lane_sum(g * rows_dot(g, coarse_ref[...]))
    alpha = rz / pq
    rz_next = rz - 2.0 * alpha * pq + alpha * alpha * qmq
    grow = 1.0 + rz_next / rz
    pap = grow * grow * (pq + pe) - 2.0 * alpha * grow * (qmq + te) + alpha * alpha * tat
    alpha_next = rz_next / pap
    adj = (alpha + alpha_next * grow) * p_ref[...] - (alpha * alpha_next) * t_ref[...]
    out_ref[:, 0, :] = adj
    adj_ref[...] = adj
    make_table(table_ref, adj)
    edge_ref[...] = wpack_ref[...] * tile_energy(lambda a: pack_ref[a], stiff_ref, table_ref, u_ref)


def energy_kernel(stiff_ref, adj_ref, dofs_ref, density_ref, passive_ref, grad_ref, table_ref, u_ref):
    make_table(table_ref, adj_ref[...])

    @pl.loop(0, grad_ref.shape[0] // 8)
    def _(tile):
        rows = pl.ds(pl.multiple_of(8 * tile, 8), 8)
        energy = tile_energy(lambda a: dofs_ref[a, rows, :], stiff_ref, table_ref, u_ref)
        rho = density_ref[rows, :]
        grad_ref[rows, :] = jnp.where(passive_ref[rows, :] == 1, 0.0, -penalty * rho * rho * energy)


def filter_kernel(place_ref, grad_ref, mine_ref, xe_ref, xo_ref, ye_ref, yo_ref,
                  ee_ref, eo_ref, oe_ref, oo_ref, out_ref):
    grad = grad_ref[...]
    ex, ey = grad.shape
    x_odd, y_odd = place_ref[0] != 0, place_ref[1] != 0
    has = [jnp.where(place_ref[2 + i] != 0, 1.0, 0.0) for i in range(4)]

    def choose(flag, a, b):
        return jnp.where(jnp.broadcast_to(flag, a.shape), a, b)

    xe, xo, ye, yo = xe_ref[...], xo_ref[...], ye_ref[...], yo_ref[...]
    below, above = choose(x_odd, xe, xo), choose(x_odd, xo, xe)
    before, after = choose(y_odd, ye, yo), choose(y_odd, yo, ye)
    ee, eo, oe, oo = ee_ref[...], eo_ref[...], oe_ref[...], oo_ref[...]
    diag_ye = (choose(x_odd, ee, oe), choose(x_odd, oe, ee))
    diag_yo = (choose(x_odd, eo, oo), choose(x_odd, oo, eo))
    below_before, below_after = (choose(y_odd, diag_ye[0], diag_yo[0]), choose(y_odd, diag_yo[0], diag_ye[0]))
    above_before, above_after = (choose(y_odd, diag_ye[1], diag_yo[1]), choose(y_odd, diag_yo[1], diag_ye[1]))
    mine = mine_ref[...]
    last = LANES - 1
    corner = [
        below_before[3:4, last:] / diag, below_after[3:4, :1] / diag,
        above_before[0:1, last:] / diag, above_after[0:1, :1] / diag,
    ]
    lane = lax.broadcasted_iota(jnp.int32, (1, LANES), 1)

    def shifted(row, low, high, length):
        left = jnp.where(lane == 0, low, pltpu.roll(row, 1, 1))
        right = jnp.where(lane == length - 1, high, pltpu.roll(row, LANES - 1, 1))
        return left + right

    def half(row, second):
        return pltpu.roll(row, LANES - ex, 1) if second else row

    g_before1, g_before2 = half(before[5:6], True), half(before[5:6], False)
    g_after1, g_after2 = half(after[4:5], False), half(after[4:5], True)
    col_first, col_last = half(mine[4:5], False), half(mine[5:6], True)
    g_below1, g_below2 = below[3:4], below[2:3]
    g_above1, g_above2 = above[0:1], above[1:2]
    s_below1, s_above1 = g_below1 / diag, g_above1 / diag
    s_before1, s_after1 = g_before1 / diag, g_after1 / diag

    def ring(g1, s2, inner, beside, there):
        return there * (g1 + radius_sq * (s2 + inner + beside)) / diag

    def at(row, j):
        return row[:, j : j + 1]

    n_below = ring(g_below1, g_below2 / diag, mine[0:1] / diag,
                   shifted(s_below1, corner[0], corner[1], ey), has[0])
    n_above = ring(g_above1, g_above2 / diag, mine[3:4] / diag,
                   shifted(s_above1, corner[2], corner[3], ey), has[1])
    n_before = ring(g_before1, g_before2 / diag, col_first / diag,
                    shifted(s_before1, corner[0], corner[2], ex), has[2])
    n_after = ring(g_after1, g_after2 / diag, col_last / diag,
                   shifted(s_after1, corner[1], corner[3], ex), has[3])
    stack = jnp.concatenate([s_before1, s_after1, n_before, n_after, jnp.zeros((4, LANES), F32)], axis=0)
    columns = jnp.transpose(stack)[:ex]
    row_no = lax.broadcasted_iota(jnp.int32, (ex, ey), 0)
    col_no = lax.broadcasted_iota(jnp.int32, (ex, ey), 1)

    def sweep(s, below_row, above_row, before_col, after_col):
        down = jnp.where(row_no == 0, below_row, pltpu.roll(s, 1, 0))
        up = jnp.where(row_no == ex - 1, above_row, pltpu.roll(s, ex - 1, 0))
        left = jnp.where(col_no == 0, before_col, pltpu.roll(s, 1, 1))
        right = jnp.where(col_no == ey - 1, after_col, pltpu.roll(s, ey - 1, 1))
        return (grad + radius_sq * (up + down + right + left)) / diag

    s = grad / diag
    s = sweep(s, s_below1, s_above1, columns[:, 0:1], columns[:, 1:2])
    out_ref[...] = sweep(s, n_below, n_above, columns[:, 2:3], columns[:, 3:4])


def swaps(size):
    out = []
    for first in (0, 1):
        pairs = [(i, i + 1) for i in range(first, size - 1, 2)]
        out.append(pairs + [(j, i) for i, j in pairs])
    return out


def swap_over(array, axis, pairs):
    return lax.ppermute(array, axis, pairs) if pairs else jnp.zeros_like(array)


def f32(*shape):
    return jax.ShapeDtypeStruct(shape, F32)


def cost(flops, moved):
    return pl.CostEstimate(flops=flops, bytes_accessed=moved, transcendentals=0)


def params():
    return pltpu.CompilerParams(vmem_limit_bytes=24 * 1024 * 1024)


def edge_pack(array):
    ex, ey = array.shape[-2:]
    rows = jnp.concatenate([array[..., :2, :], array[..., ex - 2 :, :]], axis=-2)
    cols = jnp.concatenate([array[..., :2], array[..., ey - 2 :]], axis=-1)
    cols = jnp.swapaxes(cols, -1, -2).reshape(array.shape[:-2] + (4 * ex // LANES, LANES))
    pad = jnp.zeros(array.shape[:-2] + (8 - rows.shape[-2] - cols.shape[-2], LANES), array.dtype)
    return jnp.concatenate([rows, cols, pad], axis=-2)


def on_device(loads, dual_op, iface, precond, corner_map, coarse_inv, elem_stiff, elem_dofs, density, passive):
    nx, ny = lax.axis_size("gx"), lax.axis_size("gy")
    everyone = nx * ny
    unknowns = dual_op.shape[-1]
    modes = corner_map.shape[1]
    ex, ey = density.shape
    x, y = lax.axis_index("gx"), lax.axis_index("gy")
    place = jnp.stack([x % 2, y % 2, x > 0, x < nx - 1, y > 0, y < ny - 1]).astype(jnp.int32)
    x_even, x_odd = swaps(nx)
    y_even, y_odd = swaps(ny)

    send, p = pl.pallas_call(
        first_kernel, out_shape=(f32(everyone, CASES, modes), f32(CASES, unknowns)),
        in_specs=[VMEM] * 3, out_specs=(VMEM, VMEM), compiler_params=params(), name="first",
    )(loads, precond, corner_map)
    got = lax.all_to_all(send, ("gx", "gy"), 0, 0)

    side = f32(SIDE_C + modes, R)
    yloc, rest, mine_e, mine_o, hot = pl.pallas_call(
        side_kernel,
        out_shape=(f32(CASES, unknowns), f32(CASES, unknowns), side, side,
                   jax.ShapeDtypeStruct((2, R, unknowns), BF16)),
        in_specs=[SMEM] + [VMEM] * 5, out_specs=(VMEM,) * 5, compiler_params=params(), name="sides",
        cost_estimate=cost(40_000_000, 4_000_000),
    )(place, p, dual_op, iface, precond, corner_map)
    theirs_e = swap_over(mine_e, "gx", x_even)
    theirs_o = swap_over(mine_o, "gx", x_odd)

    send, t = pl.pallas_call(
        second_kernel, out_shape=(f32(everyone, 2 * CASES, modes), f32(CASES, unknowns)),
        in_specs=[VMEM] * 14, out_specs=(VMEM, VMEM), compiler_params=params(), name="second",
    )(got, coarse_inv, loads, p, yloc, rest, precond, corner_map, dual_op,
      mine_e, mine_o, theirs_e, theirs_o, hot)
    got = lax.all_to_all(send, ("gx", "gy"), 0, 0)

    weight = jnp.where(passive == 1, 0.0, -penalty * density * density)
    table = pltpu.VMEM((CASES, 8, 8, LANES), F32)
    gathered = pltpu.VMEM((8, CASES, 8, LANES), F32)
    adjoint, adj, edge = pl.pallas_call(
        adjoint_kernel, out_shape=(f32(CASES, 1, unknowns), f32(CASES, unknowns), f32(8, LANES)),
        in_specs=[SMEM] + [VMEM] * 6, out_specs=(VMEM,) * 3, scratch_shapes=[table, gathered],
        compiler_params=params(), name="adjoint",
    )(elem_stiff, got, coarse_inv, p, t, edge_pack(elem_dofs), edge_pack(weight))

    xe, xo = swap_over(edge, "gx", x_even), swap_over(edge, "gx", x_odd)
    ye, yo = swap_over(edge, "gy", y_even), swap_over(edge, "gy", y_odd)
    corners = []
    for px in (x_even, x_odd):
        for py in (y_even, y_odd):
            pairs = [(a * ny + c, b * ny + d) for a, b in px for c, d in py]
            corners.append(swap_over(edge, ("gx", "gy"), pairs))

    grad = pl.pallas_call(
        energy_kernel, out_shape=f32(ex, ey), in_specs=[SMEM] + [VMEM] * 4, out_specs=VMEM,
        scratch_shapes=[table, gathered], compiler_params=params(), name="energy",
        cost_estimate=cost(60_000_000, 20_000_000),
    )(elem_stiff, adj, elem_dofs, density, passive)

    sens = pl.pallas_call(
        filter_kernel, out_shape=f32(ex, ey), in_specs=[SMEM] + [VMEM] * 10, out_specs=VMEM,
        compiler_params=params(), name="smooth",
    )(place, grad, edge, xe, xo, ye, yo, *corners)
    return adjoint, sens


def solution(mesh):
    placed = (
        P(None, "gy", "gx"),
        P("gy", "gx", None),
        P("gy", "gx", None),
        P("gy", "gx"),
        P("gy", None, "gx"),
        P(),
        P(),
        P(None, "gx", "gy"),
        P("gx", "gy"),
        P("gx", "gy"),
    )
    return jax.shard_map(
        on_device,
        mesh=mesh,
        in_specs=placed,
        out_specs=(P(None, "gy", "gx"), P("gx", "gy")),
        check_vma=False,
    )
```

```python
import jax
import jax.numpy as jnp
from jax import lax
from jax.experimental import pallas as pl
from jax.experimental.pallas import tpu as pltpu
from jax.sharding import PartitionSpec as P

R = 128
LANES = 128
CASES = 8

coupling = 0.3
radius_sq = 2.0
penalty = 3.0
diag = 1.0 + 4.0 * radius_sq

HI = lax.Precision.HIGHEST
F32 = jnp.float32
BF16 = jnp.bfloat16
VMEM = pl.BlockSpec(memory_space=pltpu.VMEM)
HBM = pl.BlockSpec(memory_space=pltpu.HBM)

SIDE_P, SIDE_Y, SIDE_M, SIDE_C = 0, 8, 16, 24
RZ, PE, PQ, QMQ, TLT, TE = range(6)
KEEP_P, KEEP_Y, KEEP_REST, KEEP_S = 0, 8, 16, 24
FIELDS = 3 * CASES


def rows_dot(a, b):
    return lax.dot_general(a, b, (((1,), (1,)), ((), ())), precision=HI, preferred_element_type=F32)


def plain_dot(a, b):
    return lax.dot_general(a, b, (((1,), (0,)), ((), ())), precision=HI, preferred_element_type=F32)


def halves(x):
    high = x.astype(BF16)
    low = (x - high.astype(F32)).astype(BF16)
    return jnp.concatenate([high, low], axis=0)


def lane_sum(x):
    return jnp.sum(x, axis=1, keepdims=True)


def pattern(idx):
    return idx & (LANES - 1), (idx & 128) != 0, (idx & 256) != 0, (idx & 512) != 0


def pick(blocks, where):
    lane, bit0, bit1, bit2 = where
    got = [jnp.take_along_axis(b, lane, axis=1, mode="promise_in_bounds") for b in blocks]
    got = [jnp.where(bit0, got[2 * i + 1], got[2 * i]) for i in range(4)]
    got = [jnp.where(bit1, got[2 * i + 1], got[2 * i]) for i in range(2)]
    return jnp.where(bit2, got[1], got[0])


def blocks_of(row8):
    return [row8[:, LANES * h : LANES * (h + 1)] for h in range(8)]


def is_odd(axis):
    return lax.axis_index(axis) & 1 == 1


def at_lanes(columns, first=0):
    lane = lax.broadcasted_iota(jnp.int32, (CASES, LANES), 1)
    block = jnp.zeros((CASES, LANES), F32)
    for j, column in enumerate(columns):
        block = jnp.where(lane == first + j, column, block)
    return block


def fetch(sems, pairs):
    copies = [pltpu.make_async_copy(a, b, sems.at[i]) for i, (a, b) in enumerate(pairs)]
    for copy in copies:
        copy.start()
    return copies


def first_kernel(loads_hbm, pre_hbm, corner_hbm, send_ref, loads_ref, pre_ref, corner_ref, sems):
    copies = fetch(sems, ((loads_hbm, loads_ref), (pre_hbm, pre_ref), (corner_hbm, corner_ref)))
    for copy in copies:
        copy.wait()
    part = rows_dot(pre_ref[...] * loads_ref[:, 0, :], corner_ref[0])
    for d in range(send_ref.shape[0]):
        send_ref[d] = part


def side_kernel(loads_hbm, op_hbm, iface_hbm, pre_hbm, corner_hbm,
                keep_ref, even_ref, odd_ref, inverse_ref,
                loads_ref, op_ref, iface_ref, pre_ref, corner_ref, sems):
    copies = fetch(sems, ((loads_hbm, loads_ref), (pre_hbm, pre_ref), (iface_hbm, iface_ref),
                          (corner_hbm, corner_ref), (op_hbm, op_ref)))
    for copy in copies[:3]:
        copy.wait()
    loads = loads_ref[:, 0, :]
    p = pre_ref[...] * loads
    keep_ref[KEEP_P : KEEP_P + 8] = p
    pre = jnp.broadcast_to(pre_ref[...], (8, pre_ref.shape[1]))
    left = iface_ref[0, :, :R]
    right = iface_ref[0, :, R : 2 * R]
    x_odd = jnp.broadcast_to(is_odd("gx"), (1, R))
    sides = ((jnp.where(x_odd, left, right), even_ref), (jnp.where(x_odd, right, left), odd_ref))
    copies[3].wait()
    chosen = []
    for side, (idx, out) in enumerate(sides):
        where = pattern(jnp.broadcast_to(idx, (8, R)))
        scale = pick(blocks_of(pre), where)
        chosen.append((where, scale))
        out[SIDE_P : SIDE_P + 8] = pick(blocks_of(p), where)
        out[SIDE_M : SIDE_M + 8] = scale
        for j in range(corner_ref.shape[1] // 8):
            rows = corner_ref[0, 8 * j : 8 * j + 8]
            out[SIDE_C + 8 * j : SIDE_C + 8 * j + 8] = scale * pick(blocks_of(rows), where)
        column = jnp.transpose(jnp.broadcast_to(idx, (R, R)))
        number = lax.broadcasted_iota(jnp.int32, (R, LANES), 0) + 1
        for h in range(8):
            at = lax.broadcasted_iota(jnp.int32, (R, LANES), 1) + LANES * h
            found = jnp.sum(jnp.where(column == at, number, 0), axis=0, keepdims=True)
            inverse_ref[side, :, LANES * h : LANES * (h + 1)] = jnp.broadcast_to(found, (8, LANES))
    copies[4].wait()
    both = lax.dot_general(halves(p), op_ref[0], (((1,), (1,)), ((), ())), preferred_element_type=F32)
    y, rest = both[:CASES], both[CASES:]
    keep_ref[KEEP_Y : KEEP_Y + 8] = y
    keep_ref[KEEP_REST : KEEP_REST + 8] = rest
    keep_ref[KEEP_S : KEEP_S + 8, :LANES] = at_lanes((lane_sum(loads * p), lane_sum(p * rest)))
    for (where, scale), (_, out) in zip(chosen, sides):
        out[SIDE_Y : SIDE_Y + 8] = scale * pick(blocks_of(y), where)


def spread(values, inverse):
    out = []
    for h in range(8):
        at = inverse[:, LANES * h : LANES * (h + 1)]
        got = jnp.take_along_axis(values, jnp.maximum(at - 1, 0), axis=1, mode="promise_in_bounds")
        out.append(jnp.where(at > 0, got, 0.0))
    return jnp.concatenate(out, axis=1)


def second_kernel(got_ref, keep_ref, mine_e_ref, mine_o_ref, theirs_e_ref, theirs_o_ref, inverse_ref,
                  coarse_ref, corner_ref, op_ref, pre_hbm, send_ref, t_ref, pre_ref, sems):
    copies = fetch(sems, ((pre_hbm, pre_ref),))
    total = got_ref[0]
    for d in range(1, got_ref.shape[0]):
        total = total + got_ref[d]
    p = keep_ref[KEEP_P : KEEP_P + 8]
    base = keep_ref[KEEP_Y : KEEP_Y + 8]
    pairs = ((mine_e_ref, theirs_e_ref), (mine_o_ref, theirs_o_ref))
    for side, (_, theirs) in enumerate(pairs):
        base = base + spread(-coupling * theirs[SIDE_P : SIDE_P + 8], inverse_ref[side])
    w = rows_dot(total, coarse_ref[...])
    q = base + plain_dot(w, corner_ref[0])
    copies[0].wait()
    t = pre_ref[...] * q
    t_ref[...] = t
    g = rows_dot(t, corner_ref[0])
    tlt = None
    for mine, theirs in pairs:
        p_mine, p_theirs = mine[SIDE_P : SIDE_P + 8], theirs[SIDE_P : SIDE_P + 8]
        t_mine = mine[SIDE_Y : SIDE_Y + 8] - coupling * mine[SIDE_M : SIDE_M + 8] * p_theirs
        t_mine = t_mine + plain_dot(w, mine[SIDE_C:])
        t_theirs = theirs[SIDE_Y : SIDE_Y + 8] - coupling * theirs[SIDE_M : SIDE_M + 8] * p_mine
        t_theirs = t_theirs + plain_dot(w, theirs[SIDE_C:])
        term = -coupling * lane_sum(t_mine * t_theirs)
        tlt = term if tlt is None else tlt + term
    both = lax.dot_general(halves(t), op_ref[0], (((1,), (1,)), ((), ())), preferred_element_type=F32)
    tlt = tlt + lane_sum(t * (both[:CASES] + both[CASES:]))
    rest = keep_ref[KEEP_REST : KEEP_REST + 8]
    block = keep_ref[KEEP_S : KEEP_S + 8, :LANES]
    block = block + at_lanes((lane_sum(p * q), lane_sum(q * t), tlt, lane_sum(t * rest)), PQ)
    for d in range(send_ref.shape[0]):
        send_ref[d, :CASES] = g
        send_ref[d, CASES:] = block


def make_table(table_ref, vec):
    for c in range(CASES):
        for h in range(8):
            table_ref[c, h] = jnp.broadcast_to(vec[c : c + 1, LANES * h : LANES * (h + 1)], (8, LANES))


def gather_tile(dofs, table_ref, u_ref):
    for a in range(8):
        where = pattern(dofs(a))
        for c in range(CASES):
            u_ref[a, c] = pick([table_ref[c, h] for h in range(8)], where)


def stiff_row(stiff_ref, a, u):
    v = stiff_ref[a, 0] * u[0]
    for b in range(1, 8):
        v = v + stiff_ref[a, b] * u[b]
    return v


def edge_tiles(first, second):
    ex, ey = first.shape
    lane = lax.broadcasted_iota(jnp.int32, (1, LANES), 1)
    turned = jnp.transpose(jnp.concatenate([first, second], axis=0))
    swapped = pltpu.roll(turned, LANES - ex, 1)
    out = []
    for array, low, high in ((first, turned, swapped), (second, swapped, turned)):
        cols = [jnp.where(lane < ex, low[j : j + 1], high[j + 1 : j + 2]) for j in (0, ey - 2)]
        out.append(jnp.concatenate([array[0:2], array[ex - 2 :]] + cols + [array[0:2]], axis=0))
    return out


def p_kernel(keep_ref, dofs_ref, stiff_hbm, density_hbm, passive_hbm,
             kp_ref, pp_ref, pack_ref, weight_ref, table_ref, u_ref, stiff_ref, density_ref, passive_ref, sems):
    copies = fetch(sems, ((stiff_hbm, stiff_ref), (density_hbm, density_ref), (passive_hbm, passive_ref)))
    make_table(table_ref, keep_ref[KEEP_P : KEEP_P + 8])
    for a in range(0, 8, 2):
        first, second = edge_tiles(dofs_ref[a].astype(F32), dofs_ref[a + 1].astype(F32))
        pack_ref[a] = first.astype(jnp.int32)
        pack_ref[a + 1] = second.astype(jnp.int32)
    for copy in copies:
        copy.wait()
    rho = density_ref[...]
    weight = jnp.where(passive_ref[...] == 1, 0.0, -penalty * rho * rho)
    count = weight.shape[0] // 8
    for i in range(count):
        weight_ref[i] = weight[8 * i : 8 * i + 8]
    weight_ref[count] = edge_tiles(weight, weight)[0]

    def work(dofs, tile):
        gather_tile(dofs, table_ref, u_ref)
        scale = weight_ref[tile]
        for c in range(CASES):
            u = [u_ref[a, c] for a in range(8)]
            pp = None
            for a in range(8):
                v = stiff_row(stiff_ref, a, u)
                kp_ref[tile, a, c] = v
                pp = u[a] * v if pp is None else pp + u[a] * v
            pp_ref[tile, c] = scale * pp

    @pl.loop(0, count)
    def _(tile):
        rows = pl.ds(pl.multiple_of(8 * tile, 8), 8)
        work(lambda a: dofs_ref[a, rows, :], tile)

    work(lambda a: pack_ref[a], count)


def t_fields(stiff_ref, kp, scale, u_ref, c):
    u = [u_ref[a, c] for a in range(8)]
    pt = tt = None
    for a in range(8):
        v = stiff_ref[a, a] * u[a]
        for b in range(a + 1, 8):
            v = v + (stiff_ref[a, b] + stiff_ref[b, a]) * u[b]
        one, two = u[a] * kp(a, c), u[a] * v
        pt, tt = (one, two) if pt is None else (pt + one, tt + two)
    return scale * pt, scale * tt


def edge_kernel(t_ref, pack_ref, kp_ref, pp_ref, weight_ref, stiff_hbm,
                row_e_ref, row_o_ref, col_e_ref, col_o_ref, table_ref, u_ref, field_ref, stiff_ref, sems):
    copies = fetch(sems, ((stiff_hbm, stiff_ref),))
    make_table(table_ref, t_ref[...])
    gather_tile(lambda a: pack_ref[a], table_ref, u_ref)
    copies[0].wait()
    tile = kp_ref.shape[0] - 1
    for c in range(CASES):
        pt, tt = t_fields(stiff_ref, lambda a, c: kp_ref[tile, a, c], weight_ref[tile], u_ref, c)
        field_ref[c] = pp_ref[tile, c]
        field_ref[CASES + c] = pt
        field_ref[2 * CASES + c] = tt
    x_odd = jnp.broadcast_to(is_odd("gx"), (FIELDS, LANES))
    y_odd = jnp.broadcast_to(is_odd("gy"), (FIELDS, LANES))
    for i in range(2):
        low, high = field_ref[:, i, :], field_ref[:, 3 - i, :]
        row_e_ref[FIELDS * i : FIELDS * (i + 1)] = jnp.where(x_odd, low, high)
        row_o_ref[FIELDS * i : FIELDS * (i + 1)] = jnp.where(x_odd, high, low)
    low, high = field_ref[:, 4, :], field_ref[:, 5, :]
    col_e_ref[...] = jnp.where(y_odd, low, high)
    col_o_ref[...] = jnp.where(y_odd, high, low)


def t_kernel(t_ref, dofs_ref, kp_ref, weight_ref, stiff_hbm, pt_ref, tt_ref, table_ref, u_ref, stiff_ref, sems):
    copies = fetch(sems, ((stiff_hbm, stiff_ref),))
    make_table(table_ref, t_ref[...])
    copies[0].wait()

    @pl.loop(0, pt_ref.shape[0])
    def _(tile):
        rows = pl.ds(pl.multiple_of(8 * tile, 8), 8)
        gather_tile(lambda a: dofs_ref[a, rows, :], table_ref, u_ref)
        for c in range(CASES):
            pt_ref[tile, c], tt_ref[tile, c] = t_fields(
                stiff_ref, lambda a, c: kp_ref[tile, a, c], weight_ref[tile], u_ref, c)


def last_kernel(got_ref, coarse_ref, keep_ref, t_ref, pp_ref, pt_ref, tt_ref,
                mine_ye_ref, mine_yo_ref, xe_ref, xo_ref, ye_ref, yo_ref, ee_ref, eo_ref, oe_ref, oo_ref,
                adj_ref, out_ref):
    total = got_ref[0]
    for d in range(1, got_ref.shape[0]):
        total = total + got_ref[d]
    g, s = total[:CASES], total[CASES:]
    rz, pq, qmq, tlt, pe, te = (s[:, j : j + 1] for j in (RZ, PQ, QMQ, TLT, PE, TE))
    tat = tlt + lane_sum(g * rows_dot(g, coarse_ref[...]))
    alpha = rz / pq
    rz_next = rz - 2.0 * alpha * pq + alpha * alpha * qmq
    grow = 1.0 + rz_next / rz
    pap = grow * grow * (pq + pe) - 2.0 * alpha * grow * (qmq + te) + alpha * alpha * tat
    alpha_next = rz_next / pap
    of_p, of_t = alpha + alpha_next * grow, -(alpha * alpha_next)
    adj_ref[:, 0, :] = of_p * keep_ref[KEEP_P : KEEP_P + 8] + of_t * t_ref[...]

    factors = [of_p * of_p, 2.0 * of_p * of_t, of_t * of_t]
    wide = [jnp.broadcast_to(f, (CASES, LANES)) for f in factors]
    splat = [[jnp.broadcast_to(f[c : c + 1], (8, LANES)) for c in range(CASES)] for f in wide]
    tiles = []
    for i in range(pt_ref.shape[0]):
        tile = None
        for ref, factor in zip((pp_ref, pt_ref, tt_ref), splat):
            for c in range(CASES):
                term = factor[c] * ref[i, c]
                tile = term if tile is None else tile + term
        tiles.append(tile)
    grad = jnp.concatenate(tiles, axis=0)
    column = jnp.concatenate(wide, axis=0)

    def combine(fields):
        return jnp.sum(column * fields, axis=0, keepdims=True)

    ex, ey = grad.shape
    x_odd, y_odd = is_odd("gx"), is_odd("gy")
    has = []
    for axis in ("gx", "gy"):
        at, size = lax.axis_index(axis), lax.axis_size(axis)
        has += [jnp.where(at > 0, 1.0, 0.0), jnp.where(at < size - 1, 1.0, 0.0)]

    def choose(flag, a, b):
        return jnp.where(jnp.broadcast_to(flag, a.shape), a, b)

    def two(a, b, flag):
        return choose(flag, a, b), choose(flag, b, a)

    rows = [[combine(ref[FIELDS * i : FIELDS * (i + 1)]) for i in range(2)] for ref in (xe_ref, xo_ref)]
    g_below1, g_above1 = two(rows[0][0], rows[1][0], x_odd)
    g_below2, g_above2 = two(rows[0][1], rows[1][1], x_odd)
    before, after = two(combine(ye_ref[...]), combine(yo_ref[...]), y_odd)
    col_low, col_high = two(combine(mine_ye_ref[...]), combine(mine_yo_ref[...]), y_odd)
    ee, eo, oe, oo = (combine(ref[:FIELDS]) for ref in (ee_ref, eo_ref, oe_ref, oo_ref))
    below_e, above_e = two(ee, oe, x_odd)
    below_o, above_o = two(eo, oo, x_odd)
    below_before, below_after = two(below_e, below_o, y_odd)
    above_before, above_after = two(above_e, above_o, y_odd)
    last = LANES - 1
    corner = [below_before[:, last:] / diag, below_after[:, :1] / diag,
              above_before[:, last:] / diag, above_after[:, :1] / diag]
    lane = lax.broadcasted_iota(jnp.int32, (1, LANES), 1)

    def shifted(row, low, high, length):
        left = jnp.where(lane == 0, low, pltpu.roll(row, 1, 1))
        right = jnp.where(lane == length - 1, high, pltpu.roll(row, LANES - 1, 1))
        return left + right

    def upper(row):
        return pltpu.roll(row, LANES - ex, 1)

    g_before1, g_before2 = upper(before), before
    g_after1, g_after2 = after, upper(after)
    col_first, col_last = col_low, upper(col_high)
    s_below1, s_above1 = g_below1 / diag, g_above1 / diag
    s_before1, s_after1 = g_before1 / diag, g_after1 / diag

    def ring(g1, g2, inner, beside, there):
        return there * (g1 + radius_sq * (g2 / diag + inner / diag + beside)) / diag

    n_below = ring(g_below1, g_below2, grad[0:1], shifted(s_below1, corner[0], corner[1], ey), has[0])
    n_above = ring(g_above1, g_above2, grad[ex - 1 :], shifted(s_above1, corner[2], corner[3], ey), has[1])
    n_before = ring(g_before1, g_before2, col_first, shifted(s_before1, corner[0], corner[2], ex), has[2])
    n_after = ring(g_after1, g_after2, col_last, shifted(s_after1, corner[1], corner[3], ex), has[3])
    stack = jnp.concatenate([s_before1, s_after1, n_before, n_after, jnp.zeros((4, LANES), F32)], axis=0)
    columns = jnp.transpose(stack)[:ex]
    row_no = lax.broadcasted_iota(jnp.int32, (ex, ey), 0)
    col_no = lax.broadcasted_iota(jnp.int32, (ex, ey), 1)

    def sweep(s, below_row, above_row, before_col, after_col):
        down = jnp.where(row_no == 0, below_row, pltpu.roll(s, 1, 0))
        up = jnp.where(row_no == ex - 1, above_row, pltpu.roll(s, ex - 1, 0))
        left = jnp.where(col_no == 0, before_col, pltpu.roll(s, 1, 1))
        right = jnp.where(col_no == ey - 1, after_col, pltpu.roll(s, ey - 1, 1))
        return (grad + radius_sq * (up + down + right + left)) / diag

    s = sweep(grad / diag, s_below1, s_above1, columns[:, 0:1], columns[:, 1:2])
    out_ref[...] = sweep(s, n_below, n_above, columns[:, 2:3], columns[:, 3:4])


def swaps(size):
    out = []
    for first in (0, 1):
        pairs = [(i, i + 1) for i in range(first, size - 1, 2)]
        out.append(pairs + [(j, i) for i, j in pairs])
    return out


def swap_over(array, axis, pairs):
    return lax.ppermute(array, axis, pairs) if pairs else jnp.zeros_like(array)


def f32(*shape):
    return jax.ShapeDtypeStruct(shape, F32)


def call(kernel, name, out_shape, in_specs, scratch, moved):
    single = not isinstance(out_shape, tuple)
    return pl.pallas_call(
        kernel, out_shape=out_shape, in_specs=in_specs,
        out_specs=VMEM if single else (VMEM,) * len(out_shape), scratch_shapes=scratch, name=name,
        compiler_params=pltpu.CompilerParams(vmem_limit_bytes=LIMIT),
        cost_estimate=pl.CostEstimate(flops=1_000_000, bytes_accessed=moved, transcendentals=0),
    )


LIMIT = 6 * 1024 * 1024


def on_device(loads, dual_op, iface, precond, corner_map, coarse_inv, elem_stiff, elem_dofs, density, passive):
    nx, ny = lax.axis_size("gx"), lax.axis_size("gy")
    everyone = nx * ny
    unknowns = dual_op.shape[-1]
    modes = corner_map.shape[1]
    ex, ey = density.shape
    tiles = ex // 8
    x_even, x_odd = swaps(nx)
    y_even, y_odd = swaps(ny)

    def held(array):
        return pltpu.VMEM(array.shape, array.dtype)

    def copies(n):
        return pltpu.SemaphoreType.DMA((n,))

    stiff = pltpu.SMEM(elem_stiff.shape, F32)
    table = pltpu.VMEM((CASES, 8, 8, LANES), F32)
    gathered = pltpu.VMEM((8, CASES, 8, LANES), F32)

    send = call(first_kernel, "first", f32(everyone, CASES, modes), [HBM] * 3,
                [held(loads), held(precond), held(corner_map), copies(3)], 4_000_000,
                )(loads, precond, corner_map)
    got = lax.all_to_all(send, ("gx", "gy"), 0, 0)

    side = f32(SIDE_C + modes, R)
    keep, mine_e, mine_o, inverse = call(
        side_kernel, "sides",
        (f32(KEEP_S + 8, unknowns), side, side, jax.ShapeDtypeStruct((2, 8, unknowns), jnp.int32)),
        [HBM] * 5,
        [held(loads), held(dual_op), held(iface), held(precond), held(corner_map), copies(5)], 8_000_000,
    )(loads, dual_op, iface, precond, corner_map)
    theirs_e = swap_over(mine_e, "gx", x_even)
    theirs_o = swap_over(mine_o, "gx", x_odd)

    kp, pp, pack, weight = call(
        p_kernel, "pfields",
        (f32(tiles + 1, 8, CASES, 8, LANES), f32(tiles + 1, CASES, 8, LANES),
         jax.ShapeDtypeStruct((8, 8, LANES), jnp.int32), f32(tiles + 1, 8, LANES)),
        [VMEM] * 2 + [HBM] * 3, [table, gathered, stiff, held(density), held(passive), copies(3)], 24_000_000,
    )(keep, elem_dofs, elem_stiff, density, passive)
    got, pack = lax.optimization_barrier((got, pack))

    send, t = call(
        second_kernel, "second", (f32(everyone, 2 * CASES, modes), f32(CASES, unknowns)),
        [VMEM] * 10 + [HBM], [held(precond), copies(1)], 9_000_000,
    )(got, keep, mine_e, mine_o, theirs_e, theirs_o, inverse, coarse_inv, corner_map, dual_op, precond)
    got = lax.all_to_all(send, ("gx", "gy"), 0, 0)

    row = f32(2 * FIELDS, LANES)
    col = f32(FIELDS, LANES)
    row_e, row_o, col_e, col_o = call(
        edge_kernel, "edges", (row, row, col, col), [VMEM] * 5 + [HBM],
        [table, gathered, pltpu.VMEM((FIELDS, 8, LANES), F32), stiff, copies(1)], 4_000_000,
    )(t, pack, kp, pp, weight, elem_stiff)
    near = [swap_over(row_e, "gx", x_even), swap_over(row_o, "gx", x_odd),
            swap_over(col_e, "gy", y_even), swap_over(col_o, "gy", y_odd)]
    for array, px in ((row_e, x_even), (row_o, x_odd)):
        for py in (y_even, y_odd):
            pairs = [(a * ny + c, b * ny + d) for a, b in px for c, d in py]
            near.append(swap_over(array, ("gx", "gy"), pairs))

    field = f32(tiles, CASES, 8, LANES)
    pt, tt = call(
        t_kernel, "tfields", (field, field), [VMEM] * 4 + [HBM], [table, gathered, stiff, copies(1)], 22_000_000,
    )(t, elem_dofs, kp, weight, elem_stiff)

    adjoint, sens = call(
        last_kernel, "last", (f32(CASES, 1, unknowns), f32(ex, ey)), [VMEM] * 17, [], 4_000_000,
    )(got, coarse_inv, keep, t, pp, pt, tt, col_e, col_o, *near)
    return adjoint, sens


def solution(mesh):
    placed = (
        P(None, "gy", "gx"),
        P("gy", "gx", None),
        P("gy", "gx", None),
        P("gy", "gx"),
        P("gy", None, "gx"),
        P(),
        P(),
        P(None, "gx", "gy"),
        P("gx", "gy"),
        P("gx", "gy"),
    )
    return jax.shard_map(
        on_device,
        mesh=mesh,
        in_specs=placed,
        out_specs=(P(None, "gy", "gx"), P("gx", "gy")),
        check_vma=False,
    )
```

```python
import jax
import jax.numpy as jnp
from jax import lax
from jax.experimental import pallas as pl
from jax.experimental.pallas import tpu as pltpu
from jax.sharding import PartitionSpec as P

R = 128
LANES = 128
CASES = 8

coupling = 0.3
radius_sq = 2.0
penalty = 3.0
diag = 1.0 + 4.0 * radius_sq

HI = lax.Precision.HIGHEST
F32 = jnp.float32
BF16 = jnp.bfloat16
VMEM = pl.BlockSpec(memory_space=pltpu.VMEM)
HBM = pl.BlockSpec(memory_space=pltpu.HBM)

SIDE_P, SIDE_Y, SIDE_M, SIDE_C = 0, 8, 16, 24
RZ, PE, PQ, QMQ, TLT, TE = range(6)
KEEP_P, KEEP_Y, KEEP_REST, KEEP_S = 0, 8, 16, 24
FIELDS = 3 * CASES


def rows_dot(a, b):
    return lax.dot_general(a, b, (((1,), (1,)), ((), ())), precision=HI, preferred_element_type=F32)


def plain_dot(a, b):
    return lax.dot_general(a, b, (((1,), (0,)), ((), ())), precision=HI, preferred_element_type=F32)


def halves(x):
    high = x.astype(BF16)
    low = (x - high.astype(F32)).astype(BF16)
    return jnp.concatenate([high, low], axis=0)


def lane_sum(x):
    return jnp.sum(x, axis=1, keepdims=True)


def pattern(idx):
    return idx & (LANES - 1), (idx & 128) != 0, (idx & 256) != 0, (idx & 512) != 0


def pick(blocks, where):
    lane, bit0, bit1, bit2 = where
    got = [jnp.take_along_axis(b, lane, axis=1, mode="promise_in_bounds") for b in blocks]
    got = [jnp.where(bit0, got[2 * i + 1], got[2 * i]) for i in range(4)]
    got = [jnp.where(bit1, got[2 * i + 1], got[2 * i]) for i in range(2)]
    return jnp.where(bit2, got[1], got[0])


def blocks_of(row8):
    return [row8[:, LANES * h : LANES * (h + 1)] for h in range(8)]


def is_odd(axis):
    return lax.axis_index(axis) & 1 == 1


def at_lanes(columns, first=0):
    lane = lax.broadcasted_iota(jnp.int32, (CASES, LANES), 1)
    block = jnp.zeros((CASES, LANES), F32)
    for j, column in enumerate(columns):
        block = jnp.where(lane == first + j, column, block)
    return block


def fetch(sems, pairs):
    copies = [pltpu.make_async_copy(a, b, sems.at[i]) for i, (a, b) in enumerate(pairs)]
    for copy in copies:
        copy.start()
    return copies


def first_kernel(loads_hbm, pre_hbm, corner_hbm, send_ref, loads_ref, pre_ref, corner_ref, sems):
    copies = fetch(sems, ((loads_hbm, loads_ref), (pre_hbm, pre_ref), (corner_hbm, corner_ref)))
    for copy in copies:
        copy.wait()
    part = rows_dot(pre_ref[...] * loads_ref[:, 0, :], corner_ref[0])
    for d in range(send_ref.shape[0]):
        send_ref[d] = part


def side_kernel(loads_hbm, op_hbm, iface_hbm, pre_hbm, corner_hbm,
                keep_ref, even_ref, odd_ref, inverse_ref,
                loads_ref, op_ref, iface_ref, pre_ref, corner_ref, sems):
    copies = fetch(sems, ((loads_hbm, loads_ref), (pre_hbm, pre_ref), (iface_hbm, iface_ref),
                          (corner_hbm, corner_ref), (op_hbm, op_ref)))
    for copy in copies[:3]:
        copy.wait()
    loads = loads_ref[:, 0, :]
    p = pre_ref[...] * loads
    keep_ref[KEEP_P : KEEP_P + 8] = p
    pre = jnp.broadcast_to(pre_ref[...], (8, pre_ref.shape[1]))
    left = iface_ref[0, :, :R]
    right = iface_ref[0, :, R : 2 * R]
    x_odd = jnp.broadcast_to(is_odd("gx"), (1, R))
    sides = ((jnp.where(x_odd, left, right), even_ref), (jnp.where(x_odd, right, left), odd_ref))
    copies[3].wait()
    chosen = []
    for side, (idx, out) in enumerate(sides):
        where = pattern(jnp.broadcast_to(idx, (8, R)))
        scale = pick(blocks_of(pre), where)
        chosen.append((where, scale))
        out[SIDE_P : SIDE_P + 8] = pick(blocks_of(p), where)
        out[SIDE_M : SIDE_M + 8] = scale
        for j in range(corner_ref.shape[1] // 8):
            rows = corner_ref[0, 8 * j : 8 * j + 8]
            out[SIDE_C + 8 * j : SIDE_C + 8 * j + 8] = scale * pick(blocks_of(rows), where)
        column = jnp.transpose(jnp.broadcast_to(idx, (R, R)))
        number = lax.broadcasted_iota(jnp.int32, (R, LANES), 0) + 1
        for h in range(8):
            at = lax.broadcasted_iota(jnp.int32, (R, LANES), 1) + LANES * h
            found = jnp.sum(jnp.where(column == at, number, 0), axis=0, keepdims=True)
            inverse_ref[side, :, LANES * h : LANES * (h + 1)] = jnp.broadcast_to(found, (8, LANES))
    copies[4].wait()
    both = lax.dot_general(halves(p), op_ref[0], (((1,), (1,)), ((), ())), preferred_element_type=F32)
    y, rest = both[:CASES], both[CASES:]
    keep_ref[KEEP_Y : KEEP_Y + 8] = y
    keep_ref[KEEP_REST : KEEP_REST + 8] = rest
    keep_ref[KEEP_S : KEEP_S + 8, :LANES] = at_lanes((lane_sum(loads * p), lane_sum(p * rest)))
    for (where, scale), (_, out) in zip(chosen, sides):
        out[SIDE_Y : SIDE_Y + 8] = scale * pick(blocks_of(y), where)


def spread(values, inverse):
    out = []
    for h in range(8):
        at = inverse[:, LANES * h : LANES * (h + 1)]
        got = jnp.take_along_axis(values, jnp.maximum(at - 1, 0), axis=1, mode="promise_in_bounds")
        out.append(jnp.where(at > 0, got, 0.0))
    return jnp.concatenate(out, axis=1)


def second_kernel(got_ref, keep_ref, mine_e_ref, mine_o_ref, theirs_e_ref, theirs_o_ref, inverse_ref,
                  coarse_ref, corner_ref, pre_hbm, op_hbm, send_ref, t_ref, pre_ref, op_ref, sems):
    copies = fetch(sems, ((pre_hbm, pre_ref), (op_hbm, op_ref)))
    total = got_ref[0]
    for d in range(1, got_ref.shape[0]):
        total = total + got_ref[d]
    p = keep_ref[KEEP_P : KEEP_P + 8]
    base = keep_ref[KEEP_Y : KEEP_Y + 8]
    pairs = ((mine_e_ref, theirs_e_ref), (mine_o_ref, theirs_o_ref))
    for side, (_, theirs) in enumerate(pairs):
        base = base + spread(-coupling * theirs[SIDE_P : SIDE_P + 8], inverse_ref[side])
    w = rows_dot(total, coarse_ref[...])
    q = base + plain_dot(w, corner_ref[0])
    copies[0].wait()
    t = pre_ref[...] * q
    t_ref[...] = t
    g = rows_dot(t, corner_ref[0])
    tlt = None
    for mine, theirs in pairs:
        p_mine, p_theirs = mine[SIDE_P : SIDE_P + 8], theirs[SIDE_P : SIDE_P + 8]
        t_mine = mine[SIDE_Y : SIDE_Y + 8] - coupling * mine[SIDE_M : SIDE_M + 8] * p_theirs
        t_mine = t_mine + plain_dot(w, mine[SIDE_C:])
        t_theirs = theirs[SIDE_Y : SIDE_Y + 8] - coupling * theirs[SIDE_M : SIDE_M + 8] * p_mine
        t_theirs = t_theirs + plain_dot(w, theirs[SIDE_C:])
        term = -coupling * lane_sum(t_mine * t_theirs)
        tlt = term if tlt is None else tlt + term
    copies[1].wait()
    both = lax.dot_general(halves(t), op_ref[0], (((1,), (1,)), ((), ())), preferred_element_type=F32)
    tlt = tlt + lane_sum(t * (both[:CASES] + both[CASES:]))
    rest = keep_ref[KEEP_REST : KEEP_REST + 8]
    block = keep_ref[KEEP_S : KEEP_S + 8, :LANES]
    block = block + at_lanes((lane_sum(p * q), lane_sum(q * t), tlt, lane_sum(t * rest)), PQ)
    for d in range(send_ref.shape[0]):
        send_ref[d, :CASES] = g
        send_ref[d, CASES:] = block


def make_table(table_ref, vec):
    for c in range(CASES):
        for h in range(8):
            table_ref[c, h] = jnp.broadcast_to(vec[c : c + 1, LANES * h : LANES * (h + 1)], (8, LANES))


def gather_tile(dofs, table_ref, u_ref):
    for a in range(8):
        where = pattern(dofs(a))
        for c in range(CASES):
            u_ref[a, c] = pick([table_ref[c, h] for h in range(8)], where)


def stiff_row(stiff_ref, a, u):
    v = stiff_ref[a, 0] * u[0]
    for b in range(1, 8):
        v = v + stiff_ref[a, b] * u[b]
    return v


def edge_tiles(first, second):
    ex, ey = first.shape
    lane = lax.broadcasted_iota(jnp.int32, (1, LANES), 1)
    turned = jnp.transpose(jnp.concatenate([first, second], axis=0))
    swapped = pltpu.roll(turned, LANES - ex, 1)
    out = []
    for array, low, high in ((first, turned, swapped), (second, swapped, turned)):
        cols = [jnp.where(lane < ex, low[j : j + 1], high[j + 1 : j + 2]) for j in (0, ey - 2)]
        out.append(jnp.concatenate([array[0:2], array[ex - 2 :]] + cols + [array[0:2]], axis=0))
    return out


def p_kernel(keep_ref, dofs_ref, stiff_hbm, density_hbm, passive_hbm,
             kp_hbm, pp_ref, pack_ref, weight_ref,
             table_ref, u_ref, kp_ref, stiff_ref, density_ref, passive_ref, sems, kp_sems):
    copies = fetch(sems, ((stiff_hbm, stiff_ref), (density_hbm, density_ref), (passive_hbm, passive_ref)))
    make_table(table_ref, keep_ref[KEEP_P : KEEP_P + 8])
    for a in range(0, 8, 2):
        first, second = edge_tiles(dofs_ref[a].astype(F32), dofs_ref[a + 1].astype(F32))
        pack_ref[a] = first.astype(jnp.int32)
        pack_ref[a + 1] = second.astype(jnp.int32)
    for copy in copies:
        copy.wait()
    rho = density_ref[...]
    weight = jnp.where(passive_ref[...] == 1, 0.0, -penalty * rho * rho)
    count = weight.shape[0] // 8
    for i in range(count):
        weight_ref[i] = weight[8 * i : 8 * i + 8]
    weight_ref[count] = edge_tiles(weight, weight)[0]

    def work(dofs, tile):
        gather_tile(dofs, table_ref, u_ref)
        scale = weight_ref[tile]
        for c in range(CASES):
            u = [u_ref[a, c] for a in range(8)]
            pp = None
            for a in range(8):
                v = stiff_row(stiff_ref, a, u)
                kp_ref[tile, a, c] = v
                pp = u[a] * v if pp is None else pp + u[a] * v
            pp_ref[tile, c] = scale * pp
        pltpu.make_async_copy(kp_ref.at[tile], kp_hbm.at[tile], kp_sems.at[tile]).start()

    @pl.loop(0, count)
    def _(tile):
        rows = pl.ds(pl.multiple_of(8 * tile, 8), 8)
        work(lambda a: dofs_ref[a, rows, :], tile)

    work(lambda a: pack_ref[a], count)
    for i in range(count + 1):
        pltpu.make_async_copy(kp_ref.at[i], kp_hbm.at[i], kp_sems.at[i]).wait()


def t_fields(stiff_ref, kp, scale, u_ref, c):
    u = [u_ref[a, c] for a in range(8)]
    pt = tt = None
    for a in range(8):
        v = stiff_ref[a, a] * u[a]
        for b in range(a + 1, 8):
            v = v + (stiff_ref[a, b] + stiff_ref[b, a]) * u[b]
        one, two = u[a] * kp(a, c), u[a] * v
        pt, tt = (one, two) if pt is None else (pt + one, tt + two)
    return scale * pt, scale * tt


def edge_kernel(t_ref, pack_ref, pp_ref, weight_ref, kp_hbm, stiff_hbm,
                row_e_ref, row_o_ref, col_e_ref, col_o_ref, table_ref, u_ref, kp_ref, field_ref, stiff_ref, sems):
    tile = kp_hbm.shape[0] - 1
    copies = fetch(sems, ((stiff_hbm, stiff_ref), (kp_hbm.at[tile], kp_ref)))
    make_table(table_ref, t_ref[...])
    gather_tile(lambda a: pack_ref[a], table_ref, u_ref)
    for copy in copies:
        copy.wait()
    for c in range(CASES):
        pt, tt = t_fields(stiff_ref, lambda a, c: kp_ref[a, c], weight_ref[tile], u_ref, c)
        field_ref[c] = pp_ref[tile, c]
        field_ref[CASES + c] = pt
        field_ref[2 * CASES + c] = tt
    x_odd = jnp.broadcast_to(is_odd("gx"), (FIELDS, LANES))
    y_odd = jnp.broadcast_to(is_odd("gy"), (FIELDS, LANES))
    for i in range(2):
        low, high = field_ref[:, i, :], field_ref[:, 3 - i, :]
        row_e_ref[FIELDS * i : FIELDS * (i + 1)] = jnp.where(x_odd, low, high)
        row_o_ref[FIELDS * i : FIELDS * (i + 1)] = jnp.where(x_odd, high, low)
    low, high = field_ref[:, 4, :], field_ref[:, 5, :]
    col_e_ref[...] = jnp.where(y_odd, low, high)
    col_o_ref[...] = jnp.where(y_odd, high, low)


def t_kernel(t_ref, dofs_ref, weight_ref, kp_hbm, stiff_hbm, pt_ref, tt_ref,
             table_ref, u_ref, kp_ref, stiff_ref, sems, kp_sems):
    count = pt_ref.shape[0]
    copies = fetch(sems, ((stiff_hbm, stiff_ref),))
    fetch(kp_sems, [(kp_hbm.at[i], kp_ref.at[i]) for i in range(count)])
    make_table(table_ref, t_ref[...])
    copies[0].wait()

    @pl.loop(0, count)
    def _(tile):
        rows = pl.ds(pl.multiple_of(8 * tile, 8), 8)
        gather_tile(lambda a: dofs_ref[a, rows, :], table_ref, u_ref)
        pltpu.make_async_copy(kp_hbm.at[tile], kp_ref.at[tile], kp_sems.at[tile]).wait()
        for c in range(CASES):
            pt_ref[tile, c], tt_ref[tile, c] = t_fields(
                stiff_ref, lambda a, c: kp_ref[tile, a, c], weight_ref[tile], u_ref, c)


def last_kernel(got_ref, coarse_ref, keep_ref, t_ref, pp_ref, pt_ref, tt_ref,
                mine_ye_ref, mine_yo_ref, xe_ref, xo_ref, ye_ref, yo_ref, ee_ref, eo_ref, oe_ref, oo_ref,
                adj_ref, out_ref):
    total = got_ref[0]
    for d in range(1, got_ref.shape[0]):
        total = total + got_ref[d]
    g, s = total[:CASES], total[CASES:]
    rz, pq, qmq, tlt, pe, te = (s[:, j : j + 1] for j in (RZ, PQ, QMQ, TLT, PE, TE))
    tat = tlt + lane_sum(g * rows_dot(g, coarse_ref[...]))
    alpha = rz / pq
    rz_next = rz - 2.0 * alpha * pq + alpha * alpha * qmq
    grow = 1.0 + rz_next / rz
    pap = grow * grow * (pq + pe) - 2.0 * alpha * grow * (qmq + te) + alpha * alpha * tat
    alpha_next = rz_next / pap
    of_p, of_t = alpha + alpha_next * grow, -(alpha * alpha_next)
    adj_ref[:, 0, :] = of_p * keep_ref[KEEP_P : KEEP_P + 8] + of_t * t_ref[...]

    factors = [of_p * of_p, 2.0 * of_p * of_t, of_t * of_t]
    wide = [jnp.broadcast_to(f, (CASES, LANES)) for f in factors]
    splat = [[jnp.broadcast_to(f[c : c + 1], (8, LANES)) for c in range(CASES)] for f in wide]
    tiles = []
    for i in range(pt_ref.shape[0]):
        tile = None
        for ref, factor in zip((pp_ref, pt_ref, tt_ref), splat):
            for c in range(CASES):
                term = factor[c] * ref[i, c]
                tile = term if tile is None else tile + term
        tiles.append(tile)
    grad = jnp.concatenate(tiles, axis=0)
    column = jnp.concatenate(wide, axis=0)

    def combine(fields):
        return jnp.sum(column * fields, axis=0, keepdims=True)

    ex, ey = grad.shape
    x_odd, y_odd = is_odd("gx"), is_odd("gy")
    has = []
    for axis in ("gx", "gy"):
        at, size = lax.axis_index(axis), lax.axis_size(axis)
        has += [jnp.where(at > 0, 1.0, 0.0), jnp.where(at < size - 1, 1.0, 0.0)]

    def choose(flag, a, b):
        return jnp.where(jnp.broadcast_to(flag, a.shape), a, b)

    def two(a, b, flag):
        return choose(flag, a, b), choose(flag, b, a)

    rows = [[combine(ref[FIELDS * i : FIELDS * (i + 1)]) for i in range(2)] for ref in (xe_ref, xo_ref)]
    g_below1, g_above1 = two(rows[0][0], rows[1][0], x_odd)
    g_below2, g_above2 = two(rows[0][1], rows[1][1], x_odd)
    before, after = two(combine(ye_ref[...]), combine(yo_ref[...]), y_odd)
    col_low, col_high = two(combine(mine_ye_ref[...]), combine(mine_yo_ref[...]), y_odd)
    ee, eo, oe, oo = (combine(ref[:FIELDS]) for ref in (ee_ref, eo_ref, oe_ref, oo_ref))
    below_e, above_e = two(ee, oe, x_odd)
    below_o, above_o = two(eo, oo, x_odd)
    below_before, below_after = two(below_e, below_o, y_odd)
    above_before, above_after = two(above_e, above_o, y_odd)
    last = LANES - 1
    corner = [below_before[:, last:] / diag, below_after[:, :1] / diag,
              above_before[:, last:] / diag, above_after[:, :1] / diag]
    lane = lax.broadcasted_iota(jnp.int32, (1, LANES), 1)

    def shifted(row, low, high, length):
        left = jnp.where(lane == 0, low, pltpu.roll(row, 1, 1))
        right = jnp.where(lane == length - 1, high, pltpu.roll(row, LANES - 1, 1))
        return left + right

    def upper(row):
        return pltpu.roll(row, LANES - ex, 1)

    g_before1, g_before2 = upper(before), before
    g_after1, g_after2 = after, upper(after)
    col_first, col_last = col_low, upper(col_high)
    s_below1, s_above1 = g_below1 / diag, g_above1 / diag
    s_before1, s_after1 = g_before1 / diag, g_after1 / diag

    def ring(g1, g2, inner, beside, there):
        return there * (g1 + radius_sq * (g2 / diag + inner / diag + beside)) / diag

    n_below = ring(g_below1, g_below2, grad[0:1], shifted(s_below1, corner[0], corner[1], ey), has[0])
    n_above = ring(g_above1, g_above2, grad[ex - 1 :], shifted(s_above1, corner[2], corner[3], ey), has[1])
    n_before = ring(g_before1, g_before2, col_first, shifted(s_before1, corner[0], corner[2], ex), has[2])
    n_after = ring(g_after1, g_after2, col_last, shifted(s_after1, corner[1], corner[3], ex), has[3])
    stack = jnp.concatenate([s_before1, s_after1, n_before, n_after, jnp.zeros((4, LANES), F32)], axis=0)
    columns = jnp.transpose(stack)[:ex]
    row_no = lax.broadcasted_iota(jnp.int32, (ex, ey), 0)
    col_no = lax.broadcasted_iota(jnp.int32, (ex, ey), 1)

    def sweep(s, below_row, above_row, before_col, after_col):
        down = jnp.where(row_no == 0, below_row, pltpu.roll(s, 1, 0))
        up = jnp.where(row_no == ex - 1, above_row, pltpu.roll(s, ex - 1, 0))
        left = jnp.where(col_no == 0, before_col, pltpu.roll(s, 1, 1))
        right = jnp.where(col_no == ey - 1, after_col, pltpu.roll(s, ey - 1, 1))
        return (grad + radius_sq * (up + down + right + left)) / diag

    s = sweep(grad / diag, s_below1, s_above1, columns[:, 0:1], columns[:, 1:2])
    out_ref[...] = sweep(s, n_below, n_above, columns[:, 2:3], columns[:, 3:4])


def swaps(size):
    out = []
    for first in (0, 1):
        pairs = [(i, i + 1) for i in range(first, size - 1, 2)]
        out.append(pairs + [(j, i) for i, j in pairs])
    return out


def swap_over(array, axis, pairs):
    return lax.ppermute(array, axis, pairs) if pairs else jnp.zeros_like(array)


def f32(*shape):
    return jax.ShapeDtypeStruct(shape, F32)


def call(kernel, name, out_shape, in_specs, scratch, moved, first_in_hbm=False):
    single = not isinstance(out_shape, tuple)
    return pl.pallas_call(
        kernel, out_shape=out_shape, in_specs=in_specs,
        out_specs=VMEM if single else (HBM if first_in_hbm else VMEM,) + (VMEM,) * (len(out_shape) - 1), scratch_shapes=scratch, name=name,
        compiler_params=pltpu.CompilerParams(vmem_limit_bytes=LIMIT),
        cost_estimate=pl.CostEstimate(flops=1_000_000, bytes_accessed=moved, transcendentals=0),
    )


LIMIT = 6 * 1024 * 1024


def on_device(loads, dual_op, iface, precond, corner_map, coarse_inv, elem_stiff, elem_dofs, density, passive):
    nx, ny = lax.axis_size("gx"), lax.axis_size("gy")
    everyone = nx * ny
    unknowns = dual_op.shape[-1]
    modes = corner_map.shape[1]
    ex, ey = density.shape
    tiles = ex // 8
    x_even, x_odd = swaps(nx)
    y_even, y_odd = swaps(ny)

    def held(array):
        return pltpu.VMEM(array.shape, array.dtype)

    def in_hbm(array):
        return pltpu.with_memory_space_constraint(array, pltpu.HBM)

    def copies(n):
        return pltpu.SemaphoreType.DMA((n,))

    stiff = pltpu.SMEM(elem_stiff.shape, F32)
    table = pltpu.VMEM((CASES, 8, 8, LANES), F32)
    gathered = pltpu.VMEM((8, CASES, 8, LANES), F32)

    send = call(first_kernel, "first", f32(everyone, CASES, modes), [HBM] * 3,
                [held(loads), held(precond), held(corner_map), copies(3)], 4_000_000,
                )(in_hbm(loads), in_hbm(precond), in_hbm(corner_map))
    got = lax.all_to_all(send, ("gx", "gy"), 0, 0)

    side = f32(SIDE_C + modes, R)
    keep, mine_e, mine_o, inverse = call(
        side_kernel, "sides",
        (f32(KEEP_S + 8, unknowns), side, side, jax.ShapeDtypeStruct((2, 8, unknowns), jnp.int32)),
        [HBM] * 5,
        [held(loads), held(dual_op), held(iface), held(precond), held(corner_map), copies(5)], 8_000_000,
    )(*(in_hbm(a) for a in (loads, dual_op, iface, precond, corner_map)))
    theirs_e = swap_over(mine_e, "gx", x_even)
    theirs_o = swap_over(mine_o, "gx", x_odd)

    kp, pp, pack, weight = call(
        p_kernel, "pfields",
        (pltpu.HBM((tiles + 1, 8, CASES, 8, LANES), F32), f32(tiles + 1, CASES, 8, LANES),
         jax.ShapeDtypeStruct((8, 8, LANES), jnp.int32), f32(tiles + 1, 8, LANES)),
        [VMEM] * 2 + [HBM] * 3,
        [table, gathered, pltpu.VMEM((tiles + 1, 8, CASES, 8, LANES), F32), stiff, held(density), held(passive),
         copies(3), copies(tiles + 1)], 24_000_000, first_in_hbm=True,
    )(keep, elem_dofs, in_hbm(elem_stiff), in_hbm(density), in_hbm(passive))
    got, pack = lax.optimization_barrier((got, pack))

    send, t = call(
        second_kernel, "second", (f32(everyone, 2 * CASES, modes), f32(CASES, unknowns)),
        [VMEM] * 9 + [HBM] * 2, [held(precond), held(dual_op), copies(2)], 9_000_000,
    )(got, keep, mine_e, mine_o, theirs_e, theirs_o, inverse, coarse_inv, corner_map, in_hbm(precond), in_hbm(dual_op))
    got = lax.all_to_all(send, ("gx", "gy"), 0, 0)

    row = f32(2 * FIELDS, LANES)
    col = f32(FIELDS, LANES)
    row_e, row_o, col_e, col_o = call(
        edge_kernel, "edges", (row, row, col, col), [VMEM] * 4 + [HBM] * 2,
        [table, gathered, gathered, pltpu.VMEM((FIELDS, 8, LANES), F32), stiff, copies(2)], 4_000_000,
    )(t, pack, pp, weight, in_hbm(kp), in_hbm(elem_stiff))
    near = [swap_over(row_e, "gx", x_even), swap_over(row_o, "gx", x_odd),
            swap_over(col_e, "gy", y_even), swap_over(col_o, "gy", y_odd)]
    for array, px in ((row_e, x_even), (row_o, x_odd)):
        for py in (y_even, y_odd):
            pairs = [(a * ny + c, b * ny + d) for a, b in px for c, d in py]
            near.append(swap_over(array, ("gx", "gy"), pairs))

    field = f32(tiles, CASES, 8, LANES)
    pt, tt = call(
        t_kernel, "tfields", (field, field), [VMEM] * 3 + [HBM] * 2,
        [table, gathered, pltpu.VMEM((tiles, 8, CASES, 8, LANES), F32), stiff, copies(1), copies(tiles)], 22_000_000,
    )(t, elem_dofs, weight, in_hbm(kp), in_hbm(elem_stiff))

    adjoint, sens = call(
        last_kernel, "last", (f32(CASES, 1, unknowns), f32(ex, ey)), [VMEM] * 17, [], 4_000_000,
    )(got, coarse_inv, keep, t, pp, pt, tt, col_e, col_o, *near)
    return adjoint, sens


def solution(mesh):
    placed = (
        P(None, "gy", "gx"),
        P("gy", "gx", None),
        P("gy", "gx", None),
        P("gy", "gx"),
        P("gy", None, "gx"),
        P(),
        P(),
        P(None, "gx", "gy"),
        P("gx", "gy"),
        P("gx", "gy"),
    )
    return jax.shard_map(
        on_device,
        mesh=mesh,
        in_specs=placed,
        out_specs=(P(None, "gy", "gx"), P("gx", "gy")),
        check_vma=False,
    )
```

```python
import jax
import jax.numpy as jnp
from jax import lax
from jax.experimental import pallas as pl
from jax.experimental.pallas import tpu as pltpu
from jax.sharding import PartitionSpec as P

R = 128
LANES = 128
CASES = 8

coupling = 0.3
radius_sq = 2.0
penalty = 3.0
diag = 1.0 + 4.0 * radius_sq

HI = lax.Precision.HIGHEST
F32 = jnp.float32
BF16 = jnp.bfloat16
VMEM = pl.BlockSpec(memory_space=pltpu.VMEM)
HBM = pl.BlockSpec(memory_space=pltpu.HBM)

SIDE_P, SIDE_Y, SIDE_M, SIDE_C = 0, 8, 16, 24
RZ, PE, PQ, QMQ, TLT, TE = range(6)
KEEP_P, KEEP_Y, KEEP_REST, KEEP_S = 0, 8, 16, 24
FIELDS = 3 * CASES
CORNER_PP, CORNER_PT, CORNER_TT = 8, 12, 16


def rows_dot(a, b):
    return lax.dot_general(a, b, (((1,), (1,)), ((), ())), precision=HI, preferred_element_type=F32)


def plain_dot(a, b):
    return lax.dot_general(a, b, (((1,), (0,)), ((), ())), precision=HI, preferred_element_type=F32)


def halves(x):
    high = x.astype(BF16)
    low = (x - high.astype(F32)).astype(BF16)
    return jnp.concatenate([high, low], axis=0)


def lane_sum(x):
    return jnp.sum(x, axis=1, keepdims=True)


def pattern(idx):
    return idx & (LANES - 1), (idx & 128) != 0, (idx & 256) != 0, (idx & 512) != 0


def pick(blocks, where):
    lane, bit0, bit1, bit2 = where
    got = [jnp.take_along_axis(b, lane, axis=1, mode="promise_in_bounds") for b in blocks]
    got = [jnp.where(bit0, got[2 * i + 1], got[2 * i]) for i in range(4)]
    got = [jnp.where(bit1, got[2 * i + 1], got[2 * i]) for i in range(2)]
    return jnp.where(bit2, got[1], got[0])


def blocks_of(row8):
    return [row8[:, LANES * h : LANES * (h + 1)] for h in range(8)]


def is_odd(axis):
    return lax.axis_index(axis) & 1 == 1


def at_lanes(columns, first=0):
    lane = lax.broadcasted_iota(jnp.int32, (CASES, LANES), 1)
    block = jnp.zeros((CASES, LANES), F32)
    for j, column in enumerate(columns):
        block = jnp.where(lane == first + j, column, block)
    return block


def fetch(sems, pairs):
    copies = [pltpu.make_async_copy(a, b, sems.at[i]) for i, (a, b) in enumerate(pairs)]
    for copy in copies:
        copy.start()
    return copies


def first_kernel(loads_hbm, pre_hbm, corner_hbm, send_ref, loads_ref, pre_ref, corner_ref, sems):
    copies = fetch(sems, ((loads_hbm, loads_ref), (pre_hbm, pre_ref), (corner_hbm, corner_ref)))
    for copy in copies:
        copy.wait()
    part = rows_dot(pre_ref[...] * loads_ref[:, 0, :], corner_ref[0])
    for d in range(send_ref.shape[0]):
        send_ref[d] = part


def edge_tiles(first, second):
    ex, ey = first.shape
    lane = lax.broadcasted_iota(jnp.int32, (1, LANES), 1)
    turned = jnp.transpose(jnp.concatenate([first, second], axis=0))
    swapped = pltpu.roll(turned, LANES - ex, 1)
    out = []
    for array, low, high in ((first, turned, swapped), (second, swapped, turned)):
        cols = [jnp.where(lane < ex, low[j : j + 1], high[j + 1 : j + 2]) for j in (0, ey - 2)]
        out.append(jnp.concatenate([array[0:2], array[ex - 2 :]] + cols + [array[0:2]], axis=0))
    return out


def corner_lanes(low, high):
    lane = lax.broadcasted_iota(jnp.int32, low.shape, 1)
    out = jnp.where(lane == 0, low, jnp.where(lane == 1, pltpu.roll(low, 2, 1), 0))
    return jnp.where(lane == 2, pltpu.roll(high, 2, 1), jnp.where(lane == 3, pltpu.roll(high, 4, 1), out))


def corner_values(vec, where):
    return [pick(blocks_of(vec), pattern(jnp.broadcast_to(where[a : a + 1], (8, LANES)))) for a in range(8)]


def stiff_row(stiff_ref, a, u):
    v = stiff_ref[a, 0] * u[0]
    for b in range(1, 8):
        v = v + stiff_ref[a, b] * u[b]
    return v


def side_kernel(loads_hbm, op_hbm, iface_hbm, pre_hbm, corner_hbm, stiff_hbm, dofs_hbm, density_hbm, passive_hbm,
                keep_ref, even_ref, odd_ref, inverse_ref, pack_ref, weight_ref, spot_ref, spot_kp_ref,
                loads_ref, op_ref, iface_ref, pre_ref, corner_ref, stiff_ref, dofs_ref, density_ref, passive_ref,
                sems):
    copies = fetch(sems, ((loads_hbm, loads_ref), (pre_hbm, pre_ref), (iface_hbm, iface_ref),
                          (corner_hbm, corner_ref), (op_hbm, op_ref), (stiff_hbm, stiff_ref),
                          (dofs_hbm, dofs_ref), (density_hbm, density_ref), (passive_hbm, passive_ref)))
    for copy in copies[:3]:
        copy.wait()
    loads = loads_ref[:, 0, :]
    p = pre_ref[...] * loads
    keep_ref[KEEP_P : KEEP_P + 8] = p
    pre = jnp.broadcast_to(pre_ref[...], (8, pre_ref.shape[1]))
    left = iface_ref[0, :, :R]
    right = iface_ref[0, :, R : 2 * R]
    x_odd = jnp.broadcast_to(is_odd("gx"), (1, R))
    sides = ((jnp.where(x_odd, left, right), even_ref), (jnp.where(x_odd, right, left), odd_ref))
    copies[3].wait()
    copies[4].wait()
    both = lax.dot_general(halves(p), op_ref[0], (((1,), (1,)), ((), ())), preferred_element_type=F32)
    y, rest = both[:CASES], both[CASES:]
    keep_ref[KEEP_Y : KEEP_Y + 8] = y
    keep_ref[KEEP_REST : KEEP_REST + 8] = rest
    for idx, out in sides:
        where = pattern(jnp.broadcast_to(idx, (8, R)))
        scale = pick(blocks_of(pre), where)
        out[SIDE_P : SIDE_P + 8] = pick(blocks_of(p), where)
        out[SIDE_M : SIDE_M + 8] = scale
        for j in range(corner_ref.shape[1] // 8):
            rows = corner_ref[0, 8 * j : 8 * j + 8]
            out[SIDE_C + 8 * j : SIDE_C + 8 * j + 8] = scale * pick(blocks_of(rows), where)
        out[SIDE_Y : SIDE_Y + 8] = scale * pick(blocks_of(y), where)
    for side, (idx, _) in enumerate(sides):
        column = jnp.transpose(jnp.broadcast_to(idx, (R, R)))
        number = lax.broadcasted_iota(jnp.int32, (R, LANES), 0) + 1
        for h in range(8):
            at = lax.broadcasted_iota(jnp.int32, (R, LANES), 1) + LANES * h
            found = jnp.sum(jnp.where(column == at, number, 0), axis=0, keepdims=True)
            inverse_ref[side, :, LANES * h : LANES * (h + 1)] = jnp.broadcast_to(found, (8, LANES))
    for copy in copies[5:]:
        copy.wait()
    for a in range(0, 8, 2):
        first, second = edge_tiles(dofs_ref[a].astype(F32), dofs_ref[a + 1].astype(F32))
        pack_ref[a] = first.astype(jnp.int32)
        pack_ref[a + 1] = second.astype(jnp.int32)
    rho = density_ref[...]
    weight = jnp.where(passive_ref[...] == 1, 0.0, -penalty * rho * rho)
    ex = weight.shape[0]
    for i in range(ex // 8):
        weight_ref[i] = weight[8 * i : 8 * i + 8]
    weight_ref[ex // 8] = edge_tiles(weight, weight)[0]
    spot = corner_lanes(dofs_ref[:, 0, :], dofs_ref[:, ex - 1, :])
    spot_ref[...] = spot
    spot_weight = jnp.broadcast_to(corner_lanes(weight[0:1], weight[ex - 1 :]), (8, LANES))
    u = corner_values(p, spot)
    pp = None
    for a in range(8):
        v = stiff_row(stiff_ref, a, u)
        spot_kp_ref[a] = spot_weight * v
        pp = u[a] * v if pp is None else pp + u[a] * v
    spot_kp_ref[8] = spot_weight
    block = at_lanes((lane_sum(loads * p), lane_sum(p * rest)))
    lane = lax.broadcasted_iota(jnp.int32, (CASES, LANES), 1)
    pp = jnp.where(lane < 4, spot_weight * pp, 0.0)
    keep_ref[KEEP_S : KEEP_S + 8, :LANES] = block + pltpu.roll(pp, CORNER_PP, 1)


def spread(values, inverse):
    out = []
    for h in range(8):
        at = inverse[:, LANES * h : LANES * (h + 1)]
        got = jnp.take_along_axis(values, jnp.maximum(at - 1, 0), axis=1, mode="promise_in_bounds")
        out.append(jnp.where(at > 0, got, 0.0))
    return jnp.concatenate(out, axis=1)


def second_kernel(got_ref, keep_ref, mine_e_ref, mine_o_ref, theirs_e_ref, theirs_o_ref, inverse_ref,
                  spot_ref, spot_kp_ref, coarse_ref, corner_ref, pre_hbm, op_hbm, stiff_hbm,
                  send_ref, t_ref, pre_ref, op_ref, stiff_ref, sems):
    copies = fetch(sems, ((pre_hbm, pre_ref), (op_hbm, op_ref), (stiff_hbm, stiff_ref)))
    total = got_ref[0]
    for d in range(1, got_ref.shape[0]):
        total = total + got_ref[d]
    p = keep_ref[KEEP_P : KEEP_P + 8]
    base = keep_ref[KEEP_Y : KEEP_Y + 8]
    pairs = ((mine_e_ref, theirs_e_ref), (mine_o_ref, theirs_o_ref))
    for side, (_, theirs) in enumerate(pairs):
        base = base + spread(-coupling * theirs[SIDE_P : SIDE_P + 8], inverse_ref[side])
    w = rows_dot(total, coarse_ref[...])
    q = base + plain_dot(w, corner_ref[0])
    copies[0].wait()
    t = pre_ref[...] * q
    t_ref[...] = t
    g = rows_dot(t, corner_ref[0])
    tlt = None
    for mine, theirs in pairs:
        p_mine, p_theirs = mine[SIDE_P : SIDE_P + 8], theirs[SIDE_P : SIDE_P + 8]
        t_mine = mine[SIDE_Y : SIDE_Y + 8] - coupling * mine[SIDE_M : SIDE_M + 8] * p_theirs
        t_mine = t_mine + plain_dot(w, mine[SIDE_C:])
        t_theirs = theirs[SIDE_Y : SIDE_Y + 8] - coupling * theirs[SIDE_M : SIDE_M + 8] * p_mine
        t_theirs = t_theirs + plain_dot(w, theirs[SIDE_C:])
        term = -coupling * lane_sum(t_mine * t_theirs)
        tlt = term if tlt is None else tlt + term
    copies[1].wait()
    both = lax.dot_general(halves(t), op_ref[0], (((1,), (1,)), ((), ())), preferred_element_type=F32)
    tlt = tlt + lane_sum(t * (both[:CASES] + both[CASES:]))
    rest = keep_ref[KEEP_REST : KEEP_REST + 8]
    block = keep_ref[KEEP_S : KEEP_S + 8, :LANES]
    block = block + at_lanes((lane_sum(p * q), lane_sum(q * t), tlt, lane_sum(t * rest)), PQ)
    copies[2].wait()
    u = corner_values(t, spot_ref[...])
    pt = tt = None
    for a in range(8):
        one, two = u[a] * spot_kp_ref[a], u[a] * stiff_row(stiff_ref, a, u)
        pt, tt = (one, two) if pt is None else (pt + one, tt + two)
    lane = lax.broadcasted_iota(jnp.int32, (CASES, LANES), 1)
    pt, tt = jnp.where(lane < 4, pt, 0.0), jnp.where(lane < 4, spot_kp_ref[8] * tt, 0.0)
    block = block + pltpu.roll(pt, CORNER_PT, 1) + pltpu.roll(tt, CORNER_TT, 1)
    for d in range(send_ref.shape[0]):
        send_ref[d, :CASES] = g
        send_ref[d, CASES:] = block


def make_tables(table_ref, *vectors):
    for i, vec in enumerate(vectors):
        for c in range(CASES):
            for h in range(8):
                row = vec[c : c + 1, LANES * h : LANES * (h + 1)]
                table_ref[i, c, h] = jnp.broadcast_to(row, (8, LANES))


def tile_fields(dofs, scale, stiff_ref, table_ref, u_ref, put):
    for a in range(8):
        where = pattern(dofs(a))
        for c in range(CASES):
            for i in range(2):
                u_ref[i, a, c] = pick([table_ref[i, c, h] for h in range(8)], where)
    for c in range(CASES):
        p = [u_ref[0, a, c] for a in range(8)]
        t = [u_ref[1, a, c] for a in range(8)]
        pp = pt = tt = None
        for a in range(8):
            v = stiff_row(stiff_ref, a, p)
            w = stiff_ref[a, a] * t[a]
            for b in range(a + 1, 8):
                w = w + (stiff_ref[a, b] + stiff_ref[b, a]) * t[b]
            terms = p[a] * v, t[a] * v, t[a] * w
            pp, pt, tt = terms if pp is None else (pp + terms[0], pt + terms[1], tt + terms[2])
        put(c, scale * pp, scale * pt, scale * tt)


def edge_kernel(keep_ref, t_ref, pack_ref, weight_ref, stiff_hbm,
                row_e_ref, row_o_ref, col_e_ref, col_o_ref, table_ref, u_ref, field_ref, stiff_ref, sems):
    copies = fetch(sems, ((stiff_hbm, stiff_ref),))
    make_tables(table_ref, keep_ref[KEEP_P : KEEP_P + 8], t_ref[...])
    copies[0].wait()

    def put(c, *fields):
        for i, field in enumerate(fields):
            field_ref[CASES * i + c] = field

    tile_fields(lambda a: pack_ref[a], weight_ref[weight_ref.shape[0] - 1], stiff_ref, table_ref, u_ref, put)
    x_odd = jnp.broadcast_to(is_odd("gx"), (FIELDS, LANES))
    y_odd = jnp.broadcast_to(is_odd("gy"), (FIELDS, LANES))
    for i in range(2):
        low, high = field_ref[:, i, :], field_ref[:, 3 - i, :]
        row_e_ref[FIELDS * i : FIELDS * (i + 1)] = jnp.where(x_odd, low, high)
        row_o_ref[FIELDS * i : FIELDS * (i + 1)] = jnp.where(x_odd, high, low)
    low, high = field_ref[:, 4, :], field_ref[:, 5, :]
    col_e_ref[...] = jnp.where(y_odd, low, high)
    col_o_ref[...] = jnp.where(y_odd, high, low)


def field_kernel(keep_ref, t_ref, dofs_ref, weight_ref, stiff_hbm, pp_ref, pt_ref, tt_ref,
                 table_ref, u_ref, stiff_ref, sems):
    copies = fetch(sems, ((stiff_hbm, stiff_ref),))
    make_tables(table_ref, keep_ref[KEEP_P : KEEP_P + 8], t_ref[...])
    copies[0].wait()

    @pl.loop(0, pp_ref.shape[0])
    def _(tile):
        rows = pl.ds(pl.multiple_of(8 * tile, 8), 8)

        def put(c, pp, pt, tt):
            pp_ref[tile, c], pt_ref[tile, c], tt_ref[tile, c] = pp, pt, tt

        tile_fields(lambda a: dofs_ref[a, rows, :], weight_ref[tile], stiff_ref, table_ref, u_ref, put)


def last_kernel(got_ref, coarse_ref, keep_ref, t_ref, pp_ref, pt_ref, tt_ref,
                mine_ye_ref, mine_yo_ref, xe_ref, xo_ref, ye_ref, yo_ref,
                adj_ref, out_ref):
    total = got_ref[0]
    for d in range(1, got_ref.shape[0]):
        total = total + got_ref[d]
    g, s = total[:CASES], total[CASES:]
    rz, pq, qmq, tlt, pe, te = (s[:, j : j + 1] for j in (RZ, PQ, QMQ, TLT, PE, TE))
    tat = tlt + lane_sum(g * rows_dot(g, coarse_ref[...]))
    alpha = rz / pq
    rz_next = rz - 2.0 * alpha * pq + alpha * alpha * qmq
    grow = 1.0 + rz_next / rz
    pap = grow * grow * (pq + pe) - 2.0 * alpha * grow * (qmq + te) + alpha * alpha * tat
    alpha_next = rz_next / pap
    of_p, of_t = alpha + alpha_next * grow, -(alpha * alpha_next)
    adj_ref[:, 0, :] = of_p * keep_ref[KEEP_P : KEEP_P + 8] + of_t * t_ref[...]

    factors = [of_p * of_p, 2.0 * of_p * of_t, of_t * of_t]
    wide = [jnp.broadcast_to(f, (CASES, LANES)) for f in factors]
    splat = [[jnp.broadcast_to(f[c : c + 1], (8, LANES)) for c in range(CASES)] for f in wide]
    tiles = []
    for i in range(pt_ref.shape[0]):
        tile = None
        for ref, factor in zip((pp_ref, pt_ref, tt_ref), splat):
            for c in range(CASES):
                term = factor[c] * ref[i, c]
                tile = term if tile is None else tile + term
        tiles.append(tile)
    grad = jnp.concatenate(tiles, axis=0)
    column = jnp.concatenate(wide, axis=0)

    def combine(fields):
        return jnp.sum(column * fields, axis=0, keepdims=True)

    ex, ey = grad.shape
    x_odd, y_odd = is_odd("gx"), is_odd("gy")
    has = []
    for axis in ("gx", "gy"):
        at, size = lax.axis_index(axis), lax.axis_size(axis)
        has += [jnp.where(at > 0, 1.0, 0.0), jnp.where(at < size - 1, 1.0, 0.0)]

    def choose(flag, a, b):
        return jnp.where(jnp.broadcast_to(flag, a.shape), a, b)

    def two(a, b, flag):
        return choose(flag, a, b), choose(flag, b, a)

    rows = [[combine(ref[FIELDS * i : FIELDS * (i + 1)]) for i in range(2)] for ref in (xe_ref, xo_ref)]
    g_below1, g_above1 = two(rows[0][0], rows[1][0], x_odd)
    g_below2, g_above2 = two(rows[0][1], rows[1][1], x_odd)
    before, after = two(combine(ye_ref[...]), combine(yo_ref[...]), y_odd)
    col_low, col_high = two(combine(mine_ye_ref[...]), combine(mine_yo_ref[...]), y_odd)
    wide_lane = lax.broadcasted_iota(jnp.int32, (CASES, LANES), 1)
    of_lane = jnp.where(wide_lane < CORNER_PT, wide[0], jnp.where(wide_lane < CORNER_TT, wide[1], wide[2]))
    x, y = lax.axis_index("gx"), lax.axis_index("gy")
    nx, ny = lax.axis_size("gx"), lax.axis_size("gy")

    def corner_of(dx, dy, there, k):
        whose = jnp.clip(x + dx, 0, nx - 1) * ny + jnp.clip(y + dy, 0, ny - 1)
        row = jnp.sum(of_lane * got_ref[whose, CASES:, :], axis=0, keepdims=True)
        parts = [row[:, at + k : at + k + 1] for at in (CORNER_PP, CORNER_PT, CORNER_TT)]
        return there * (parts[0] + parts[1] + parts[2]) / diag

    corner = [corner_of(-1, -1, has[0] * has[2], 3), corner_of(-1, 1, has[0] * has[3], 2),
              corner_of(1, -1, has[1] * has[2], 1), corner_of(1, 1, has[1] * has[3], 0)]
    lane = lax.broadcasted_iota(jnp.int32, (1, LANES), 1)

    def shifted(row, low, high, length):
        left = jnp.where(lane == 0, low, pltpu.roll(row, 1, 1))
        right = jnp.where(lane == length - 1, high, pltpu.roll(row, LANES - 1, 1))
        return left + right

    def upper(row):
        return pltpu.roll(row, LANES - ex, 1)

    g_before1, g_before2 = upper(before), before
    g_after1, g_after2 = after, upper(after)
    col_first, col_last = col_low, upper(col_high)
    s_below1, s_above1 = g_below1 / diag, g_above1 / diag
    s_before1, s_after1 = g_before1 / diag, g_after1 / diag

    def ring(g1, g2, inner, beside, there):
        return there * (g1 + radius_sq * (g2 / diag + inner / diag + beside)) / diag

    n_below = ring(g_below1, g_below2, grad[0:1], shifted(s_below1, corner[0], corner[1], ey), has[0])
    n_above = ring(g_above1, g_above2, grad[ex - 1 :], shifted(s_above1, corner[2], corner[3], ey), has[1])
    n_before = ring(g_before1, g_before2, col_first, shifted(s_before1, corner[0], corner[2], ex), has[2])
    n_after = ring(g_after1, g_after2, col_last, shifted(s_after1, corner[1], corner[3], ex), has[3])
    stack = jnp.concatenate([s_before1, s_after1, n_before, n_after, jnp.zeros((4, LANES), F32)], axis=0)
    columns = jnp.transpose(stack)[:ex]
    row_no = lax.broadcasted_iota(jnp.int32, (ex, ey), 0)
    col_no = lax.broadcasted_iota(jnp.int32, (ex, ey), 1)

    def sweep(s, below_row, above_row, before_col, after_col):
        down = jnp.where(row_no == 0, below_row, pltpu.roll(s, 1, 0))
        up = jnp.where(row_no == ex - 1, above_row, pltpu.roll(s, ex - 1, 0))
        left = jnp.where(col_no == 0, before_col, pltpu.roll(s, 1, 1))
        right = jnp.where(col_no == ey - 1, after_col, pltpu.roll(s, ey - 1, 1))
        return (grad + radius_sq * (up + down + right + left)) / diag

    s = sweep(grad / diag, s_below1, s_above1, columns[:, 0:1], columns[:, 1:2])
    out_ref[...] = sweep(s, n_below, n_above, columns[:, 2:3], columns[:, 3:4])


def swaps(size):
    out = []
    for first in (0, 1):
        pairs = [(i, i + 1) for i in range(first, size - 1, 2)]
        out.append(pairs + [(j, i) for i, j in pairs])
    return out


def swap_over(array, axis, pairs):
    return lax.ppermute(array, axis, pairs) if pairs else jnp.zeros_like(array)


def f32(*shape):
    return jax.ShapeDtypeStruct(shape, F32)


def call(kernel, name, out_shape, in_specs, scratch, moved):
    single = not isinstance(out_shape, tuple)
    return pl.pallas_call(
        kernel, out_shape=out_shape, in_specs=in_specs,
        out_specs=VMEM if single else (VMEM,) * len(out_shape), scratch_shapes=scratch, name=name,
        compiler_params=pltpu.CompilerParams(vmem_limit_bytes=LIMIT),
        cost_estimate=pl.CostEstimate(flops=1_000_000, bytes_accessed=moved, transcendentals=0),
    )


LIMIT = 6 * 1024 * 1024


def on_device(loads, dual_op, iface, precond, corner_map, coarse_inv, elem_stiff, elem_dofs, density, passive):
    nx, ny = lax.axis_size("gx"), lax.axis_size("gy")
    everyone = nx * ny
    unknowns = dual_op.shape[-1]
    modes = corner_map.shape[1]
    ex, ey = density.shape
    tiles = ex // 8
    x_even, x_odd = swaps(nx)
    y_even, y_odd = swaps(ny)

    def held(array):
        return pltpu.VMEM(array.shape, array.dtype)

    def in_hbm(array):
        return pltpu.with_memory_space_constraint(array, pltpu.HBM)

    def copies(n):
        return pltpu.SemaphoreType.DMA((n,))

    stiff = pltpu.SMEM(elem_stiff.shape, F32)
    table = pltpu.VMEM((2, CASES, 8, 8, LANES), F32)
    gathered = pltpu.VMEM((2, 8, CASES, 8, LANES), F32)

    send = call(first_kernel, "first", f32(everyone, CASES, modes), [HBM] * 3,
                [held(loads), held(precond), held(corner_map), copies(3)], 4_000_000,
                )(in_hbm(loads), in_hbm(precond), in_hbm(corner_map))
    got = lax.all_to_all(send, ("gx", "gy"), 0, 0)

    side = f32(SIDE_C + modes, R)
    params = (loads, dual_op, iface, precond, corner_map, elem_stiff, elem_dofs, density, passive)
    keep, mine_e, mine_o, inverse, pack, weight, spot, spot_kp = call(
        side_kernel, "sides",
        (f32(KEEP_S + 8, unknowns), side, side, jax.ShapeDtypeStruct((2, 8, unknowns), jnp.int32),
         jax.ShapeDtypeStruct((8, 8, LANES), jnp.int32), f32(tiles + 1, 8, LANES),
         jax.ShapeDtypeStruct((8, LANES), jnp.int32), f32(9, 8, LANES)),
        [HBM] * 9, [stiff if a is elem_stiff else held(a) for a in params] + [copies(9)], 10_000_000,
    )(*(in_hbm(a) for a in params))
    theirs_e = swap_over(mine_e, "gx", x_even)
    theirs_o = swap_over(mine_o, "gx", x_odd)

    send, t = call(
        second_kernel, "second", (f32(everyone, 2 * CASES, modes), f32(CASES, unknowns)),
        [VMEM] * 11 + [HBM] * 3, [held(precond), held(dual_op), stiff, copies(3)], 9_000_000,
    )(got, keep, mine_e, mine_o, theirs_e, theirs_o, inverse, spot, spot_kp, coarse_inv, corner_map,
      in_hbm(precond), in_hbm(dual_op), in_hbm(elem_stiff))
    got = lax.all_to_all(send, ("gx", "gy"), 0, 0)

    row = f32(2 * FIELDS, LANES)
    col = f32(FIELDS, LANES)
    row_e, row_o, col_e, col_o = call(
        edge_kernel, "edges", (row, row, col, col), [VMEM] * 4 + [HBM],
        [table, gathered, pltpu.VMEM((FIELDS, 8, LANES), F32), stiff, copies(1)], 4_000_000,
    )(keep, t, pack, weight, in_hbm(elem_stiff))
    near = [swap_over(row_e, "gx", x_even), swap_over(row_o, "gx", x_odd),
            swap_over(col_e, "gy", y_even), swap_over(col_o, "gy", y_odd)]

    field = f32(tiles, CASES, 8, LANES)
    pp, pt, tt = call(
        field_kernel, "fields", (field,) * 3, [VMEM] * 4 + [HBM], [table, gathered, stiff, copies(1)], 36_000_000,
    )(keep, t, elem_dofs, weight, in_hbm(elem_stiff))

    adjoint, sens = call(
        last_kernel, "last", (f32(CASES, 1, unknowns), f32(ex, ey)), [VMEM] * 13, [], 4_000_000,
    )(got, coarse_inv, keep, t, pp, pt, tt, col_e, col_o, *near)
    return adjoint, sens


def solution(mesh):
    placed = (
        P(None, "gy", "gx"),
        P("gy", "gx", None),
        P("gy", "gx", None),
        P("gy", "gx"),
        P("gy", None, "gx"),
        P(),
        P(),
        P(None, "gx", "gy"),
        P("gx", "gy"),
        P("gx", "gy"),
    )
    return jax.shard_map(
        on_device,
        mesh=mesh,
        in_specs=placed,
        out_specs=(P(None, "gy", "gx"), P("gx", "gy")),
        check_vma=False,
    )
```

```python
import jax
import jax.numpy as jnp
from jax import lax
from jax.experimental import pallas as pl
from jax.experimental.pallas import tpu as pltpu
from jax.sharding import PartitionSpec as P

R = 128
LANES = 128
CASES = 8

coupling = 0.3
radius_sq = 2.0
penalty = 3.0
diag = 1.0 + 4.0 * radius_sq

HI = lax.Precision.HIGHEST
F32 = jnp.float32
BF16 = jnp.bfloat16
VMEM = pl.BlockSpec(memory_space=pltpu.VMEM)
HBM = pl.BlockSpec(memory_space=pltpu.HBM)

SIDE_P, SIDE_Y, SIDE_M, SIDE_C = 0, 8, 16, 24
RZ, PE, PQ, QMQ, TLT, TE = range(6)
KEEP_P, KEEP_Y, KEEP_REST, KEEP_S = 0, 8, 16, 24
FIELDS = 3 * CASES
EARLY = 5
CORNER_PP, CORNER_PT, CORNER_TT = 8, 12, 16


def rows_dot(a, b):
    return lax.dot_general(a, b, (((1,), (1,)), ((), ())), precision=HI, preferred_element_type=F32)


def plain_dot(a, b):
    return lax.dot_general(a, b, (((1,), (0,)), ((), ())), precision=HI, preferred_element_type=F32)


def halves(x):
    high = x.astype(BF16)
    low = (x - high.astype(F32)).astype(BF16)
    return jnp.concatenate([high, low], axis=0)


def split(x):
    high = x.astype(BF16)
    return high, (x - high.astype(F32)).astype(BF16)


def split_dot(a, pair, dim):
    stack = halves(a)
    dims = (((1,), (dim,)), ((), ()))
    main = lax.dot_general(stack, pair[0], dims, preferred_element_type=F32)
    rest = lax.dot_general(stack, pair[1], dims, preferred_element_type=F32)
    return main[:8] + main[8:] + rest[:8]


def lane_sum(x):
    return jnp.sum(x, axis=1, keepdims=True)


def pattern(idx):
    return idx & (LANES - 1), (idx & 128) != 0, (idx & 256) != 0, (idx & 512) != 0


def pick(blocks, where):
    lane, bit0, bit1, bit2 = where
    got = [jnp.take_along_axis(b, lane, axis=1, mode="promise_in_bounds") for b in blocks]
    got = [jnp.where(bit0, got[2 * i + 1], got[2 * i]) for i in range(4)]
    got = [jnp.where(bit1, got[2 * i + 1], got[2 * i]) for i in range(2)]
    return jnp.where(bit2, got[1], got[0])


def blocks_of(row8):
    return [row8[:, LANES * h : LANES * (h + 1)] for h in range(8)]


def is_odd(axis):
    return lax.axis_index(axis) & 1 == 1


def at_lanes(columns, first=0):
    lane = lax.broadcasted_iota(jnp.int32, (CASES, LANES), 1)
    block = jnp.zeros((CASES, LANES), F32)
    for j, column in enumerate(columns):
        block = jnp.where(lane == first + j, column, block)
    return block


def fetch(sems, pairs):
    copies = [pltpu.make_async_copy(a, b, sems.at[i]) for i, (a, b) in enumerate(pairs)]
    for copy in copies:
        copy.start()
    return copies


def first_kernel(loads_hbm, pre_hbm, corner_hbm, send_ref, loads_ref, pre_ref, corner_ref, sems):
    piece = corner_ref.shape[2] // 4
    parts = [pl.ds(piece * i, piece) for i in range(4)]
    copies = fetch(sems, [(loads_hbm, loads_ref), (pre_hbm, pre_ref)]
                   + [(corner_hbm.at[:, :, k], corner_ref.at[:, :, k]) for k in parts])
    copies[0].wait()
    copies[1].wait()
    p = pre_ref[...] * loads_ref[:, 0, :]
    part = None
    for i, k in enumerate(parts):
        copies[2 + i].wait()
        term = split_dot(p[:, piece * i : piece * (i + 1)], split(corner_ref[0, :, k]), 1)
        part = term if part is None else part + term
    for d in range(send_ref.shape[0]):
        send_ref[d] = part


def edge_tiles(first, second):
    ex, ey = first.shape
    lane = lax.broadcasted_iota(jnp.int32, (1, LANES), 1)
    turned = jnp.transpose(jnp.concatenate([first, second], axis=0))
    swapped = pltpu.roll(turned, LANES - ex, 1)
    out = []
    for array, low, high in ((first, turned, swapped), (second, swapped, turned)):
        cols = [jnp.where(lane < ex, low[j : j + 1], high[j + 1 : j + 2]) for j in (0, ey - 2)]
        out.append(jnp.concatenate([array[0:2], array[ex - 2 :]] + cols + [array[0:2]], axis=0))
    return out


def corner_lanes(low, high):
    lane = lax.broadcasted_iota(jnp.int32, low.shape, 1)
    out = jnp.where(lane == 0, low, jnp.where(lane == 1, pltpu.roll(low, 2, 1), 0))
    return jnp.where(lane == 2, pltpu.roll(high, 2, 1), jnp.where(lane == 3, pltpu.roll(high, 4, 1), out))


def corner_values(vec, where):
    return [pick(blocks_of(vec), pattern(jnp.broadcast_to(where[a : a + 1], (8, LANES)))) for a in range(8)]


def stiff_row(stiff_ref, a, u):
    v = stiff_ref[a, 0] * u[0]
    for b in range(1, 8):
        v = v + stiff_ref[a, b] * u[b]
    return v


def side_indices(iface_ref):
    left = jnp.broadcast_to(iface_ref[0, :, :R], (8, R))
    right = jnp.broadcast_to(iface_ref[0, :, R : 2 * R], (8, R))
    x_odd = jnp.broadcast_to(is_odd("gx"), (8, R))
    return jnp.where(x_odd, left, right), jnp.where(x_odd, right, left)


def side_kernel(loads_hbm, op_hbm, iface_hbm, pre_hbm, corner_hbm,
                keep_ref, even_ref, odd_ref, loads_ref, op_ref, iface_ref, pre_ref, corner_ref, sems):
    copies = fetch(sems, ((loads_hbm, loads_ref), (pre_hbm, pre_ref), (iface_hbm, iface_ref),
                          (corner_hbm, corner_ref), (op_hbm, op_ref)))
    for copy in copies[:4]:
        copy.wait()
    loads = loads_ref[:, 0, :]
    p = pre_ref[...] * loads
    keep_ref[KEEP_P : KEEP_P + 8] = p
    pre = jnp.broadcast_to(pre_ref[...], (8, pre_ref.shape[1]))
    chosen = []
    for idx, out in zip(side_indices(iface_ref), (even_ref, odd_ref)):
        where = pattern(idx)
        scale = pick(blocks_of(pre), where)
        chosen.append((where, scale, out))
        out[SIDE_P : SIDE_P + 8] = pick(blocks_of(p), where)
        out[SIDE_M : SIDE_M + 8] = scale
        for j in range(corner_ref.shape[1] // 8):
            rows = corner_ref[0, 8 * j : 8 * j + 8]
            out[SIDE_C + 8 * j : SIDE_C + 8 * j + 8] = scale * pick(blocks_of(rows), where)
    copies[4].wait()
    both = lax.dot_general(halves(p), op_ref[0], (((1,), (1,)), ((), ())), preferred_element_type=F32)
    y, rest = both[:CASES], both[CASES:]
    keep_ref[KEEP_Y : KEEP_Y + 8] = y
    keep_ref[KEEP_REST : KEEP_REST + 8] = rest
    keep_ref[KEEP_S : KEEP_S + 8, :LANES] = at_lanes((lane_sum(loads * p), lane_sum(p * rest)))
    for where, scale, out in chosen:
        out[SIDE_Y : SIDE_Y + 8] = scale * pick(blocks_of(y), where)


def early_kernel(keep_ref, dofs_ref, iface_hbm, corner_hbm, stiff_hbm, density_hbm, passive_hbm,
                 index_ref, inverse_ref, chigh_ref, clow_ref, pack_ref, weight_ref, spot_ref, spot_kp_ref,
                 kp_ref, pp_ref,
                 table_ref, u_ref, iface_ref, corner_ref, stiff_ref, density_ref, passive_ref, sems):
    copies = fetch(sems, ((iface_hbm, iface_ref), (stiff_hbm, stiff_ref), (density_hbm, density_ref),
                          (passive_hbm, passive_ref), (corner_hbm, corner_ref)))
    p = keep_ref[KEEP_P : KEEP_P + 8]
    make_tables(table_ref, p)
    for a in range(0, 8, 2):
        first, second = edge_tiles(dofs_ref[a].astype(F32), dofs_ref[a + 1].astype(F32))
        pack_ref[a] = first.astype(jnp.int32)
        pack_ref[a + 1] = second.astype(jnp.int32)
    for copy in copies:
        copy.wait()
    for side, idx in enumerate(side_indices(iface_ref)):
        index_ref[side] = idx
        column = jnp.transpose(jnp.broadcast_to(idx[0:1], (R, R)))
        number = lax.broadcasted_iota(jnp.int32, (R, LANES), 0) + 1
        for h in range(8):
            at = lax.broadcasted_iota(jnp.int32, (R, LANES), 1) + LANES * h
            found = jnp.sum(jnp.where(column == at, number, 0), axis=0, keepdims=True)
            inverse_ref[side, :, LANES * h : LANES * (h + 1)] = jnp.broadcast_to(found, (8, LANES))
    chigh_ref[...], clow_ref[...] = split(corner_ref[0])
    rho = density_ref[...]
    weight = jnp.where(passive_ref[...] == 1, 0.0, -penalty * rho * rho)
    ex = weight.shape[0]
    for i in range(ex // 8):
        weight_ref[i] = weight[8 * i : 8 * i + 8]
    weight_ref[ex // 8] = edge_tiles(weight, weight)[0]
    spot = corner_lanes(dofs_ref[:, 0, :], dofs_ref[:, ex - 1, :])
    spot_ref[...] = spot
    spot_weight = jnp.broadcast_to(corner_lanes(weight[0:1], weight[ex - 1 :]), (8, LANES))
    u = corner_values(p, spot)
    pp = None
    for a in range(8):
        v = stiff_row(stiff_ref, a, u)
        spot_kp_ref[a] = spot_weight * v
        pp = u[a] * v if pp is None else pp + u[a] * v
    lane = lax.broadcasted_iota(jnp.int32, (CASES, LANES), 1)
    spot_kp_ref[8] = spot_weight
    spot_kp_ref[9] = pltpu.roll(jnp.where(lane < 4, spot_weight * pp, 0.0), CORNER_PP, 1)

    def work(dofs, at, scale):
        gather_tile(dofs, table_ref, u_ref, 0)
        for c in range(CASES):
            u = [u_ref[0, a, c] for a in range(8)]
            pp = None
            for a in range(8):
                v = stiff_row(stiff_ref, a, u)
                kp_ref[at, a, c] = v
                pp = u[a] * v if pp is None else pp + u[a] * v
            pp_ref[at, c] = scale * pp

    @pl.loop(0, EARLY)
    def _(tile):
        rows = pl.ds(pl.multiple_of(8 * tile, 8), 8)
        work(lambda a: dofs_ref[a, rows, :], tile, weight_ref[tile])

    work(lambda a: pack_ref[a], EARLY, weight_ref[ex // 8])


def spread(values, inverse):
    out = []
    for h in range(8):
        at = inverse[:, LANES * h : LANES * (h + 1)]
        got = jnp.take_along_axis(values, jnp.maximum(at - 1, 0), axis=1, mode="promise_in_bounds")
        out.append(jnp.where(at > 0, got, 0.0))
    return jnp.concatenate(out, axis=1)


def second_kernel(got_ref, keep_ref, mine_e_ref, mine_o_ref, theirs_e_ref, theirs_o_ref, index_ref, inverse_ref,
                  spot_ref, spot_kp_ref, coarse_ref, chigh_ref, clow_ref, pre_hbm, op_hbm, stiff_hbm,
                  send_ref, t_ref, pre_ref, op_ref, stiff_ref, sems):
    copies = fetch(sems, ((pre_hbm, pre_ref), (op_hbm, op_ref), (stiff_hbm, stiff_ref)))
    total = got_ref[0]
    for d in range(1, got_ref.shape[0]):
        total = total + got_ref[d]
    corner = chigh_ref[...], clow_ref[...]
    p = keep_ref[KEEP_P : KEEP_P + 8]
    base = keep_ref[KEEP_Y : KEEP_Y + 8]
    pairs = ((mine_e_ref, theirs_e_ref), (mine_o_ref, theirs_o_ref))
    for side, (_, theirs) in enumerate(pairs):
        base = base + spread(-coupling * theirs[SIDE_P : SIDE_P + 8], inverse_ref[side])
    w = split_dot(total, split(coarse_ref[...]), 1)
    q = base + split_dot(w, corner, 0)
    for copy in copies:
        copy.wait()
    t = pre_ref[...] * q
    t_ref[...] = t
    both = lax.dot_general(halves(t), op_ref[0], (((1,), (1,)), ((), ())), preferred_element_type=F32)
    g = split_dot(t, corner, 1)
    tlt = lane_sum(t * (both[:CASES] + both[CASES:]))
    for side, (mine, theirs) in enumerate(pairs):
        t_mine = pick(blocks_of(t), pattern(index_ref[side]))
        t_theirs = theirs[SIDE_Y : SIDE_Y + 8] - coupling * theirs[SIDE_M : SIDE_M + 8] * mine[SIDE_P : SIDE_P + 8]
        t_theirs = t_theirs + split_dot(w, split(theirs[SIDE_C:]), 0)
        tlt = tlt - coupling * lane_sum(t_mine * t_theirs)
    rest = keep_ref[KEEP_REST : KEEP_REST + 8]
    block = keep_ref[KEEP_S : KEEP_S + 8, :LANES]
    block = block + at_lanes((lane_sum(p * q), lane_sum(q * t), tlt, lane_sum(t * rest)), PQ)
    u = corner_values(t, spot_ref[...])
    pt = tt = None
    for a in range(8):
        one, two = u[a] * spot_kp_ref[a], u[a] * stiff_row(stiff_ref, a, u)
        pt, tt = (one, two) if pt is None else (pt + one, tt + two)
    lane = lax.broadcasted_iota(jnp.int32, (CASES, LANES), 1)
    pt, tt = jnp.where(lane < 4, pt, 0.0), jnp.where(lane < 4, spot_kp_ref[8] * tt, 0.0)
    block = block + spot_kp_ref[9] + pltpu.roll(pt, CORNER_PT, 1) + pltpu.roll(tt, CORNER_TT, 1)
    for d in range(send_ref.shape[0]):
        send_ref[d, :CASES] = g
        send_ref[d, CASES:] = block


def make_tables(table_ref, *vectors):
    for i, vec in enumerate(vectors):
        for c in range(CASES):
            for h in range(8):
                row = vec[c : c + 1, LANES * h : LANES * (h + 1)]
                table_ref[i, c, h] = jnp.broadcast_to(row, (8, LANES))


def gather_tile(dofs, table_ref, u_ref, *which):
    for a in range(8):
        where = pattern(dofs(a))
        for c in range(CASES):
            for i in which:
                u_ref[i, a, c] = pick([table_ref[i, c, h] for h in range(8)], where)


def t_fields(t, kp, stiff_ref):
    pt = tt = None
    for a in range(8):
        w = stiff_ref[a, a] * t[a]
        for b in range(a + 1, 8):
            w = w + (stiff_ref[a, b] + stiff_ref[b, a]) * t[b]
        one, two = t[a] * kp[a], t[a] * w
        pt, tt = (one, two) if pt is None else (pt + one, tt + two)
    return pt, tt


def edge_kernel(t_ref, pack_ref, weight_ref, kp_ref, pp_ref, stiff_hbm,
                row_e_ref, row_o_ref, col_e_ref, col_o_ref, table_ref, u_ref, field_ref, stiff_ref, sems):
    copies = fetch(sems, ((stiff_hbm, stiff_ref),))
    make_tables(table_ref, t_ref[...])
    gather_tile(lambda a: pack_ref[a], table_ref, u_ref, 0)
    copies[0].wait()
    scale = weight_ref[weight_ref.shape[0] - 1]
    for c in range(CASES):
        pt, tt = t_fields([u_ref[0, a, c] for a in range(8)], [kp_ref[EARLY, a, c] for a in range(8)], stiff_ref)
        field_ref[c] = pp_ref[EARLY, c]
        field_ref[CASES + c] = scale * pt
        field_ref[2 * CASES + c] = scale * tt
    x_odd = jnp.broadcast_to(is_odd("gx"), (FIELDS, LANES))
    y_odd = jnp.broadcast_to(is_odd("gy"), (FIELDS, LANES))
    for i in range(2):
        low, high = field_ref[:, i, :], field_ref[:, 3 - i, :]
        row_e_ref[FIELDS * i : FIELDS * (i + 1)] = jnp.where(x_odd, low, high)
        row_o_ref[FIELDS * i : FIELDS * (i + 1)] = jnp.where(x_odd, high, low)
    low, high = field_ref[:, 4, :], field_ref[:, 5, :]
    col_e_ref[...] = jnp.where(y_odd, low, high)
    col_o_ref[...] = jnp.where(y_odd, high, low)


def field_kernel(keep_ref, t_ref, dofs_ref, weight_ref, kp_ref, stiff_hbm, pp_ref, pt_ref, tt_ref,
                 table_ref, u_ref, stiff_ref, sems):
    copies = fetch(sems, ((stiff_hbm, stiff_ref),))
    make_tables(table_ref, t_ref[...], keep_ref[KEEP_P : KEEP_P + 8])
    copies[0].wait()

    def rows_of(tile):
        return pl.ds(pl.multiple_of(8 * tile, 8), 8)

    def t_at(c):
        return [u_ref[0, a, c] for a in range(8)]

    @pl.loop(0, EARLY)
    def _(tile):
        rows = rows_of(tile)
        gather_tile(lambda a: dofs_ref[a, rows, :], table_ref, u_ref, 0)
        scale = weight_ref[tile]
        for c in range(CASES):
            pt, tt = t_fields(t_at(c), [kp_ref[tile, a, c] for a in range(8)], stiff_ref)
            pt_ref[tile, c], tt_ref[tile, c] = scale * pt, scale * tt

    @pl.loop(EARLY, pt_ref.shape[0])
    def _(tile):
        rows = rows_of(tile)
        gather_tile(lambda a: dofs_ref[a, rows, :], table_ref, u_ref, 0, 1)
        scale = weight_ref[tile]
        for c in range(CASES):
            p = [u_ref[1, a, c] for a in range(8)]
            kp = [stiff_row(stiff_ref, a, p) for a in range(8)]
            pp = p[0] * kp[0]
            for a in range(1, 8):
                pp = pp + p[a] * kp[a]
            pt, tt = t_fields(t_at(c), kp, stiff_ref)
            pp_ref[tile - EARLY, c], pt_ref[tile, c], tt_ref[tile, c] = scale * pp, scale * pt, scale * tt


def last_kernel(got_ref, coarse_ref, keep_ref, t_ref, early_ref, late_ref, pt_ref, tt_ref,
                mine_ye_ref, mine_yo_ref, xe_ref, xo_ref, ye_ref, yo_ref,
                adj_ref, out_ref):
    total = got_ref[0]
    for d in range(1, got_ref.shape[0]):
        total = total + got_ref[d]
    g, s = total[:CASES], total[CASES:]
    rz, pq, qmq, tlt, pe, te = (s[:, j : j + 1] for j in (RZ, PQ, QMQ, TLT, PE, TE))
    tat = tlt + lane_sum(g * rows_dot(g, coarse_ref[...]))
    alpha = rz / pq
    rz_next = rz - 2.0 * alpha * pq + alpha * alpha * qmq
    grow = 1.0 + rz_next / rz
    pap = grow * grow * (pq + pe) - 2.0 * alpha * grow * (qmq + te) + alpha * alpha * tat
    alpha_next = rz_next / pap
    of_p, of_t = alpha + alpha_next * grow, -(alpha * alpha_next)
    adj_ref[:, 0, :] = of_p * keep_ref[KEEP_P : KEEP_P + 8] + of_t * t_ref[...]

    factors = [of_p * of_p, 2.0 * of_p * of_t, of_t * of_t]
    wide = [jnp.broadcast_to(f, (CASES, LANES)) for f in factors]
    splat = [[jnp.broadcast_to(f[c : c + 1], (8, LANES)) for c in range(CASES)] for f in wide]
    tiles = []
    for i in range(pt_ref.shape[0]):
        tile = None
        pp = early_ref.at[i] if i < EARLY else late_ref.at[i - EARLY]
        for ref, factor in zip((pp, pt_ref.at[i], tt_ref.at[i]), splat):
            for c in range(CASES):
                term = factor[c] * ref[c]
                tile = term if tile is None else tile + term
        tiles.append(tile)
    grad = jnp.concatenate(tiles, axis=0)
    column = jnp.concatenate(wide, axis=0)

    def combine(fields):
        return jnp.sum(column * fields, axis=0, keepdims=True)

    ex, ey = grad.shape
    x_odd, y_odd = is_odd("gx"), is_odd("gy")
    has = []
    for axis in ("gx", "gy"):
        at, size = lax.axis_index(axis), lax.axis_size(axis)
        has += [jnp.where(at > 0, 1.0, 0.0), jnp.where(at < size - 1, 1.0, 0.0)]

    def choose(flag, a, b):
        return jnp.where(jnp.broadcast_to(flag, a.shape), a, b)

    def two(a, b, flag):
        return choose(flag, a, b), choose(flag, b, a)

    rows = [[combine(ref[FIELDS * i : FIELDS * (i + 1)]) for i in range(2)] for ref in (xe_ref, xo_ref)]
    g_below1, g_above1 = two(rows[0][0], rows[1][0], x_odd)
    g_below2, g_above2 = two(rows[0][1], rows[1][1], x_odd)
    before, after = two(combine(ye_ref[...]), combine(yo_ref[...]), y_odd)
    col_low, col_high = two(combine(mine_ye_ref[...]), combine(mine_yo_ref[...]), y_odd)
    wide_lane = lax.broadcasted_iota(jnp.int32, (CASES, LANES), 1)
    of_lane = jnp.where(wide_lane < CORNER_PT, wide[0], jnp.where(wide_lane < CORNER_TT, wide[1], wide[2]))
    x, y = lax.axis_index("gx"), lax.axis_index("gy")
    nx, ny = lax.axis_size("gx"), lax.axis_size("gy")

    def corner_of(dx, dy, there, k):
        whose = jnp.clip(x + dx, 0, nx - 1) * ny + jnp.clip(y + dy, 0, ny - 1)
        row = jnp.sum(of_lane * got_ref[whose, CASES:, :], axis=0, keepdims=True)
        parts = [row[:, at + k : at + k + 1] for at in (CORNER_PP, CORNER_PT, CORNER_TT)]
        return there * (parts[0] + parts[1] + parts[2]) / diag

    corner = [corner_of(-1, -1, has[0] * has[2], 3), corner_of(-1, 1, has[0] * has[3], 2),
              corner_of(1, -1, has[1] * has[2], 1), corner_of(1, 1, has[1] * has[3], 0)]
    lane = lax.broadcasted_iota(jnp.int32, (1, LANES), 1)

    def shifted(row, low, high, length):
        left = jnp.where(lane == 0, low, pltpu.roll(row, 1, 1))
        right = jnp.where(lane == length - 1, high, pltpu.roll(row, LANES - 1, 1))
        return left + right

    def upper(row):
        return pltpu.roll(row, LANES - ex, 1)

    g_before1, g_before2 = upper(before), before
    g_after1, g_after2 = after, upper(after)
    col_first, col_last = col_low, upper(col_high)
    s_below1, s_above1 = g_below1 / diag, g_above1 / diag
    s_before1, s_after1 = g_before1 / diag, g_after1 / diag

    def ring(g1, g2, inner, beside, there):
        return there * (g1 + radius_sq * (g2 / diag + inner / diag + beside)) / diag

    n_below = ring(g_below1, g_below2, grad[0:1], shifted(s_below1, corner[0], corner[1], ey), has[0])
    n_above = ring(g_above1, g_above2, grad[ex - 1 :], shifted(s_above1, corner[2], corner[3], ey), has[1])
    n_before = ring(g_before1, g_before2, col_first, shifted(s_before1, corner[0], corner[2], ex), has[2])
    n_after = ring(g_after1, g_after2, col_last, shifted(s_after1, corner[1], corner[3], ex), has[3])
    stack = jnp.concatenate([s_before1, s_after1, n_before, n_after, jnp.zeros((4, LANES), F32)], axis=0)
    columns = jnp.transpose(stack)[:ex]
    row_no = lax.broadcasted_iota(jnp.int32, (ex, ey), 0)
    col_no = lax.broadcasted_iota(jnp.int32, (ex, ey), 1)

    def sweep(s, below_row, above_row, before_col, after_col):
        down = jnp.where(row_no == 0, below_row, pltpu.roll(s, 1, 0))
        up = jnp.where(row_no == ex - 1, above_row, pltpu.roll(s, ex - 1, 0))
        left = jnp.where(col_no == 0, before_col, pltpu.roll(s, 1, 1))
        right = jnp.where(col_no == ey - 1, after_col, pltpu.roll(s, ey - 1, 1))
        return (grad + radius_sq * (up + down + right + left)) / diag

    s = sweep(grad / diag, s_below1, s_above1, columns[:, 0:1], columns[:, 1:2])
    out_ref[...] = sweep(s, n_below, n_above, columns[:, 2:3], columns[:, 3:4])


def swaps(size):
    out = []
    for first in (0, 1):
        pairs = [(i, i + 1) for i in range(first, size - 1, 2)]
        out.append(pairs + [(j, i) for i, j in pairs])
    return out


def swap_over(array, axis, pairs):
    return lax.ppermute(array, axis, pairs) if pairs else jnp.zeros_like(array)


def f32(*shape):
    return jax.ShapeDtypeStruct(shape, F32)


def s32(*shape):
    return jax.ShapeDtypeStruct(shape, jnp.int32)


def bf16(*shape):
    return jax.ShapeDtypeStruct(shape, BF16)


def call(kernel, name, out_shape, in_specs, scratch, moved):
    single = not isinstance(out_shape, tuple)
    return pl.pallas_call(
        kernel, out_shape=out_shape, in_specs=in_specs,
        out_specs=VMEM if single else (VMEM,) * len(out_shape), scratch_shapes=scratch, name=name,
        compiler_params=pltpu.CompilerParams(vmem_limit_bytes=LIMIT),
        cost_estimate=pl.CostEstimate(flops=1_000_000, bytes_accessed=moved, transcendentals=0),
    )


LIMIT = 6 * 1024 * 1024


def on_device(loads, dual_op, iface, precond, corner_map, coarse_inv, elem_stiff, elem_dofs, density, passive):
    nx, ny = lax.axis_size("gx"), lax.axis_size("gy")
    everyone = nx * ny
    unknowns = dual_op.shape[-1]
    modes = corner_map.shape[1]
    ex, ey = density.shape
    tiles = ex // 8
    x_even, x_odd = swaps(nx)
    y_even, y_odd = swaps(ny)

    def held(array):
        return pltpu.VMEM(array.shape, array.dtype)

    def in_hbm(array):
        return pltpu.with_memory_space_constraint(array, pltpu.HBM)

    def copies(n):
        return pltpu.SemaphoreType.DMA((n,))

    stiff = pltpu.SMEM(elem_stiff.shape, F32)
    one_table = pltpu.VMEM((1, CASES, 8, 8, LANES), F32)
    one_gathered = pltpu.VMEM((1, 8, CASES, 8, LANES), F32)
    table = pltpu.VMEM((2, CASES, 8, 8, LANES), F32)
    gathered = pltpu.VMEM((2, 8, CASES, 8, LANES), F32)

    send = call(first_kernel, "first", f32(everyone, CASES, modes), [HBM] * 3,
                [held(loads), held(precond), held(corner_map), copies(6)], 4_000_000,
                )(in_hbm(loads), in_hbm(precond), in_hbm(corner_map))
    got = lax.all_to_all(send, ("gx", "gy"), 0, 0)

    side = f32(SIDE_C + modes, R)
    params = (loads, dual_op, iface, precond, corner_map)
    keep, mine_e, mine_o = call(
        side_kernel, "sides", (f32(KEEP_S + 8, unknowns), side, side),
        [HBM] * 5, [held(a) for a in params] + [copies(5)], 8_000_000,
    )(*(in_hbm(a) for a in params))
    theirs_e = swap_over(mine_e, "gx", x_even)
    theirs_o = swap_over(mine_o, "gx", x_odd)

    field = f32(EARLY + 1, CASES, 8, LANES)
    params = (iface, corner_map, elem_stiff, density, passive)
    index, inverse, chigh, clow, pack, weight, spot, spot_kp, kp, pp = call(
        early_kernel, "early",
        (s32(2, 8, R), s32(2, 8, unknowns), bf16(modes, unknowns), bf16(modes, unknowns), s32(8, 8, LANES),
         f32(tiles + 1, 8, LANES), s32(8, LANES), f32(10, 8, LANES), f32(EARLY + 1, 8, CASES, 8, LANES), field),
        [VMEM] * 2 + [HBM] * 5,
        [one_table, one_gathered] + [stiff if a is elem_stiff else held(a) for a in params] + [copies(5)], 18_000_000,
    )(keep, elem_dofs, *(in_hbm(a) for a in params))
    got, spot = lax.optimization_barrier((got, spot))

    send, t = call(
        second_kernel, "second", (f32(everyone, 2 * CASES, modes), f32(CASES, unknowns)),
        [VMEM] * 13 + [HBM] * 3, [held(precond), held(dual_op), stiff, copies(3)], 9_000_000,
    )(got, keep, mine_e, mine_o, theirs_e, theirs_o, index, inverse, spot, spot_kp, coarse_inv, chigh, clow,
      in_hbm(precond), in_hbm(dual_op), in_hbm(elem_stiff))
    got = lax.all_to_all(send, ("gx", "gy"), 0, 0)

    row = f32(2 * FIELDS, LANES)
    col = f32(FIELDS, LANES)
    row_e, row_o, col_e, col_o = call(
        edge_kernel, "edges", (row, row, col, col), [VMEM] * 5 + [HBM],
        [one_table, one_gathered, pltpu.VMEM((FIELDS, 8, LANES), F32), stiff, copies(1)], 4_000_000,
    )(t, pack, weight, kp, pp, in_hbm(elem_stiff))
    near = [swap_over(row_e, "gx", x_even), swap_over(row_o, "gx", x_odd),
            swap_over(col_e, "gy", y_even), swap_over(col_o, "gy", y_odd)]

    late, pt, tt = call(
        field_kernel, "fields",
        (f32(tiles - EARLY, CASES, 8, LANES), f32(tiles, CASES, 8, LANES), f32(tiles, CASES, 8, LANES)),
        [VMEM] * 5 + [HBM], [table, gathered, stiff, copies(1)], 36_000_000,
    )(keep, t, elem_dofs, weight, kp, in_hbm(elem_stiff))

    adjoint, sens = call(
        last_kernel, "last", (f32(CASES, 1, unknowns), f32(ex, ey)), [VMEM] * 14, [], 4_000_000,
    )(got, coarse_inv, keep, t, pp, late, pt, tt, col_e, col_o, *near)
    return adjoint, sens


def solution(mesh):
    placed = (
        P(None, "gy", "gx"),
        P("gy", "gx", None),
        P("gy", "gx", None),
        P("gy", "gx"),
        P("gy", None, "gx"),
        P(),
        P(),
        P(None, "gx", "gy"),
        P("gx", "gy"),
        P("gx", "gy"),
    )
    return jax.shard_map(
        on_device,
        mesh=mesh,
        in_specs=placed,
        out_specs=(P(None, "gy", "gx"), P("gx", "gy")),
        check_vma=False,
    )
```

```python
import jax
import jax.numpy as jnp
from jax import lax
from jax.experimental import pallas as pl
from jax.experimental.pallas import tpu as pltpu
from jax.sharding import PartitionSpec as P

R = 128
LANES = 128
CASES = 8

coupling = 0.3
radius_sq = 2.0
penalty = 3.0
diag = 1.0 + 4.0 * radius_sq

HI = lax.Precision.HIGHEST
F32 = jnp.float32
BF16 = jnp.bfloat16
VMEM = pl.BlockSpec(memory_space=pltpu.VMEM)
HBM = pl.BlockSpec(memory_space=pltpu.HBM)

SIDE_P, SIDE_Y, SIDE_M, SIDE_C = 0, 8, 16, 24
RZ, PE, PQ, QMQ, TLT, TE = range(6)
KEEP_P, KEEP_Y, KEEP_REST, KEEP_S = 0, 8, 16, 24
FIELDS = 3 * CASES
EARLY = 5
CORNER_PP, CORNER_PT, CORNER_TT = 8, 12, 16


def rows_dot(a, b):
    return lax.dot_general(a, b, (((1,), (1,)), ((), ())), precision=HI, preferred_element_type=F32)


def plain_dot(a, b):
    return lax.dot_general(a, b, (((1,), (0,)), ((), ())), precision=HI, preferred_element_type=F32)


def halves(x):
    high = x.astype(BF16)
    low = (x - high.astype(F32)).astype(BF16)
    return jnp.concatenate([high, low], axis=0)


def split(x):
    high = x.astype(BF16)
    return high, (x - high.astype(F32)).astype(BF16)


def split_dot(a, pair, dim):
    stack = halves(a)
    dims = (((1,), (dim,)), ((), ()))
    main = lax.dot_general(stack, pair[0], dims, preferred_element_type=F32)
    rest = lax.dot_general(stack, pair[1], dims, preferred_element_type=F32)
    return main[:8] + main[8:] + rest[:8]


def lane_sum(x):
    return jnp.sum(x, axis=1, keepdims=True)


def pattern(idx):
    return idx & (LANES - 1), (idx & 128) != 0, (idx & 256) != 0, (idx & 512) != 0


def pick(blocks, where):
    lane, bit0, bit1, bit2 = where
    got = [jnp.take_along_axis(b, lane, axis=1, mode="promise_in_bounds") for b in blocks]
    got = [jnp.where(bit0, got[2 * i + 1], got[2 * i]) for i in range(4)]
    got = [jnp.where(bit1, got[2 * i + 1], got[2 * i]) for i in range(2)]
    return jnp.where(bit2, got[1], got[0])


def blocks_of(row8):
    return [row8[:, LANES * h : LANES * (h + 1)] for h in range(8)]


def is_odd(axis):
    return lax.axis_index(axis) & 1 == 1


def sides_there(axis):
    at, size = lax.axis_index(axis), lax.axis_size(axis)
    return jnp.where(at > 0, 1.0, 0.0), jnp.where(at < size - 1, 1.0, 0.0)


def op_dot(vec, op_ref):
    out = lax.dot_general(halves(vec), op_ref[0], (((1,), (1,)), ((), ())), preferred_element_type=F32)
    return out[:CASES], out[CASES:]


def at_lanes(columns, first=0):
    lane = lax.broadcasted_iota(jnp.int32, (CASES, LANES), 1)
    block = jnp.zeros((CASES, LANES), F32)
    for j, column in enumerate(columns):
        block = jnp.where(lane == first + j, column, block)
    return block


def fetch(sems, pairs):
    copies = [pltpu.make_async_copy(a, b, sems.at[i]) for i, (a, b) in enumerate(pairs)]
    for copy in copies:
        copy.start()
    return copies


def first_kernel(loads_hbm, pre_hbm, corner_hbm, send_ref, loads_ref, pre_ref, corner_ref, sems):
    piece = corner_ref.shape[2] // 4
    parts = [pl.ds(piece * i, piece) for i in range(4)]
    copies = fetch(sems, [(loads_hbm, loads_ref), (pre_hbm, pre_ref)]
                   + [(corner_hbm.at[:, :, k], corner_ref.at[:, :, k]) for k in parts])
    copies[0].wait()
    copies[1].wait()
    p = pre_ref[...] * loads_ref[:, 0, :]
    part = None
    for i, k in enumerate(parts):
        copies[2 + i].wait()
        term = split_dot(p[:, piece * i : piece * (i + 1)], split(corner_ref[0, :, k]), 1)
        part = term if part is None else part + term
    for d in range(send_ref.shape[0]):
        send_ref[d] = part


def edge_tiles(first, second):
    ex, ey = first.shape
    lane = lax.broadcasted_iota(jnp.int32, (1, LANES), 1)
    turned = jnp.transpose(jnp.concatenate([first, second], axis=0))
    swapped = pltpu.roll(turned, LANES - ex, 1)
    out = []
    for array, low, high in ((first, turned, swapped), (second, swapped, turned)):
        cols = [jnp.where(lane < ex, low[j : j + 1], high[j + 1 : j + 2]) for j in (0, ey - 2)]
        out.append(jnp.concatenate([array[0:2], array[ex - 2 :]] + cols + [array[0:2]], axis=0))
    return out


def corner_lanes(low, high):
    lane = lax.broadcasted_iota(jnp.int32, low.shape, 1)
    out = jnp.where(lane == 0, low, jnp.where(lane == 1, pltpu.roll(low, 2, 1), 0))
    return jnp.where(lane == 2, pltpu.roll(high, 2, 1), jnp.where(lane == 3, pltpu.roll(high, 4, 1), out))


def corner_values(vec, where):
    return [pick(blocks_of(vec), pattern(jnp.broadcast_to(where[a : a + 1], (8, LANES)))) for a in range(8)]


def stiff_row(stiff_ref, a, u):
    v = stiff_ref[a, 0] * u[0]
    for b in range(1, 8):
        v = v + stiff_ref[a, b] * u[b]
    return v


def side_indices(iface_ref):
    left = jnp.broadcast_to(iface_ref[0, :, :R], (8, R))
    right = jnp.broadcast_to(iface_ref[0, :, R : 2 * R], (8, R))
    x_odd = jnp.broadcast_to(is_odd("gx"), (8, R))
    return jnp.where(x_odd, left, right), jnp.where(x_odd, right, left)


def side_kernel(loads_hbm, op_hbm, iface_hbm, pre_hbm, corner_hbm,
                keep_ref, even_ref, odd_ref, index_ref, inverse_ref, chigh_ref, clow_ref,
                loads_ref, op_ref, iface_ref, pre_ref, corner_ref, sems):
    copies = fetch(sems, ((loads_hbm, loads_ref), (pre_hbm, pre_ref), (iface_hbm, iface_ref),
                          (corner_hbm, corner_ref), (op_hbm, op_ref)))
    for copy in copies[:4]:
        copy.wait()
    loads = loads_ref[:, 0, :]
    p = pre_ref[...] * loads
    keep_ref[KEEP_P : KEEP_P + 8] = p
    pre = jnp.broadcast_to(pre_ref[...], (8, pre_ref.shape[1]))
    chosen = []
    for idx, out in zip(side_indices(iface_ref), (even_ref, odd_ref)):
        where = pattern(idx)
        scale = pick(blocks_of(pre), where)
        chosen.append((where, scale, out))
        out[SIDE_P : SIDE_P + 8] = pick(blocks_of(p), where)
        out[SIDE_M : SIDE_M + 8] = scale
        for j in range(corner_ref.shape[1] // 8):
            rows = corner_ref[0, 8 * j : 8 * j + 8]
            out[SIDE_C + 8 * j : SIDE_C + 8 * j + 8] = scale * pick(blocks_of(rows), where)
    for side, idx in enumerate(side_indices(iface_ref)):
        index_ref[side] = idx
        column = jnp.transpose(jnp.broadcast_to(idx[0:1], (R, R)))
        number = lax.broadcasted_iota(jnp.int32, (R, LANES), 0) + 1
        for h in range(8):
            at = lax.broadcasted_iota(jnp.int32, (R, LANES), 1) + LANES * h
            found = jnp.sum(jnp.where(column == at, number, 0), axis=0, keepdims=True)
            inverse_ref[side, :, LANES * h : LANES * (h + 1)] = jnp.broadcast_to(found, (8, LANES))
    chigh_ref[...], clow_ref[...] = split(corner_ref[0])
    copies[4].wait()
    y, rest = op_dot(p, op_ref)
    keep_ref[KEEP_Y : KEEP_Y + 8] = y
    keep_ref[KEEP_REST : KEEP_REST + 8] = rest
    keep_ref[KEEP_S : KEEP_S + 8, :LANES] = at_lanes((lane_sum(loads * p), lane_sum(p * rest)))
    for where, scale, out in chosen:
        out[SIDE_Y : SIDE_Y + 8] = scale * pick(blocks_of(y), where)


def early_kernel(keep_ref, dofs_ref, stiff_hbm, density_hbm, passive_hbm,
                 pack_ref, weight_ref, spot_ref, spot_kp_ref,
                 kp_ref, pp_ref, table_ref, u_ref, other_ref, all_dofs_ref, all_weight_ref,
                 stiff_ref, density_ref, passive_ref, sems):
    copies = fetch(sems, ((stiff_hbm, stiff_ref), (density_hbm, density_ref), (passive_hbm, passive_ref)))
    p = keep_ref[KEEP_P : KEEP_P + 8]
    make_tables(table_ref, p)
    for a in range(0, 8, 2):
        first, second = edge_tiles(dofs_ref[a].astype(F32), dofs_ref[a + 1].astype(F32))
        pack_ref[a] = first.astype(jnp.int32)
        pack_ref[a + 1] = second.astype(jnp.int32)
    for copy in copies:
        copy.wait()
    rho = density_ref[...]
    weight = jnp.where(passive_ref[...] == 1, 0.0, -penalty * rho * rho)
    ex = weight.shape[0]
    for i in range(ex // 8):
        weight_ref[i] = weight[8 * i : 8 * i + 8]
    weight_ref[ex // 8] = edge_tiles(weight, weight)[0]
    spot = corner_lanes(dofs_ref[:, 0, :], dofs_ref[:, ex - 1, :])
    spot_ref[...] = spot
    spot_weight = jnp.broadcast_to(corner_lanes(weight[0:1], weight[ex - 1 :]), (8, LANES))
    u = corner_values(p, spot)
    pp = None
    for a in range(8):
        v = stiff_row(stiff_ref, a, u)
        spot_kp_ref[a] = spot_weight * v
        pp = u[a] * v if pp is None else pp + u[a] * v
    lane = lax.broadcasted_iota(jnp.int32, (CASES, LANES), 1)
    spot_kp_ref[8] = spot_weight
    spot_kp_ref[9] = pltpu.roll(jnp.where(lane < 4, spot_weight * pp, 0.0), CORNER_PP, 1)

    for i in range(EARLY):
        for a in range(8):
            all_dofs_ref[i, a] = dofs_ref[a, 8 * i : 8 * i + 8]
        all_weight_ref[i] = weight[8 * i : 8 * i + 8]
    for a in range(8):
        all_dofs_ref[EARLY, a] = pack_ref[a]
    all_weight_ref[EARLY] = weight_ref[ex // 8]

    def gather(i, ref):
        gather_tile(lambda a: all_dofs_ref[i, a], table_ref, ref, 0)

    def fields(i, ref):
        scale = all_weight_ref[i]
        for c in range(CASES):
            u = [ref[0, a, c] for a in range(8)]
            pp = None
            for a in range(8):
                v = stiff_row(stiff_ref, a, u)
                kp_ref[i, a, c] = v
                pp = u[a] * v if pp is None else pp + u[a] * v
            pp_ref[i, c] = scale * pp

    staggered(EARLY + 1, gather, fields, (u_ref, other_ref))


def spread(values, inverse):
    out = []
    for h in range(8):
        at = inverse[:, LANES * h : LANES * (h + 1)]
        got = jnp.take_along_axis(values, jnp.maximum(at - 1, 0), axis=1, mode="promise_in_bounds")
        out.append(jnp.where(at > 0, got, 0.0))
    return jnp.concatenate(out, axis=1)


def second_kernel(got_ref, keep_ref, mine_e_ref, mine_o_ref, theirs_e_ref, theirs_o_ref, index_ref, inverse_ref,
                  spot_ref, spot_kp_ref, coarse_ref, chigh_ref, clow_ref, pre_hbm, op_hbm, stiff_hbm,
                  send_ref, t_ref, pre_ref, op_ref, stiff_ref, sems):
    copies = fetch(sems, ((pre_hbm, pre_ref), (stiff_hbm, stiff_ref), (op_hbm, op_ref)))
    total = got_ref[0]
    for d in range(1, got_ref.shape[0]):
        total = total + got_ref[d]
    corner = chigh_ref[...], clow_ref[...]
    p = keep_ref[KEEP_P : KEEP_P + 8]
    base = keep_ref[KEEP_Y : KEEP_Y + 8]
    pairs = ((mine_e_ref, theirs_e_ref), (mine_o_ref, theirs_o_ref))
    below, above = sides_there("gx")
    x_odd = is_odd("gx")
    couplings = [-coupling * jnp.where(x_odd, a, b) for a, b in ((below, above), (above, below))]
    for side, (_, theirs) in enumerate(pairs):
        base = base + spread(couplings[side] * theirs[SIDE_P : SIDE_P + 8], inverse_ref[side])
    w = split_dot(total, split(coarse_ref[...]), 1)
    q = base + split_dot(w, corner, 0)
    copies[0].wait()
    t = pre_ref[...] * q
    t_ref[...] = t
    g = split_dot(t, corner, 1)
    tlt = None
    for side, (mine, theirs) in enumerate(pairs):
        t_mine = pick(blocks_of(t), pattern(index_ref[side]))
        t_theirs = theirs[SIDE_Y : SIDE_Y + 8] - coupling * theirs[SIDE_M : SIDE_M + 8] * mine[SIDE_P : SIDE_P + 8]
        t_theirs = t_theirs + split_dot(w, split(theirs[SIDE_C:]), 0)
        term = couplings[side] * lane_sum(t_mine * t_theirs)
        tlt = term if tlt is None else tlt + term
    copies[1].wait()
    u = corner_values(t, spot_ref[...])
    pt = tt = None
    for a in range(8):
        one, two = u[a] * spot_kp_ref[a], u[a] * stiff_row(stiff_ref, a, u)
        pt, tt = (one, two) if pt is None else (pt + one, tt + two)
    lane = lax.broadcasted_iota(jnp.int32, (CASES, LANES), 1)
    pt, tt = jnp.where(lane < 4, pt, 0.0), jnp.where(lane < 4, spot_kp_ref[8] * tt, 0.0)
    rest = keep_ref[KEEP_REST : KEEP_REST + 8]
    block = keep_ref[KEEP_S : KEEP_S + 8, :LANES]
    block = block + spot_kp_ref[9] + pltpu.roll(pt, CORNER_PT, 1) + pltpu.roll(tt, CORNER_TT, 1)
    block = block + at_lanes((lane_sum(p * q), lane_sum(q * t), tlt, lane_sum(t * rest)), PQ)
    for d in range(send_ref.shape[0]):
        send_ref[d, :CASES] = g
    copies[2].wait()
    high, low = op_dot(t, op_ref)
    block = block + at_lanes((lane_sum(t * (high + low)),), TLT)
    for d in range(send_ref.shape[0]):
        send_ref[d, CASES:] = block


def make_tables(table_ref, *vectors):
    for i, vec in enumerate(vectors):
        for c in range(CASES):
            for h in range(8):
                row = vec[c : c + 1, LANES * h : LANES * (h + 1)]
                table_ref[i, c, h] = jnp.broadcast_to(row, (8, LANES))


def gather_tile(dofs, table_ref, u_ref, *which):
    for a in range(8):
        where = pattern(dofs(a))
        for c in range(CASES):
            for i in which:
                u_ref[i, a, c] = pick([table_ref[i, c, h] for h in range(8)], where)


def staggered(count, gather, fields, refs, ready=()):
    gather(0, refs[0])
    for copy in ready:
        copy.wait()
    pairs = (count - 1) // 2

    @pl.loop(0, pairs)
    def _(k):
        i = 2 * k
        gather(i + 1, refs[1])
        fields(i, refs[0])
        gather(i + 2, refs[0])
        fields(i + 1, refs[1])

    if count % 2 == 0:
        gather(count - 1, refs[1])
        fields(count - 2, refs[0])
        fields(count - 1, refs[1])
    else:
        fields(count - 1, refs[0])


def t_fields(t, kp, stiff_ref):
    pt = tt = None
    for a in range(8):
        w = stiff_ref[a, a] * t[a]
        for b in range(a + 1, 8):
            w = w + (stiff_ref[a, b] + stiff_ref[b, a]) * t[b]
        one, two = t[a] * kp[a], t[a] * w
        pt, tt = (one, two) if pt is None else (pt + one, tt + two)
    return pt, tt


def edge_kernel(t_ref, pack_ref, weight_ref, kp_ref, pp_ref, stiff_hbm,
                row_e_ref, row_o_ref, col_e_ref, col_o_ref, table_ref, u_ref, field_ref, stiff_ref, sems):
    copies = fetch(sems, ((stiff_hbm, stiff_ref),))
    make_tables(table_ref, t_ref[...])
    gather_tile(lambda a: pack_ref[a], table_ref, u_ref, 0)
    copies[0].wait()
    scale = weight_ref[weight_ref.shape[0] - 1]
    for c in range(CASES):
        pt, tt = t_fields([u_ref[0, a, c] for a in range(8)], [kp_ref[EARLY, a, c] for a in range(8)], stiff_ref)
        field_ref[c] = pp_ref[EARLY, c]
        field_ref[CASES + c] = scale * pt
        field_ref[2 * CASES + c] = scale * tt
    x_odd = jnp.broadcast_to(is_odd("gx"), (FIELDS, LANES))
    y_odd = jnp.broadcast_to(is_odd("gy"), (FIELDS, LANES))
    for i in range(2):
        low, high = field_ref[:, i, :], field_ref[:, 3 - i, :]
        row_e_ref[FIELDS * i : FIELDS * (i + 1)] = jnp.where(x_odd, low, high)
        row_o_ref[FIELDS * i : FIELDS * (i + 1)] = jnp.where(x_odd, high, low)
    low, high = field_ref[:, 4, :], field_ref[:, 5, :]
    col_e_ref[...] = jnp.where(y_odd, low, high)
    col_o_ref[...] = jnp.where(y_odd, high, low)


def field_kernel(keep_ref, t_ref, dofs_ref, weight_ref, kp_ref, stiff_hbm, pp_ref, pt_ref, tt_ref,
                 table_ref, u_ref, other_ref, stiff_ref, sems):
    copies = fetch(sems, ((stiff_hbm, stiff_ref),))
    make_tables(table_ref, t_ref[...], keep_ref[KEEP_P : KEEP_P + 8])

    def rows_of(tile):
        return pl.ds(pl.multiple_of(8 * tile, 8), 8)

    def t_at(ref, c):
        return [ref[0, a, c] for a in range(8)]

    def gather(tile, ref):
        gather_tile(lambda a: dofs_ref[a, rows_of(tile), :], table_ref, ref, 0)

    def fields(tile, ref):
        scale = weight_ref[tile]
        for c in range(CASES):
            pt, tt = t_fields(t_at(ref, c), [kp_ref[tile, a, c] for a in range(8)], stiff_ref)
            pt_ref[tile, c], tt_ref[tile, c] = scale * pt, scale * tt

    staggered(EARLY, gather, fields, (u_ref, other_ref), copies)

    def gather_both(i, ref):
        gather_tile(lambda a: dofs_ref[a, rows_of(i + EARLY), :], table_ref, ref, 0, 1)

    def fields_both(i, ref):
        scale = weight_ref[i + EARLY]
        for c in range(CASES):
            p = [ref[1, a, c] for a in range(8)]
            kp = [stiff_row(stiff_ref, a, p) for a in range(8)]
            pp = p[0] * kp[0]
            for a in range(1, 8):
                pp = pp + p[a] * kp[a]
            pt, tt = t_fields(t_at(ref, c), kp, stiff_ref)
            pp_ref[i, c], pt_ref[i + EARLY, c], tt_ref[i + EARLY, c] = scale * pp, scale * pt, scale * tt

    staggered(pt_ref.shape[0] - EARLY, gather_both, fields_both, (u_ref, other_ref))


def last_kernel(got_ref, coarse_ref, keep_ref, t_ref, early_ref, late_ref, pt_ref, tt_ref,
                mine_ye_ref, mine_yo_ref, xe_ref, xo_ref, ye_ref, yo_ref,
                adj_ref, out_ref):
    total = got_ref[0]
    for d in range(1, got_ref.shape[0]):
        total = total + got_ref[d]
    g, s = total[:CASES], total[CASES:]
    rz, pq, qmq, tlt, pe, te = (s[:, j : j + 1] for j in (RZ, PQ, QMQ, TLT, PE, TE))
    tat = tlt + lane_sum(g * rows_dot(g, coarse_ref[...]))
    alpha = rz / pq
    rz_next = rz - 2.0 * alpha * pq + alpha * alpha * qmq
    grow = 1.0 + rz_next / rz
    pap = grow * grow * (pq + pe) - 2.0 * alpha * grow * (qmq + te) + alpha * alpha * tat
    alpha_next = rz_next / pap
    of_p, of_t = alpha + alpha_next * grow, -(alpha * alpha_next)
    adj_ref[:, 0, :] = of_p * keep_ref[KEEP_P : KEEP_P + 8] + of_t * t_ref[...]

    factors = [of_p * of_p, 2.0 * of_p * of_t, of_t * of_t]
    wide = [jnp.broadcast_to(f, (CASES, LANES)) for f in factors]
    splat = [[jnp.broadcast_to(f[c : c + 1], (8, LANES)) for c in range(CASES)] for f in wide]
    tiles = []
    for i in range(pt_ref.shape[0]):
        tile = None
        pp = early_ref.at[i] if i < EARLY else late_ref.at[i - EARLY]
        for ref, factor in zip((pp, pt_ref.at[i], tt_ref.at[i]), splat):
            for c in range(CASES):
                term = factor[c] * ref[c]
                tile = term if tile is None else tile + term
        tiles.append(tile)
    grad = jnp.concatenate(tiles, axis=0)
    column = jnp.concatenate(wide, axis=0)

    def combine(fields):
        return jnp.sum(column * fields, axis=0, keepdims=True)

    ex, ey = grad.shape
    x_odd, y_odd = is_odd("gx"), is_odd("gy")
    has = sides_there("gx") + sides_there("gy")

    def choose(flag, a, b):
        return jnp.where(jnp.broadcast_to(flag, a.shape), a, b)

    def two(a, b, flag):
        return choose(flag, a, b), choose(flag, b, a)

    def both(values, there):
        return [v * flag for v, flag in zip(values, there)]

    rows = [[combine(ref[FIELDS * i : FIELDS * (i + 1)]) for i in range(2)] for ref in (xe_ref, xo_ref)]
    g_below1, g_above1 = both(two(rows[0][0], rows[1][0], x_odd), has[:2])
    g_below2, g_above2 = both(two(rows[0][1], rows[1][1], x_odd), has[:2])
    before, after = both(two(combine(ye_ref[...]), combine(yo_ref[...]), y_odd), has[2:])
    col_low, col_high = two(combine(mine_ye_ref[...]), combine(mine_yo_ref[...]), y_odd)
    wide_lane = lax.broadcasted_iota(jnp.int32, (CASES, LANES), 1)
    of_lane = jnp.where(wide_lane < CORNER_PT, wide[0], jnp.where(wide_lane < CORNER_TT, wide[1], wide[2]))
    x, y = lax.axis_index("gx"), lax.axis_index("gy")
    nx, ny = lax.axis_size("gx"), lax.axis_size("gy")

    def corner_of(dx, dy, there, k):
        whose = jnp.clip(x + dx, 0, nx - 1) * ny + jnp.clip(y + dy, 0, ny - 1)
        row = jnp.sum(of_lane * got_ref[whose, CASES:, :], axis=0, keepdims=True)
        parts = [row[:, at + k : at + k + 1] for at in (CORNER_PP, CORNER_PT, CORNER_TT)]
        return there * (parts[0] + parts[1] + parts[2]) / diag

    corner = [corner_of(-1, -1, has[0] * has[2], 3), corner_of(-1, 1, has[0] * has[3], 2),
              corner_of(1, -1, has[1] * has[2], 1), corner_of(1, 1, has[1] * has[3], 0)]
    lane = lax.broadcasted_iota(jnp.int32, (1, LANES), 1)

    def shifted(row, low, high, length):
        left = jnp.where(lane == 0, low, pltpu.roll(row, 1, 1))
        right = jnp.where(lane == length - 1, high, pltpu.roll(row, LANES - 1, 1))
        return left + right

    def upper(row):
        return pltpu.roll(row, LANES - ex, 1)

    g_before1, g_before2 = upper(before), before
    g_after1, g_after2 = after, upper(after)
    col_first, col_last = col_low, upper(col_high)
    s_below1, s_above1 = g_below1 / diag, g_above1 / diag
    s_before1, s_after1 = g_before1 / diag, g_after1 / diag

    def ring(g1, g2, inner, beside, there):
        return there * (g1 + radius_sq * (g2 / diag + inner / diag + beside)) / diag

    n_below = ring(g_below1, g_below2, grad[0:1], shifted(s_below1, corner[0], corner[1], ey), has[0])
    n_above = ring(g_above1, g_above2, grad[ex - 1 :], shifted(s_above1, corner[2], corner[3], ey), has[1])
    n_before = ring(g_before1, g_before2, col_first, shifted(s_before1, corner[0], corner[2], ex), has[2])
    n_after = ring(g_after1, g_after2, col_last, shifted(s_after1, corner[1], corner[3], ex), has[3])
    stack = jnp.concatenate([s_before1, s_after1, n_before, n_after, jnp.zeros((4, LANES), F32)], axis=0)
    columns = jnp.transpose(stack)[:ex]
    row_no = lax.broadcasted_iota(jnp.int32, (ex, ey), 0)
    col_no = lax.broadcasted_iota(jnp.int32, (ex, ey), 1)

    def sweep(s, below_row, above_row, before_col, after_col):
        down = jnp.where(row_no == 0, below_row, pltpu.roll(s, 1, 0))
        up = jnp.where(row_no == ex - 1, above_row, pltpu.roll(s, ex - 1, 0))
        left = jnp.where(col_no == 0, before_col, pltpu.roll(s, 1, 1))
        right = jnp.where(col_no == ey - 1, after_col, pltpu.roll(s, ey - 1, 1))
        return (grad + radius_sq * (up + down + right + left)) / diag

    s = sweep(grad / diag, s_below1, s_above1, columns[:, 0:1], columns[:, 1:2])
    out_ref[...] = sweep(s, n_below, n_above, columns[:, 2:3], columns[:, 3:4])


def swaps(size):
    out = []
    for first in (0, 1):
        pairs = [(i, i + 1) for i in range(first, size - 1, 2)]
        if first == 1 and size % 2 == 0 and size > 2:
            pairs.append((size - 1, 0))
        out.append(pairs + [(j, i) for i, j in pairs])
    return out


def swap_over(array, axis, pairs):
    return lax.ppermute(array, axis, pairs) if pairs else jnp.zeros_like(array)


def f32(*shape):
    return jax.ShapeDtypeStruct(shape, F32)


def s32(*shape):
    return jax.ShapeDtypeStruct(shape, jnp.int32)


def bf16(*shape):
    return jax.ShapeDtypeStruct(shape, BF16)


def call(kernel, name, out_shape, in_specs, scratch, moved):
    single = not isinstance(out_shape, tuple)
    return pl.pallas_call(
        kernel, out_shape=out_shape, in_specs=in_specs,
        out_specs=VMEM if single else (VMEM,) * len(out_shape), scratch_shapes=scratch, name=name,
        compiler_params=pltpu.CompilerParams(vmem_limit_bytes=LIMIT),
        cost_estimate=pl.CostEstimate(flops=1_000_000, bytes_accessed=moved, transcendentals=0),
    )


LIMIT = 6 * 1024 * 1024


def on_device(loads, dual_op, iface, precond, corner_map, coarse_inv, elem_stiff, elem_dofs, density, passive):
    nx, ny = lax.axis_size("gx"), lax.axis_size("gy")
    everyone = nx * ny
    unknowns = dual_op.shape[-1]
    modes = corner_map.shape[1]
    ex, ey = density.shape
    tiles = ex // 8
    x_even, x_odd = swaps(nx)
    y_even, y_odd = swaps(ny)

    def held(array):
        return pltpu.VMEM(array.shape, array.dtype)

    def in_hbm(array):
        return pltpu.with_memory_space_constraint(array, pltpu.HBM)

    def copies(n):
        return pltpu.SemaphoreType.DMA((n,))

    stiff = pltpu.SMEM(elem_stiff.shape, F32)
    one_table = pltpu.VMEM((1, CASES, 8, 8, LANES), F32)
    one_gathered = pltpu.VMEM((1, 8, CASES, 8, LANES), F32)
    table = pltpu.VMEM((2, CASES, 8, 8, LANES), F32)
    gathered = pltpu.VMEM((2, 8, CASES, 8, LANES), F32)

    send = call(first_kernel, "first", f32(everyone, CASES, modes), [HBM] * 3,
                [held(loads), held(precond), held(corner_map), copies(6)], 4_000_000,
                )(in_hbm(loads), in_hbm(precond), in_hbm(corner_map))
    got = lax.all_to_all(send, ("gx", "gy"), 0, 0)

    side = f32(SIDE_C + modes, R)
    params = (loads, dual_op, iface, precond, corner_map)
    keep, mine_e, mine_o, index, inverse, chigh, clow = call(
        side_kernel, "sides",
        (f32(KEEP_S + 8, unknowns), side, side, s32(2, 8, R), s32(2, 8, unknowns), bf16(modes, unknowns),
         bf16(modes, unknowns)),
        [HBM] * 5, [held(a) for a in params] + [copies(5)], 8_000_000,
    )(*(in_hbm(a) for a in params))
    theirs_o = swap_over(mine_o, "gx", x_odd)
    theirs_e = swap_over(mine_e, "gx", x_even)

    field = f32(EARLY + 1, CASES, 8, LANES)
    params = (elem_stiff, density, passive)
    pack, weight, spot, spot_kp, kp, pp = call(
        early_kernel, "early",
        (s32(8, 8, LANES), f32(tiles + 1, 8, LANES), s32(8, LANES), f32(10, 8, LANES), f32(EARLY + 1, 8, CASES, 8, LANES), field),
        [VMEM] * 2 + [HBM] * 3,
        [one_table, one_gathered, one_gathered, pltpu.VMEM((EARLY + 1, 8, 8, LANES), jnp.int32),
         pltpu.VMEM((EARLY + 1, 8, LANES), F32)] + [stiff if a is elem_stiff else held(a) for a in params] + [copies(3)], 18_000_000,
    )(keep, elem_dofs, *(in_hbm(a) for a in params))
    got, spot = lax.optimization_barrier((got, spot))

    send, t = call(
        second_kernel, "second", (f32(everyone, 2 * CASES, modes), f32(CASES, unknowns)),
        [VMEM] * 13 + [HBM] * 3, [held(precond), held(dual_op), stiff, copies(3)], 9_000_000,
    )(got, keep, mine_e, mine_o, theirs_e, theirs_o, index, inverse, spot, spot_kp, coarse_inv, chigh, clow,
      in_hbm(precond), in_hbm(dual_op), in_hbm(elem_stiff))
    got = lax.all_to_all(send, ("gx", "gy"), 0, 0)

    row = f32(2 * FIELDS, LANES)
    col = f32(FIELDS, LANES)
    row_e, row_o, col_e, col_o = call(
        edge_kernel, "edges", (row, row, col, col), [VMEM] * 5 + [HBM],
        [one_table, one_gathered, pltpu.VMEM((FIELDS, 8, LANES), F32), stiff, copies(1)], 4_000_000,
    )(t, pack, weight, kp, pp, in_hbm(elem_stiff))
    ye, yo = swap_over(col_e, "gy", y_even), swap_over(col_o, "gy", y_odd)
    xo = swap_over(row_o, "gx", x_odd)
    xe = swap_over(row_e, "gx", x_even)

    late, pt, tt = call(
        field_kernel, "fields",
        (f32(tiles - EARLY, CASES, 8, LANES), f32(tiles, CASES, 8, LANES), f32(tiles, CASES, 8, LANES)),
        [VMEM] * 5 + [HBM], [table, gathered, gathered, stiff, copies(1)], 36_000_000,
    )(keep, t, elem_dofs, weight, kp, in_hbm(elem_stiff))

    adjoint, sens = call(
        last_kernel, "last", (f32(CASES, 1, unknowns), f32(ex, ey)), [VMEM] * 14, [], 4_000_000,
    )(got, coarse_inv, keep, t, pp, late, pt, tt, col_e, col_o, xe, xo, ye, yo)
    return adjoint, sens


def solution(mesh):
    placed = (
        P(None, "gy", "gx"),
        P("gy", "gx", None),
        P("gy", "gx", None),
        P("gy", "gx"),
        P("gy", None, "gx"),
        P(),
        P(),
        P(None, "gx", "gy"),
        P("gx", "gy"),
        P("gx", "gy"),
    )
    return jax.shard_map(
        on_device,
        mesh=mesh,
        in_specs=placed,
        out_specs=(P(None, "gy", "gx"), P("gx", "gy")),
        check_vma=False,
    )
```

```python
import jax
import jax.numpy as jnp
from jax import lax
from jax.experimental import pallas as pl
from jax.experimental.pallas import tpu as pltpu
from jax.sharding import PartitionSpec as P

R = 128
LANES = 128
CASES = 8

coupling = 0.3
radius_sq = 2.0
penalty = 3.0
diag = 1.0 + 4.0 * radius_sq

HI = lax.Precision.HIGHEST
F32 = jnp.float32
BF16 = jnp.bfloat16
VMEM = pl.BlockSpec(memory_space=pltpu.VMEM)
HBM = pl.BlockSpec(memory_space=pltpu.HBM)

SIDE_P, SIDE_Y, SIDE_M, SIDE_C = 0, 8, 16, 24
RZ, PE, PQ, QMQ, TLT, TE = range(6)
KEEP_P, KEEP_Y, KEEP_REST, KEEP_S = 0, 8, 16, 24
FIELDS = 3 * CASES
EARLY = 5
CORNER_PP, CORNER_PT, CORNER_TT = 8, 12, 16


def rows_dot(a, b):
    return lax.dot_general(a, b, (((1,), (1,)), ((), ())), precision=HI, preferred_element_type=F32)


def plain_dot(a, b):
    return lax.dot_general(a, b, (((1,), (0,)), ((), ())), precision=HI, preferred_element_type=F32)


def halves(x):
    high = x.astype(BF16)
    low = (x - high.astype(F32)).astype(BF16)
    return jnp.concatenate([high, low], axis=0)


def split(x):
    high = x.astype(BF16)
    return high, (x - high.astype(F32)).astype(BF16)


def split_dot(a, pair, dim):
    stack = halves(a)
    dims = (((1,), (dim,)), ((), ()))
    main = lax.dot_general(stack, pair[0], dims, preferred_element_type=F32)
    rest = lax.dot_general(stack, pair[1], dims, preferred_element_type=F32)
    return main[:8] + main[8:] + rest[:8]


def lane_sum(x):
    return jnp.sum(x, axis=1, keepdims=True)


def pattern(idx):
    return idx & (LANES - 1), (idx & 128) != 0, (idx & 256) != 0, (idx & 512) != 0


def pick(blocks, where):
    lane, bit0, bit1, bit2 = where
    got = [jnp.take_along_axis(b, lane, axis=1, mode="promise_in_bounds") for b in blocks]
    got = [jnp.where(bit0, got[2 * i + 1], got[2 * i]) for i in range(4)]
    got = [jnp.where(bit1, got[2 * i + 1], got[2 * i]) for i in range(2)]
    return jnp.where(bit2, got[1], got[0])


def blocks_of(row8):
    return [row8[:, LANES * h : LANES * (h + 1)] for h in range(8)]


def is_odd(axis):
    return lax.axis_index(axis) & 1 == 1


def sides_there(axis):
    at, size = lax.axis_index(axis), lax.axis_size(axis)
    return jnp.where(at > 0, 1.0, 0.0), jnp.where(at < size - 1, 1.0, 0.0)


def op_dot(vec, op_ref):
    out = lax.dot_general(halves(vec), op_ref[0], (((1,), (1,)), ((), ())), preferred_element_type=F32)
    return out[:CASES], out[CASES:]


def at_lanes(columns, first=0):
    lane = lax.broadcasted_iota(jnp.int32, (CASES, LANES), 1)
    block = jnp.zeros((CASES, LANES), F32)
    for j, column in enumerate(columns):
        block = jnp.where(lane == first + j, column, block)
    return block


def fetch(sems, pairs):
    copies = [pltpu.make_async_copy(a, b, sems.at[i]) for i, (a, b) in enumerate(pairs)]
    for copy in copies:
        copy.start()
    return copies


def first_kernel(loads_hbm, pre_hbm, corner_hbm, send_ref, loads_ref, pre_ref, corner_ref, sems):
    piece = corner_ref.shape[2] // 4
    parts = [pl.ds(piece * i, piece) for i in range(4)]
    copies = fetch(sems, [(loads_hbm, loads_ref), (pre_hbm, pre_ref)]
                   + [(corner_hbm.at[:, :, k], corner_ref.at[:, :, k]) for k in parts])
    copies[0].wait()
    copies[1].wait()
    p = pre_ref[...] * loads_ref[:, 0, :]
    part = None
    for i, k in enumerate(parts):
        copies[2 + i].wait()
        term = split_dot(p[:, piece * i : piece * (i + 1)], split(corner_ref[0, :, k]), 1)
        part = term if part is None else part + term
    for d in range(send_ref.shape[0]):
        send_ref[d] = part


def edge_tiles(first, second):
    ex, ey = first.shape
    lane = lax.broadcasted_iota(jnp.int32, (1, LANES), 1)
    turned = jnp.transpose(jnp.concatenate([first, second], axis=0))
    swapped = pltpu.roll(turned, LANES - ex, 1)
    out = []
    for array, low, high in ((first, turned, swapped), (second, swapped, turned)):
        cols = [jnp.where(lane < ex, low[j : j + 1], high[j + 1 : j + 2]) for j in (0, ey - 2)]
        out.append(jnp.concatenate([array[0:2], array[ex - 2 :]] + cols + [array[0:2]], axis=0))
    return out


def corner_lanes(low, high):
    lane = lax.broadcasted_iota(jnp.int32, low.shape, 1)
    out = jnp.where(lane == 0, low, jnp.where(lane == 1, pltpu.roll(low, 2, 1), 0))
    return jnp.where(lane == 2, pltpu.roll(high, 2, 1), jnp.where(lane == 3, pltpu.roll(high, 4, 1), out))


def corner_values(vec, where):
    return [pick(blocks_of(vec), pattern(jnp.broadcast_to(where[a : a + 1], (8, LANES)))) for a in range(8)]


def stiff_row(stiff_ref, a, u):
    v = stiff_ref[a, 0] * u[0]
    for b in range(1, 8):
        v = v + stiff_ref[a, b] * u[b]
    return v


def side_indices(iface_ref):
    left = jnp.broadcast_to(iface_ref[0, :, :R], (8, R))
    right = jnp.broadcast_to(iface_ref[0, :, R : 2 * R], (8, R))
    x_odd = jnp.broadcast_to(is_odd("gx"), (8, R))
    return jnp.where(x_odd, left, right), jnp.where(x_odd, right, left)


def side_kernel(loads_hbm, op_hbm, iface_hbm, pre_hbm, corner_hbm,
                keep_ref, even_ref, odd_ref, index_ref, inverse_ref, chigh_ref, clow_ref,
                loads_ref, op_ref, iface_ref, pre_ref, corner_ref, sems):
    copies = fetch(sems, ((loads_hbm, loads_ref), (pre_hbm, pre_ref), (iface_hbm, iface_ref),
                          (corner_hbm, corner_ref), (op_hbm, op_ref)))
    for copy in copies[:4]:
        copy.wait()
    loads = loads_ref[:, 0, :]
    p = pre_ref[...] * loads
    keep_ref[KEEP_P : KEEP_P + 8] = p
    pre = jnp.broadcast_to(pre_ref[...], (8, pre_ref.shape[1]))
    chosen = []
    for idx, out in zip(side_indices(iface_ref), (even_ref, odd_ref)):
        where = pattern(idx)
        scale = pick(blocks_of(pre), where)
        chosen.append((where, scale, out))
        out[SIDE_P : SIDE_P + 8] = pick(blocks_of(p), where)
        out[SIDE_M : SIDE_M + 8] = scale
        for j in range(corner_ref.shape[1] // 8):
            rows = corner_ref[0, 8 * j : 8 * j + 8]
            out[SIDE_C + 8 * j : SIDE_C + 8 * j + 8] = scale * pick(blocks_of(rows), where)
    for side, idx in enumerate(side_indices(iface_ref)):
        index_ref[side] = idx
        column = jnp.transpose(jnp.broadcast_to(idx[0:1], (R, R)))
        number = lax.broadcasted_iota(jnp.int32, (R, LANES), 0) + 1
        for h in range(8):
            at = lax.broadcasted_iota(jnp.int32, (R, LANES), 1) + LANES * h
            found = jnp.sum(jnp.where(column == at, number, 0), axis=0, keepdims=True)
            inverse_ref[side, :, LANES * h : LANES * (h + 1)] = jnp.broadcast_to(found, (8, LANES))
    chigh_ref[...], clow_ref[...] = split(corner_ref[0])
    copies[4].wait()
    y, rest = op_dot(p, op_ref)
    keep_ref[KEEP_Y : KEEP_Y + 8] = y
    keep_ref[KEEP_REST : KEEP_REST + 8] = rest
    keep_ref[KEEP_S : KEEP_S + 8, :LANES] = at_lanes((lane_sum(loads * p), lane_sum(p * rest)))
    for where, scale, out in chosen:
        out[SIDE_Y : SIDE_Y + 8] = scale * pick(blocks_of(y), where)


def early_kernel(keep_ref, dofs_ref, stiff_hbm, density_hbm, passive_hbm,
                 pack_ref, weight_ref, spot_ref, spot_kp_ref,
                 kp_ref, pp_ref, table_ref, u_ref, other_ref, all_dofs_ref, all_weight_ref,
                 stiff_ref, density_ref, passive_ref, sems):
    copies = fetch(sems, ((stiff_hbm, stiff_ref), (density_hbm, density_ref), (passive_hbm, passive_ref)))
    p = keep_ref[KEEP_P : KEEP_P + 8]
    make_tables(table_ref, p)
    for a in range(0, 8, 2):
        first, second = edge_tiles(dofs_ref[a].astype(F32), dofs_ref[a + 1].astype(F32))
        pack_ref[a] = first.astype(jnp.int32)
        pack_ref[a + 1] = second.astype(jnp.int32)
    for copy in copies:
        copy.wait()
    rho = density_ref[...]
    weight = jnp.where(passive_ref[...] == 1, 0.0, -penalty * rho * rho)
    ex = weight.shape[0]
    for i in range(ex // 8):
        weight_ref[i] = weight[8 * i : 8 * i + 8]
    weight_ref[ex // 8] = edge_tiles(weight, weight)[0]
    spot = corner_lanes(dofs_ref[:, 0, :], dofs_ref[:, ex - 1, :])
    spot_ref[...] = spot
    spot_weight = jnp.broadcast_to(corner_lanes(weight[0:1], weight[ex - 1 :]), (8, LANES))
    u = corner_values(p, spot)
    pp = None
    for a in range(8):
        v = stiff_row(stiff_ref, a, u)
        spot_kp_ref[a] = spot_weight * v
        pp = u[a] * v if pp is None else pp + u[a] * v
    lane = lax.broadcasted_iota(jnp.int32, (CASES, LANES), 1)
    spot_kp_ref[8] = spot_weight
    spot_kp_ref[9] = pltpu.roll(jnp.where(lane < 4, spot_weight * pp, 0.0), CORNER_PP, 1)

    for i in range(EARLY):
        for a in range(8):
            all_dofs_ref[i, a] = dofs_ref[a, 8 * i : 8 * i + 8]
        all_weight_ref[i] = weight[8 * i : 8 * i + 8]
    for a in range(8):
        all_dofs_ref[EARLY, a] = pack_ref[a]
    all_weight_ref[EARLY] = weight_ref[ex // 8]

    def gather(i, ref):
        gather_tile(lambda a: all_dofs_ref[i, a], table_ref, ref, 0)

    def fields(i, ref):
        scale = all_weight_ref[i]
        for c in range(CASES):
            u = [ref[0, a, c] for a in range(8)]
            pp = None
            for a in range(8):
                v = stiff_row(stiff_ref, a, u)
                kp_ref[i, a, c] = v
                pp = u[a] * v if pp is None else pp + u[a] * v
            pp_ref[i, c] = scale * pp

    staggered(EARLY + 1, gather, fields, (u_ref, other_ref))


def spread(values, inverse):
    out = []
    for h in range(8):
        at = inverse[:, LANES * h : LANES * (h + 1)]
        got = jnp.take_along_axis(values, jnp.maximum(at - 1, 0), axis=1, mode="promise_in_bounds")
        out.append(jnp.where(at > 0, got, 0.0))
    return jnp.concatenate(out, axis=1)


def second_kernel(got_ref, keep_ref, mine_e_ref, mine_o_ref, theirs_e_ref, theirs_o_ref, index_ref, inverse_ref,
                  spot_ref, spot_kp_ref, coarse_ref, chigh_ref, clow_ref, pre_hbm, op_hbm, stiff_hbm,
                  send_ref, t_ref, pre_ref, op_ref, stiff_ref, sems):
    copies = fetch(sems, ((pre_hbm, pre_ref), (stiff_hbm, stiff_ref), (op_hbm, op_ref)))
    total = got_ref[0]
    for d in range(1, got_ref.shape[0]):
        total = total + got_ref[d]
    corner = chigh_ref[...], clow_ref[...]
    p = keep_ref[KEEP_P : KEEP_P + 8]
    base = keep_ref[KEEP_Y : KEEP_Y + 8]
    pairs = ((mine_e_ref, theirs_e_ref), (mine_o_ref, theirs_o_ref))
    below, above = sides_there("gx")
    x_odd = is_odd("gx")
    couplings = [-coupling * jnp.where(x_odd, a, b) for a, b in ((below, above), (above, below))]
    for side, (_, theirs) in enumerate(pairs):
        base = base + spread(couplings[side] * theirs[SIDE_P : SIDE_P + 8], inverse_ref[side])
    w = split_dot(total, split(coarse_ref[...]), 1)
    q = base + split_dot(w, corner, 0)
    copies[0].wait()
    t = pre_ref[...] * q
    t_ref[...] = t
    g = split_dot(t, corner, 1)
    tlt = None
    for side, (mine, theirs) in enumerate(pairs):
        t_mine = pick(blocks_of(t), pattern(index_ref[side]))
        t_theirs = theirs[SIDE_Y : SIDE_Y + 8] - coupling * theirs[SIDE_M : SIDE_M + 8] * mine[SIDE_P : SIDE_P + 8]
        t_theirs = t_theirs + split_dot(w, split(theirs[SIDE_C:]), 0)
        term = couplings[side] * lane_sum(t_mine * t_theirs)
        tlt = term if tlt is None else tlt + term
    copies[1].wait()
    u = corner_values(t, spot_ref[...])
    pt = tt = None
    for a in range(8):
        one, two = u[a] * spot_kp_ref[a], u[a] * stiff_row(stiff_ref, a, u)
        pt, tt = (one, two) if pt is None else (pt + one, tt + two)
    lane = lax.broadcasted_iota(jnp.int32, (CASES, LANES), 1)
    pt, tt = jnp.where(lane < 4, pt, 0.0), jnp.where(lane < 4, spot_kp_ref[8] * tt, 0.0)
    rest = keep_ref[KEEP_REST : KEEP_REST + 8]
    block = keep_ref[KEEP_S : KEEP_S + 8, :LANES]
    block = block + spot_kp_ref[9] + pltpu.roll(pt, CORNER_PT, 1) + pltpu.roll(tt, CORNER_TT, 1)
    block = block + at_lanes((lane_sum(p * q), lane_sum(q * t), tlt, lane_sum(t * rest)), PQ)
    for d in range(send_ref.shape[0]):
        send_ref[d, :CASES] = g
    copies[2].wait()
    high, low = op_dot(t, op_ref)
    block = block + at_lanes((lane_sum(t * (high + low)),), TLT)
    for d in range(send_ref.shape[0]):
        send_ref[d, CASES:] = block


def make_tables(table_ref, *vectors):
    for i, vec in enumerate(vectors):
        for c in range(CASES):
            for h in range(8):
                row = vec[c : c + 1, LANES * h : LANES * (h + 1)]
                table_ref[i, c, h] = jnp.broadcast_to(row, (8, LANES))


def gather_tile(dofs, table_ref, u_ref, *which):
    for a in range(8):
        where = pattern(dofs(a))
        for c in range(CASES):
            for i in which:
                u_ref[i, a, c] = pick([table_ref[i, c, h] for h in range(8)], where)


def staggered(count, gather, fields, refs, ready=()):
    gather(0, refs[0])
    for copy in ready:
        copy.wait()
    pairs = (count - 1) // 2

    @pl.loop(0, pairs)
    def _(k):
        i = 2 * k
        gather(i + 1, refs[1])
        fields(i, refs[0])
        gather(i + 2, refs[0])
        fields(i + 1, refs[1])

    if count % 2 == 0:
        gather(count - 1, refs[1])
        fields(count - 2, refs[0])
        fields(count - 1, refs[1])
    else:
        fields(count - 1, refs[0])


def t_fields(t, kp, stiff_ref):
    pt = tt = None
    for a in range(8):
        w = stiff_ref[a, a] * t[a]
        for b in range(a + 1, 8):
            w = w + (stiff_ref[a, b] + stiff_ref[b, a]) * t[b]
        one, two = t[a] * kp[a], t[a] * w
        pt, tt = (one, two) if pt is None else (pt + one, tt + two)
    return pt, tt


def edge_kernel(t_ref, pack_ref, weight_ref, kp_ref, pp_ref, stiff_hbm,
                row_e_ref, row_o_ref, col_e_ref, col_o_ref, table_ref, u_ref, field_ref, stiff_ref, sems):
    copies = fetch(sems, ((stiff_hbm, stiff_ref),))
    make_tables(table_ref, t_ref[...])
    gather_tile(lambda a: pack_ref[a], table_ref, u_ref, 0)
    copies[0].wait()
    scale = weight_ref[weight_ref.shape[0] - 1]
    for c in range(CASES):
        pt, tt = t_fields([u_ref[0, a, c] for a in range(8)], [kp_ref[EARLY, a, c] for a in range(8)], stiff_ref)
        field_ref[c] = pp_ref[EARLY, c]
        field_ref[CASES + c] = scale * pt
        field_ref[2 * CASES + c] = scale * tt
    x_odd = jnp.broadcast_to(is_odd("gx"), (FIELDS, LANES))
    y_odd = jnp.broadcast_to(is_odd("gy"), (FIELDS, LANES))
    for i in range(2):
        low, high = field_ref[:, i, :], field_ref[:, 3 - i, :]
        row_e_ref[FIELDS * i : FIELDS * (i + 1)] = jnp.where(x_odd, low, high)
        row_o_ref[FIELDS * i : FIELDS * (i + 1)] = jnp.where(x_odd, high, low)
    low, high = field_ref[:, 4, :], field_ref[:, 5, :]
    col_e_ref[...] = jnp.where(y_odd, low, high)
    col_o_ref[...] = jnp.where(y_odd, high, low)


def field_kernel(keep_ref, t_ref, dofs_ref, weight_ref, kp_ref, stiff_hbm, pp_ref, pt_ref, tt_ref,
                 table_ref, u_ref, other_ref, stiff_ref, sems):
    copies = fetch(sems, ((stiff_hbm, stiff_ref),))
    make_tables(table_ref, t_ref[...], keep_ref[KEEP_P : KEEP_P + 8])

    def rows_of(tile):
        return pl.ds(pl.multiple_of(8 * tile, 8), 8)

    def t_at(ref, c):
        return [ref[0, a, c] for a in range(8)]

    def gather(tile, ref):
        gather_tile(lambda a: dofs_ref[a, rows_of(tile), :], table_ref, ref, 0)

    def fields(tile, ref):
        scale = weight_ref[tile]
        for c in range(CASES):
            pt, tt = t_fields(t_at(ref, c), [kp_ref[tile, a, c] for a in range(8)], stiff_ref)
            pt_ref[tile, c], tt_ref[tile, c] = scale * pt, scale * tt

    staggered(EARLY, gather, fields, (u_ref, other_ref), copies)

    def gather_both(i, ref):
        gather_tile(lambda a: dofs_ref[a, rows_of(i + EARLY), :], table_ref, ref, 0, 1)

    def fields_both(i, ref):
        scale = weight_ref[i + EARLY]
        for c in range(CASES):
            p = [ref[1, a, c] for a in range(8)]
            kp = [stiff_row(stiff_ref, a, p) for a in range(8)]
            pp = p[0] * kp[0]
            for a in range(1, 8):
                pp = pp + p[a] * kp[a]
            pt, tt = t_fields(t_at(ref, c), kp, stiff_ref)
            pp_ref[i, c], pt_ref[i + EARLY, c], tt_ref[i + EARLY, c] = scale * pp, scale * pt, scale * tt

    staggered(pt_ref.shape[0] - EARLY, gather_both, fields_both, (u_ref, other_ref))


def last_kernel(got_ref, coarse_ref, keep_ref, t_ref, early_ref, late_ref, pt_ref, tt_ref,
                mine_ye_ref, mine_yo_ref, xe_ref, xo_ref, ye_ref, yo_ref,
                adj_ref, out_ref):
    total = got_ref[0]
    for d in range(1, got_ref.shape[0]):
        total = total + got_ref[d]
    g, s = total[:CASES], total[CASES:]
    rz, pq, qmq, tlt, pe, te = (s[:, j : j + 1] for j in (RZ, PQ, QMQ, TLT, PE, TE))
    tat = tlt + lane_sum(g * rows_dot(g, coarse_ref[...]))
    alpha = rz / pq
    rz_next = rz - 2.0 * alpha * pq + alpha * alpha * qmq
    grow = 1.0 + rz_next / rz
    pap = grow * grow * (pq + pe) - 2.0 * alpha * grow * (qmq + te) + alpha * alpha * tat
    alpha_next = rz_next / pap
    of_p, of_t = alpha + alpha_next * grow, -(alpha * alpha_next)
    adj_ref[:, 0, :] = of_p * keep_ref[KEEP_P : KEEP_P + 8] + of_t * t_ref[...]

    factors = [of_p * of_p, 2.0 * of_p * of_t, of_t * of_t]
    wide = [jnp.broadcast_to(f, (CASES, LANES)) for f in factors]
    splat = [[jnp.broadcast_to(f[c : c + 1], (8, LANES)) for c in range(CASES)] for f in wide]
    tiles = []
    for i in range(pt_ref.shape[0]):
        tile = None
        pp = early_ref.at[i] if i < EARLY else late_ref.at[i - EARLY]
        for ref, factor in zip((pp, pt_ref.at[i], tt_ref.at[i]), splat):
            for c in range(CASES):
                term = factor[c] * ref[c]
                tile = term if tile is None else tile + term
        tiles.append(tile)
    grad = jnp.concatenate(tiles, axis=0)
    column = jnp.concatenate(wide, axis=0)

    def combine(fields):
        return jnp.sum(column * fields, axis=0, keepdims=True)

    ex, ey = grad.shape
    x_odd, y_odd = is_odd("gx"), is_odd("gy")
    has = sides_there("gx") + sides_there("gy")

    def choose(flag, a, b):
        return jnp.where(jnp.broadcast_to(flag, a.shape), a, b)

    def two(a, b, flag):
        return choose(flag, a, b), choose(flag, b, a)

    def both(values, there):
        return [v * flag for v, flag in zip(values, there)]

    rows = [[combine(ref[FIELDS * i : FIELDS * (i + 1)]) for i in range(2)] for ref in (xe_ref, xo_ref)]
    g_below1, g_above1 = both(two(rows[0][0], rows[1][0], x_odd), has[:2])
    g_below2, g_above2 = both(two(rows[0][1], rows[1][1], x_odd), has[:2])
    before, after = both(two(combine(ye_ref[...]), combine(yo_ref[...]), y_odd), has[2:])
    col_low, col_high = two(combine(mine_ye_ref[...]), combine(mine_yo_ref[...]), y_odd)
    wide_lane = lax.broadcasted_iota(jnp.int32, (CASES, LANES), 1)
    of_lane = jnp.where(wide_lane < CORNER_PT, wide[0], jnp.where(wide_lane < CORNER_TT, wide[1], wide[2]))
    x, y = lax.axis_index("gx"), lax.axis_index("gy")
    nx, ny = lax.axis_size("gx"), lax.axis_size("gy")

    def corner_of(dx, dy, there, k):
        whose = jnp.clip(x + dx, 0, nx - 1) * ny + jnp.clip(y + dy, 0, ny - 1)
        row = jnp.sum(of_lane * got_ref[whose, CASES:, :], axis=0, keepdims=True)
        parts = [row[:, at + k : at + k + 1] for at in (CORNER_PP, CORNER_PT, CORNER_TT)]
        return there * (parts[0] + parts[1] + parts[2]) / diag

    corner = [corner_of(-1, -1, has[0] * has[2], 3), corner_of(-1, 1, has[0] * has[3], 2),
              corner_of(1, -1, has[1] * has[2], 1), corner_of(1, 1, has[1] * has[3], 0)]
    lane = lax.broadcasted_iota(jnp.int32, (1, LANES), 1)

    def shifted(row, low, high, length):
        left = jnp.where(lane == 0, low, pltpu.roll(row, 1, 1))
        right = jnp.where(lane == length - 1, high, pltpu.roll(row, LANES - 1, 1))
        return left + right

    def upper(row):
        return pltpu.roll(row, LANES - ex, 1)

    g_before1, g_before2 = upper(before), before
    g_after1, g_after2 = after, upper(after)
    col_first, col_last = col_low, upper(col_high)
    s_below1, s_above1 = g_below1 / diag, g_above1 / diag
    s_before1, s_after1 = g_before1 / diag, g_after1 / diag

    def ring(g1, g2, inner, beside, there):
        return there * (g1 + radius_sq * (g2 / diag + inner / diag + beside)) / diag

    n_below = ring(g_below1, g_below2, grad[0:1], shifted(s_below1, corner[0], corner[1], ey), has[0])
    n_above = ring(g_above1, g_above2, grad[ex - 1 :], shifted(s_above1, corner[2], corner[3], ey), has[1])
    n_before = ring(g_before1, g_before2, col_first, shifted(s_before1, corner[0], corner[2], ex), has[2])
    n_after = ring(g_after1, g_after2, col_last, shifted(s_after1, corner[1], corner[3], ex), has[3])
    stack = jnp.concatenate([s_before1, s_after1, n_before, n_after, jnp.zeros((4, LANES), F32)], axis=0)
    columns = jnp.transpose(stack)[:ex]
    row_no = lax.broadcasted_iota(jnp.int32, (ex, ey), 0)
    col_no = lax.broadcasted_iota(jnp.int32, (ex, ey), 1)

    def sweep(s, below_row, above_row, before_col, after_col):
        down = jnp.where(row_no == 0, below_row, pltpu.roll(s, 1, 0))
        up = jnp.where(row_no == ex - 1, above_row, pltpu.roll(s, ex - 1, 0))
        left = jnp.where(col_no == 0, before_col, pltpu.roll(s, 1, 1))
        right = jnp.where(col_no == ey - 1, after_col, pltpu.roll(s, ey - 1, 1))
        return (grad + radius_sq * (up + down + right + left)) / diag

    s = sweep(grad / diag, s_below1, s_above1, columns[:, 0:1], columns[:, 1:2])
    out_ref[...] = sweep(s, n_below, n_above, columns[:, 2:3], columns[:, 3:4])


def swaps(nx, ny, along_y):
    def number(along, across):
        return across * ny + along if along_y else along * ny + across

    size, other = (ny, nx) if along_y else (nx, ny)
    out = []
    for first in (0, 1):
        inner = [(i, i + 1) for i in range(first, size - 1, 2)]
        pairs = [(number(i, k), number(j, k)) for i, j in inner for k in range(other)]
        alone = [i for i in range(size) if not any(i in pair for pair in inner)]
        if inner and other % 2 == 0:
            pairs += [(number(i, k), number(i, k + 1)) for i in alone for k in range(0, other, 2)]
        out.append(pairs + [(b, a) for a, b in pairs])
    return out


def swap_over(array, pairs):
    return lax.ppermute(array, ("gx", "gy"), pairs) if pairs else jnp.zeros_like(array)


def f32(*shape):
    return jax.ShapeDtypeStruct(shape, F32)


def s32(*shape):
    return jax.ShapeDtypeStruct(shape, jnp.int32)


def bf16(*shape):
    return jax.ShapeDtypeStruct(shape, BF16)


def call(kernel, name, out_shape, in_specs, scratch, moved):
    single = not isinstance(out_shape, tuple)
    return pl.pallas_call(
        kernel, out_shape=out_shape, in_specs=in_specs,
        out_specs=VMEM if single else (VMEM,) * len(out_shape), scratch_shapes=scratch, name=name,
        compiler_params=pltpu.CompilerParams(vmem_limit_bytes=LIMIT),
        cost_estimate=pl.CostEstimate(flops=1_000_000, bytes_accessed=moved, transcendentals=0),
    )


LIMIT = 6 * 1024 * 1024


def on_device(loads, dual_op, iface, precond, corner_map, coarse_inv, elem_stiff, elem_dofs, density, passive):
    nx, ny = lax.axis_size("gx"), lax.axis_size("gy")
    everyone = nx * ny
    unknowns = dual_op.shape[-1]
    modes = corner_map.shape[1]
    ex, ey = density.shape
    tiles = ex // 8
    x_even, x_odd = swaps(nx, ny, False)
    y_even, y_odd = swaps(nx, ny, True)

    def held(array):
        return pltpu.VMEM(array.shape, array.dtype)

    def in_hbm(array):
        return pltpu.with_memory_space_constraint(array, pltpu.HBM)

    def copies(n):
        return pltpu.SemaphoreType.DMA((n,))

    stiff = pltpu.SMEM(elem_stiff.shape, F32)
    one_table = pltpu.VMEM((1, CASES, 8, 8, LANES), F32)
    one_gathered = pltpu.VMEM((1, 8, CASES, 8, LANES), F32)
    table = pltpu.VMEM((2, CASES, 8, 8, LANES), F32)
    gathered = pltpu.VMEM((2, 8, CASES, 8, LANES), F32)

    send = call(first_kernel, "first", f32(everyone, CASES, modes), [HBM] * 3,
                [held(loads), held(precond), held(corner_map), copies(6)], 4_000_000,
                )(in_hbm(loads), in_hbm(precond), in_hbm(corner_map))
    got = lax.all_to_all(send, ("gx", "gy"), 0, 0)

    side = f32(SIDE_C + modes, R)
    params = (loads, dual_op, iface, precond, corner_map)
    keep, mine_e, mine_o, index, inverse, chigh, clow = call(
        side_kernel, "sides",
        (f32(KEEP_S + 8, unknowns), side, side, s32(2, 8, R), s32(2, 8, unknowns), bf16(modes, unknowns),
         bf16(modes, unknowns)),
        [HBM] * 5, [held(a) for a in params] + [copies(5)], 8_000_000,
    )(*(in_hbm(a) for a in params))
    theirs_o = swap_over(mine_o, x_odd)
    theirs_e = swap_over(mine_e, x_even)

    field = f32(EARLY + 1, CASES, 8, LANES)
    params = (elem_stiff, density, passive)
    pack, weight, spot, spot_kp, kp, pp = call(
        early_kernel, "early",
        (s32(8, 8, LANES), f32(tiles + 1, 8, LANES), s32(8, LANES), f32(10, 8, LANES), f32(EARLY + 1, 8, CASES, 8, LANES), field),
        [VMEM] * 2 + [HBM] * 3,
        [one_table, one_gathered, one_gathered, pltpu.VMEM((EARLY + 1, 8, 8, LANES), jnp.int32),
         pltpu.VMEM((EARLY + 1, 8, LANES), F32)] + [stiff if a is elem_stiff else held(a) for a in params] + [copies(3)], 18_000_000,
    )(keep, elem_dofs, *(in_hbm(a) for a in params))
    got, spot = lax.optimization_barrier((got, spot))

    send, t = call(
        second_kernel, "second", (f32(everyone, 2 * CASES, modes), f32(CASES, unknowns)),
        [VMEM] * 13 + [HBM] * 3, [held(precond), held(dual_op), stiff, copies(3)], 9_000_000,
    )(got, keep, mine_e, mine_o, theirs_e, theirs_o, index, inverse, spot, spot_kp, coarse_inv, chigh, clow,
      in_hbm(precond), in_hbm(dual_op), in_hbm(elem_stiff))
    got = lax.all_to_all(send, ("gx", "gy"), 0, 0)

    row = f32(2 * FIELDS, LANES)
    col = f32(FIELDS, LANES)
    row_e, row_o, col_e, col_o = call(
        edge_kernel, "edges", (row, row, col, col), [VMEM] * 5 + [HBM],
        [one_table, one_gathered, pltpu.VMEM((FIELDS, 8, LANES), F32), stiff, copies(1)], 4_000_000,
    )(t, pack, weight, kp, pp, in_hbm(elem_stiff))
    ye, yo = swap_over(col_e, y_even), swap_over(col_o, y_odd)
    xo = swap_over(row_o, x_odd)
    xe = swap_over(row_e, x_even)

    late, pt, tt = call(
        field_kernel, "fields",
        (f32(tiles - EARLY, CASES, 8, LANES), f32(tiles, CASES, 8, LANES), f32(tiles, CASES, 8, LANES)),
        [VMEM] * 5 + [HBM], [table, gathered, gathered, stiff, copies(1)], 36_000_000,
    )(keep, t, elem_dofs, weight, kp, in_hbm(elem_stiff))

    adjoint, sens = call(
        last_kernel, "last", (f32(CASES, 1, unknowns), f32(ex, ey)), [VMEM] * 14, [], 4_000_000,
    )(got, coarse_inv, keep, t, pp, late, pt, tt, col_e, col_o, xe, xo, ye, yo)
    return adjoint, sens


def solution(mesh):
    placed = (
        P(None, "gy", "gx"),
        P("gy", "gx", None),
        P("gy", "gx", None),
        P("gy", "gx"),
        P("gy", None, "gx"),
        P(),
        P(),
        P(None, "gx", "gy"),
        P("gx", "gy"),
        P("gx", "gy"),
    )
    return jax.shard_map(
        on_device,
        mesh=mesh,
        in_specs=placed,
        out_specs=(P(None, "gy", "gx"), P("gx", "gy")),
        check_vma=False,
    )
```

```python
import jax
import jax.numpy as jnp
from jax import lax
from jax.experimental import pallas as pl
from jax.experimental.pallas import tpu as pltpu
from jax.sharding import PartitionSpec as P

R = 128
LANES = 128
CASES = 8

coupling = 0.3
radius_sq = 2.0
penalty = 3.0
diag = 1.0 + 4.0 * radius_sq

HI = lax.Precision.HIGHEST
F32 = jnp.float32
BF16 = jnp.bfloat16
VMEM = pl.BlockSpec(memory_space=pltpu.VMEM)
HBM = pl.BlockSpec(memory_space=pltpu.HBM)

SIDE_P, SIDE_Y, SIDE_M, SIDE_C = 0, 8, 16, 24
RZ, PE, PQ, QMQ, TLT, TE = range(6)
KEEP_P, KEEP_Y, KEEP_REST, KEEP_S = 0, 8, 16, 24
FIELDS = 3 * CASES
EARLY = 5
CORNER_PP, CORNER_PT, CORNER_TT = 8, 12, 16


def rows_dot(a, b):
    return lax.dot_general(a, b, (((1,), (1,)), ((), ())), precision=HI, preferred_element_type=F32)


def plain_dot(a, b):
    return lax.dot_general(a, b, (((1,), (0,)), ((), ())), precision=HI, preferred_element_type=F32)


def halves(x):
    high = x.astype(BF16)
    low = (x - high.astype(F32)).astype(BF16)
    return jnp.concatenate([high, low], axis=0)


def split(x):
    high = x.astype(BF16)
    return high, (x - high.astype(F32)).astype(BF16)


def split_dot(a, pair, dim):
    stack = halves(a)
    dims = (((1,), (dim,)), ((), ()))
    main = lax.dot_general(stack, pair[0], dims, preferred_element_type=F32)
    rest = lax.dot_general(stack, pair[1], dims, preferred_element_type=F32)
    return main[:8] + main[8:] + rest[:8]


def lane_sum(x):
    return jnp.sum(x, axis=1, keepdims=True)


def pattern(idx):
    return idx & (LANES - 1), (idx & 128) != 0, (idx & 256) != 0, (idx & 512) != 0


def pick(blocks, where):
    lane, bit0, bit1, bit2 = where
    got = [jnp.take_along_axis(b, lane, axis=1, mode="promise_in_bounds") for b in blocks]
    got = [jnp.where(bit0, got[2 * i + 1], got[2 * i]) for i in range(4)]
    got = [jnp.where(bit1, got[2 * i + 1], got[2 * i]) for i in range(2)]
    return jnp.where(bit2, got[1], got[0])


def blocks_of(row8):
    return [row8[:, LANES * h : LANES * (h + 1)] for h in range(8)]


def is_odd(axis):
    return lax.axis_index(axis) & 1 == 1


def sides_there(axis):
    at, size = lax.axis_index(axis), lax.axis_size(axis)
    return jnp.where(at > 0, 1.0, 0.0), jnp.where(at < size - 1, 1.0, 0.0)


def op_dot(vec, op_ref):
    out = lax.dot_general(halves(vec), op_ref[0], (((1,), (1,)), ((), ())), preferred_element_type=F32)
    return out[:CASES], out[CASES:]


def at_lanes(columns, first=0):
    lane = lax.broadcasted_iota(jnp.int32, (CASES, LANES), 1)
    block = jnp.zeros((CASES, LANES), F32)
    for j, column in enumerate(columns):
        block = jnp.where(lane == first + j, column, block)
    return block


def fetch(sems, pairs):
    copies = [pltpu.make_async_copy(a, b, sems.at[i]) for i, (a, b) in enumerate(pairs)]
    for copy in copies:
        copy.start()
    return copies


def edge_tiles(first, second):
    ex, ey = first.shape
    lane = lax.broadcasted_iota(jnp.int32, (1, LANES), 1)
    turned = jnp.transpose(jnp.concatenate([first, second], axis=0))
    swapped = pltpu.roll(turned, LANES - ex, 1)
    out = []
    for array, low, high in ((first, turned, swapped), (second, swapped, turned)):
        cols = [jnp.where(lane < ex, low[j : j + 1], high[j + 1 : j + 2]) for j in (0, ey - 2)]
        out.append(jnp.concatenate([array[0:2], array[ex - 2 :]] + cols + [array[0:2]], axis=0))
    return out


def corner_lanes(low, high):
    lane = lax.broadcasted_iota(jnp.int32, low.shape, 1)
    out = jnp.where(lane == 0, low, jnp.where(lane == 1, pltpu.roll(low, 2, 1), 0))
    return jnp.where(lane == 2, pltpu.roll(high, 2, 1), jnp.where(lane == 3, pltpu.roll(high, 4, 1), out))


def corner_values(vec, where):
    return [pick(blocks_of(vec), pattern(jnp.broadcast_to(where[a : a + 1], (8, LANES)))) for a in range(8)]


def first_kernel(loads_hbm, pre_hbm, corner_hbm, dofs_hbm, density_hbm, passive_hbm,
                 send_hbm, pack_ref, weight_ref, spot_ref,
                 send_ref, loads_ref, pre_ref, corner_ref, dofs_ref, density_ref, passive_ref, sems):
    piece = corner_ref.shape[2] // 4
    parts = [pl.ds(piece * i, piece) for i in range(4)]
    copies = fetch(sems, [(loads_hbm, loads_ref), (pre_hbm, pre_ref)]
                   + [(corner_hbm.at[:, :, k], corner_ref.at[:, :, k]) for k in parts]
                   + [(dofs_hbm, dofs_ref), (density_hbm, density_ref), (passive_hbm, passive_ref)])
    copies[0].wait()
    copies[1].wait()
    p = pre_ref[...] * loads_ref[:, 0, :]
    part = None
    for i, k in enumerate(parts):
        copies[2 + i].wait()
        term = split_dot(p[:, piece * i : piece * (i + 1)], split(corner_ref[0, :, k]), 1)
        part = term if part is None else part + term
    for d in range(send_ref.shape[0]):
        send_ref[d] = part
    out = pltpu.make_async_copy(send_ref, send_hbm, sems.at[9])
    out.start()
    for copy in copies[6:]:
        copy.wait()
    for a in range(0, 8, 2):
        first, second = edge_tiles(dofs_ref[a].astype(F32), dofs_ref[a + 1].astype(F32))
        pack_ref[a] = first.astype(jnp.int32)
        pack_ref[a + 1] = second.astype(jnp.int32)
    rho = density_ref[...]
    weight = jnp.where(passive_ref[...] == 1, 0.0, -penalty * rho * rho)
    ex = weight.shape[0]
    for i in range(ex // 8):
        weight_ref[i] = weight[8 * i : 8 * i + 8]
    weight_ref[ex // 8] = edge_tiles(weight, weight)[0]
    spot_ref[0] = corner_lanes(dofs_ref[:, 0, :], dofs_ref[:, ex - 1, :]).astype(F32)
    spot_ref[1] = jnp.broadcast_to(corner_lanes(weight[0:1], weight[ex - 1 :]), (8, LANES))
    out.wait()


def stiff_row(stiff_ref, a, u):
    v = stiff_ref[a, 0] * u[0]
    for b in range(1, 8):
        v = v + stiff_ref[a, b] * u[b]
    return v


def side_indices(iface_ref):
    left = jnp.broadcast_to(iface_ref[0, :, :R], (8, R))
    right = jnp.broadcast_to(iface_ref[0, :, R : 2 * R], (8, R))
    x_odd = jnp.broadcast_to(is_odd("gx"), (8, R))
    return jnp.where(x_odd, left, right), jnp.where(x_odd, right, left)


def side_kernel(loads_hbm, op_hbm, iface_hbm, pre_hbm, corner_hbm,
                keep_ref, even_ref, odd_ref, index_ref, inverse_ref, chigh_ref, clow_ref,
                loads_ref, op_ref, iface_ref, pre_ref, corner_ref, sems):
    copies = fetch(sems, ((loads_hbm, loads_ref), (pre_hbm, pre_ref), (iface_hbm, iface_ref),
                          (corner_hbm, corner_ref), (op_hbm, op_ref)))
    for copy in copies[:4]:
        copy.wait()
    loads = loads_ref[:, 0, :]
    p = pre_ref[...] * loads
    keep_ref[KEEP_P : KEEP_P + 8] = p
    pre = jnp.broadcast_to(pre_ref[...], (8, pre_ref.shape[1]))
    chosen = []
    for idx, out in zip(side_indices(iface_ref), (even_ref, odd_ref)):
        where = pattern(idx)
        scale = pick(blocks_of(pre), where)
        chosen.append((where, scale, out))
        out[SIDE_P : SIDE_P + 8] = pick(blocks_of(p), where)
        out[SIDE_M : SIDE_M + 8] = scale
        for j in range(corner_ref.shape[1] // 8):
            rows = corner_ref[0, 8 * j : 8 * j + 8]
            out[SIDE_C + 8 * j : SIDE_C + 8 * j + 8] = scale * pick(blocks_of(rows), where)
    for side, idx in enumerate(side_indices(iface_ref)):
        index_ref[side] = idx
        column = jnp.transpose(jnp.broadcast_to(idx[0:1], (R, R)))
        number = lax.broadcasted_iota(jnp.int32, (R, LANES), 0) + 1
        for h in range(8):
            at = lax.broadcasted_iota(jnp.int32, (R, LANES), 1) + LANES * h
            found = jnp.sum(jnp.where(column == at, number, 0), axis=0, keepdims=True)
            inverse_ref[side, :, LANES * h : LANES * (h + 1)] = jnp.broadcast_to(found, (8, LANES))
    chigh_ref[...], clow_ref[...] = split(corner_ref[0])
    copies[4].wait()
    y, rest = op_dot(p, op_ref)
    keep_ref[KEEP_Y : KEEP_Y + 8] = y
    keep_ref[KEEP_REST : KEEP_REST + 8] = rest
    keep_ref[KEEP_S : KEEP_S + 8, :LANES] = at_lanes((lane_sum(loads * p), lane_sum(p * rest)))
    for where, scale, out in chosen:
        out[SIDE_Y : SIDE_Y + 8] = scale * pick(blocks_of(y), where)


def early_kernel(keep_ref, dofs_ref, pack_ref, weight_ref, spot_ref, stiff_hbm, spot_kp_ref,
                 kp_ref, pp_ref, table_ref, u_ref, other_ref, all_dofs_ref, all_weight_ref,
                 stiff_ref, sems):
    copies = fetch(sems, ((stiff_hbm, stiff_ref),))
    p = keep_ref[KEEP_P : KEEP_P + 8]
    make_tables(table_ref, p)
    for i in range(EARLY):
        for a in range(8):
            all_dofs_ref[i, a] = dofs_ref[a, 8 * i : 8 * i + 8]
        all_weight_ref[i] = weight_ref[i]
    for a in range(8):
        all_dofs_ref[EARLY, a] = pack_ref[a]
    all_weight_ref[EARLY] = weight_ref[weight_ref.shape[0] - 1]

    def gather(i, ref):
        gather_tile(lambda a: all_dofs_ref[i, a], table_ref, ref, 0)

    def fields(i, ref):
        scale = all_weight_ref[i]
        for c in range(CASES):
            u = [ref[0, a, c] for a in range(8)]
            pp = None
            for a in range(8):
                v = stiff_row(stiff_ref, a, u)
                kp_ref[i, a, c] = v
                pp = u[a] * v if pp is None else pp + u[a] * v
            pp_ref[i, c] = scale * pp

    staggered(EARLY + 1, gather, fields, (u_ref, other_ref), copies)
    spot_weight = spot_ref[1]
    u = corner_values(p, spot_ref[0].astype(jnp.int32))
    pp = None
    for a in range(8):
        v = stiff_row(stiff_ref, a, u)
        spot_kp_ref[a] = spot_weight * v
        pp = u[a] * v if pp is None else pp + u[a] * v
    lane = lax.broadcasted_iota(jnp.int32, (CASES, LANES), 1)
    spot_kp_ref[8] = pltpu.roll(jnp.where(lane < 4, spot_weight * pp, 0.0), CORNER_PP, 1)


def spread(values, inverse):
    out = []
    for h in range(8):
        at = inverse[:, LANES * h : LANES * (h + 1)]
        got = jnp.take_along_axis(values, jnp.maximum(at - 1, 0), axis=1, mode="promise_in_bounds")
        out.append(jnp.where(at > 0, got, 0.0))
    return jnp.concatenate(out, axis=1)


def second_kernel(got_ref, keep_ref, mine_e_ref, mine_o_ref, theirs_e_ref, theirs_o_ref, index_ref, inverse_ref,
                  spot_ref, spot_kp_ref, coarse_ref, chigh_ref, clow_ref, pack_ref, weight_ref, kp_ref, pp_ref,
                  pre_hbm, op_hbm, stiff_hbm,
                  send_hbm, t_ref, row_e_ref, row_o_ref, col_e_ref, col_o_ref,
                  send_ref, table_ref, u_ref, field_ref, pre_ref, op_ref, stiff_ref, sems):
    copies = fetch(sems, ((pre_hbm, pre_ref), (stiff_hbm, stiff_ref), (op_hbm, op_ref)))
    total = got_ref[0]
    for d in range(1, got_ref.shape[0]):
        total = total + got_ref[d]
    corner = chigh_ref[...], clow_ref[...]
    p = keep_ref[KEEP_P : KEEP_P + 8]
    base = keep_ref[KEEP_Y : KEEP_Y + 8]
    pairs = ((mine_e_ref, theirs_e_ref), (mine_o_ref, theirs_o_ref))
    below, above = sides_there("gx")
    x_odd = is_odd("gx")
    couplings = [-coupling * jnp.where(x_odd, a, b) for a, b in ((below, above), (above, below))]
    for side, (_, theirs) in enumerate(pairs):
        base = base + spread(couplings[side] * theirs[SIDE_P : SIDE_P + 8], inverse_ref[side])
    w = split_dot(total, split(coarse_ref[...]), 1)
    q = base + split_dot(w, corner, 0)
    copies[0].wait()
    t = pre_ref[...] * q
    t_ref[...] = t
    g = split_dot(t, corner, 1)
    tlt = None
    for side, (mine, theirs) in enumerate(pairs):
        t_mine = pick(blocks_of(t), pattern(index_ref[side]))
        t_theirs = theirs[SIDE_Y : SIDE_Y + 8] - coupling * theirs[SIDE_M : SIDE_M + 8] * mine[SIDE_P : SIDE_P + 8]
        t_theirs = t_theirs + split_dot(w, split(theirs[SIDE_C:]), 0)
        term = couplings[side] * lane_sum(t_mine * t_theirs)
        tlt = term if tlt is None else tlt + term
    copies[1].wait()
    u = corner_values(t, spot_ref[0].astype(jnp.int32))
    pt = tt = None
    for a in range(8):
        one, two = u[a] * spot_kp_ref[a], u[a] * stiff_row(stiff_ref, a, u)
        pt, tt = (one, two) if pt is None else (pt + one, tt + two)
    lane = lax.broadcasted_iota(jnp.int32, (CASES, LANES), 1)
    pt, tt = jnp.where(lane < 4, pt, 0.0), jnp.where(lane < 4, spot_ref[1] * tt, 0.0)
    rest = keep_ref[KEEP_REST : KEEP_REST + 8]
    block = keep_ref[KEEP_S : KEEP_S + 8, :LANES]
    block = block + spot_kp_ref[8] + pltpu.roll(pt, CORNER_PT, 1) + pltpu.roll(tt, CORNER_TT, 1)
    block = block + at_lanes((lane_sum(p * q), lane_sum(q * t), tlt, lane_sum(t * rest)), PQ)
    for d in range(send_ref.shape[0]):
        send_ref[d, :CASES] = g
    copies[2].wait()
    high, low = op_dot(t, op_ref)
    block = block + at_lanes((lane_sum(t * (high + low)),), TLT)
    for d in range(send_ref.shape[0]):
        send_ref[d, CASES:] = block
    out = pltpu.make_async_copy(send_ref, send_hbm, sems.at[3])
    out.start()
    edge_fields(t, pack_ref, weight_ref, kp_ref, pp_ref, row_e_ref, row_o_ref, col_e_ref, col_o_ref,
                table_ref, u_ref, field_ref, stiff_ref)
    out.wait()


def make_tables(table_ref, *vectors):
    for i, vec in enumerate(vectors):
        for c in range(CASES):
            for h in range(8):
                row = vec[c : c + 1, LANES * h : LANES * (h + 1)]
                table_ref[i, c, h] = jnp.broadcast_to(row, (8, LANES))


def gather_tile(dofs, table_ref, u_ref, *which):
    for a in range(8):
        where = pattern(dofs(a))
        for c in range(CASES):
            for i in which:
                u_ref[i, a, c] = pick([table_ref[i, c, h] for h in range(8)], where)


def staggered(count, gather, fields, refs, ready=()):
    gather(0, refs[0])
    for copy in ready:
        copy.wait()
    pairs = (count - 1) // 2

    @pl.loop(0, pairs)
    def _(k):
        i = 2 * k
        gather(i + 1, refs[1])
        fields(i, refs[0])
        gather(i + 2, refs[0])
        fields(i + 1, refs[1])

    if count % 2 == 0:
        gather(count - 1, refs[1])
        fields(count - 2, refs[0])
        fields(count - 1, refs[1])
    else:
        fields(count - 1, refs[0])


def t_fields(t, kp, stiff_ref):
    pt = tt = None
    for a in range(8):
        w = stiff_ref[a, a] * t[a]
        for b in range(a + 1, 8):
            w = w + (stiff_ref[a, b] + stiff_ref[b, a]) * t[b]
        one, two = t[a] * kp[a], t[a] * w
        pt, tt = (one, two) if pt is None else (pt + one, tt + two)
    return pt, tt


def edge_fields(t, pack_ref, weight_ref, kp_ref, pp_ref, row_e_ref, row_o_ref, col_e_ref, col_o_ref,
                table_ref, u_ref, field_ref, stiff_ref):
    make_tables(table_ref, t)
    gather_tile(lambda a: pack_ref[a], table_ref, u_ref, 0)
    scale = weight_ref[weight_ref.shape[0] - 1]
    for c in range(CASES):
        pt, tt = t_fields([u_ref[0, a, c] for a in range(8)], [kp_ref[EARLY, a, c] for a in range(8)], stiff_ref)
        field_ref[c] = pp_ref[EARLY, c]
        field_ref[CASES + c] = scale * pt
        field_ref[2 * CASES + c] = scale * tt
    x_odd = jnp.broadcast_to(is_odd("gx"), (FIELDS, LANES))
    y_odd = jnp.broadcast_to(is_odd("gy"), (FIELDS, LANES))
    for i in range(2):
        low, high = field_ref[:, i, :], field_ref[:, 3 - i, :]
        row_e_ref[FIELDS * i : FIELDS * (i + 1)] = jnp.where(x_odd, low, high)
        row_o_ref[FIELDS * i : FIELDS * (i + 1)] = jnp.where(x_odd, high, low)
    low, high = field_ref[:, 4, :], field_ref[:, 5, :]
    col_e_ref[...] = jnp.where(y_odd, low, high)
    col_o_ref[...] = jnp.where(y_odd, high, low)


def field_kernel(keep_ref, t_ref, dofs_ref, weight_ref, kp_ref, stiff_hbm, pp_ref, pt_ref, tt_ref,
                 table_ref, u_ref, other_ref, stiff_ref, sems):
    copies = fetch(sems, ((stiff_hbm, stiff_ref),))
    make_tables(table_ref, t_ref[...], keep_ref[KEEP_P : KEEP_P + 8])

    def rows_of(tile):
        return pl.ds(pl.multiple_of(8 * tile, 8), 8)

    def t_at(ref, c):
        return [ref[0, a, c] for a in range(8)]

    def gather(tile, ref):
        gather_tile(lambda a: dofs_ref[a, rows_of(tile), :], table_ref, ref, 0)

    def fields(tile, ref):
        scale = weight_ref[tile]
        for c in range(CASES):
            pt, tt = t_fields(t_at(ref, c), [kp_ref[tile, a, c] for a in range(8)], stiff_ref)
            pt_ref[tile, c], tt_ref[tile, c] = scale * pt, scale * tt

    staggered(EARLY, gather, fields, (u_ref, other_ref), copies)

    def gather_both(i, ref):
        gather_tile(lambda a: dofs_ref[a, rows_of(i + EARLY), :], table_ref, ref, 0, 1)

    def fields_both(i, ref):
        scale = weight_ref[i + EARLY]
        for c in range(CASES):
            p = [ref[1, a, c] for a in range(8)]
            kp = [stiff_row(stiff_ref, a, p) for a in range(8)]
            pp = p[0] * kp[0]
            for a in range(1, 8):
                pp = pp + p[a] * kp[a]
            pt, tt = t_fields(t_at(ref, c), kp, stiff_ref)
            pp_ref[i, c], pt_ref[i + EARLY, c], tt_ref[i + EARLY, c] = scale * pp, scale * pt, scale * tt

    staggered(pt_ref.shape[0] - EARLY, gather_both, fields_both, (u_ref, other_ref))


def last_kernel(got_ref, coarse_ref, keep_ref, t_ref, early_ref, late_ref, pt_ref, tt_ref,
                mine_ye_ref, mine_yo_ref, xe_ref, xo_ref, ye_ref, yo_ref,
                adj_ref, out_ref):
    total = got_ref[0]
    for d in range(1, got_ref.shape[0]):
        total = total + got_ref[d]
    g, s = total[:CASES], total[CASES:]
    rz, pq, qmq, tlt, pe, te = (s[:, j : j + 1] for j in (RZ, PQ, QMQ, TLT, PE, TE))
    tat = tlt + lane_sum(g * rows_dot(g, coarse_ref[...]))
    alpha = rz / pq
    rz_next = rz - 2.0 * alpha * pq + alpha * alpha * qmq
    grow = 1.0 + rz_next / rz
    pap = grow * grow * (pq + pe) - 2.0 * alpha * grow * (qmq + te) + alpha * alpha * tat
    alpha_next = rz_next / pap
    of_p, of_t = alpha + alpha_next * grow, -(alpha * alpha_next)
    adj_ref[:, 0, :] = of_p * keep_ref[KEEP_P : KEEP_P + 8] + of_t * t_ref[...]

    factors = [of_p * of_p, 2.0 * of_p * of_t, of_t * of_t]
    wide = [jnp.broadcast_to(f, (CASES, LANES)) for f in factors]
    splat = [[jnp.broadcast_to(f[c : c + 1], (8, LANES)) for c in range(CASES)] for f in wide]
    tiles = []
    for i in range(pt_ref.shape[0]):
        tile = None
        pp = early_ref.at[i] if i < EARLY else late_ref.at[i - EARLY]
        for ref, factor in zip((pp, pt_ref.at[i], tt_ref.at[i]), splat):
            for c in range(CASES):
                term = factor[c] * ref[c]
                tile = term if tile is None else tile + term
        tiles.append(tile)
    grad = jnp.concatenate(tiles, axis=0)
    column = jnp.concatenate(wide, axis=0)

    def combine(fields):
        return jnp.sum(column * fields, axis=0, keepdims=True)

    ex, ey = grad.shape
    x_odd, y_odd = is_odd("gx"), is_odd("gy")
    has = sides_there("gx") + sides_there("gy")

    def choose(flag, a, b):
        return jnp.where(jnp.broadcast_to(flag, a.shape), a, b)

    def two(a, b, flag):
        return choose(flag, a, b), choose(flag, b, a)

    def both(values, there):
        return [v * flag for v, flag in zip(values, there)]

    rows = [[combine(ref[FIELDS * i : FIELDS * (i + 1)]) for i in range(2)] for ref in (xe_ref, xo_ref)]
    g_below1, g_above1 = both(two(rows[0][0], rows[1][0], x_odd), has[:2])
    g_below2, g_above2 = both(two(rows[0][1], rows[1][1], x_odd), has[:2])
    before, after = both(two(combine(ye_ref[...]), combine(yo_ref[...]), y_odd), has[2:])
    col_low, col_high = two(combine(mine_ye_ref[...]), combine(mine_yo_ref[...]), y_odd)
    wide_lane = lax.broadcasted_iota(jnp.int32, (CASES, LANES), 1)
    of_lane = jnp.where(wide_lane < CORNER_PT, wide[0], jnp.where(wide_lane < CORNER_TT, wide[1], wide[2]))
    x, y = lax.axis_index("gx"), lax.axis_index("gy")
    nx, ny = lax.axis_size("gx"), lax.axis_size("gy")

    def corner_of(dx, dy, there, k):
        whose = jnp.clip(x + dx, 0, nx - 1) * ny + jnp.clip(y + dy, 0, ny - 1)
        row = jnp.sum(of_lane * got_ref[whose, CASES:, :], axis=0, keepdims=True)
        parts = [row[:, at + k : at + k + 1] for at in (CORNER_PP, CORNER_PT, CORNER_TT)]
        return there * (parts[0] + parts[1] + parts[2]) / diag

    corner = [corner_of(-1, -1, has[0] * has[2], 3), corner_of(-1, 1, has[0] * has[3], 2),
              corner_of(1, -1, has[1] * has[2], 1), corner_of(1, 1, has[1] * has[3], 0)]
    lane = lax.broadcasted_iota(jnp.int32, (1, LANES), 1)

    def shifted(row, low, high, length):
        left = jnp.where(lane == 0, low, pltpu.roll(row, 1, 1))
        right = jnp.where(lane == length - 1, high, pltpu.roll(row, LANES - 1, 1))
        return left + right

    def upper(row):
        return pltpu.roll(row, LANES - ex, 1)

    g_before1, g_before2 = upper(before), before
    g_after1, g_after2 = after, upper(after)
    col_first, col_last = col_low, upper(col_high)
    s_below1, s_above1 = g_below1 / diag, g_above1 / diag
    s_before1, s_after1 = g_before1 / diag, g_after1 / diag

    def ring(g1, g2, inner, beside, there):
        return there * (g1 + radius_sq * (g2 / diag + inner / diag + beside)) / diag

    n_below = ring(g_below1, g_below2, grad[0:1], shifted(s_below1, corner[0], corner[1], ey), has[0])
    n_above = ring(g_above1, g_above2, grad[ex - 1 :], shifted(s_above1, corner[2], corner[3], ey), has[1])
    n_before = ring(g_before1, g_before2, col_first, shifted(s_before1, corner[0], corner[2], ex), has[2])
    n_after = ring(g_after1, g_after2, col_last, shifted(s_after1, corner[1], corner[3], ex), has[3])
    stack = jnp.concatenate([s_before1, s_after1, n_before, n_after, jnp.zeros((4, LANES), F32)], axis=0)
    columns = jnp.transpose(stack)[:ex]
    row_no = lax.broadcasted_iota(jnp.int32, (ex, ey), 0)
    col_no = lax.broadcasted_iota(jnp.int32, (ex, ey), 1)

    def sweep(s, below_row, above_row, before_col, after_col):
        down = jnp.where(row_no == 0, below_row, pltpu.roll(s, 1, 0))
        up = jnp.where(row_no == ex - 1, above_row, pltpu.roll(s, ex - 1, 0))
        left = jnp.where(col_no == 0, before_col, pltpu.roll(s, 1, 1))
        right = jnp.where(col_no == ey - 1, after_col, pltpu.roll(s, ey - 1, 1))
        return (grad + radius_sq * (up + down + right + left)) / diag

    s = sweep(grad / diag, s_below1, s_above1, columns[:, 0:1], columns[:, 1:2])
    out_ref[...] = sweep(s, n_below, n_above, columns[:, 2:3], columns[:, 3:4])


def swaps(nx, ny, along_y):
    def number(along, across):
        return across * ny + along if along_y else along * ny + across

    size, other = (ny, nx) if along_y else (nx, ny)
    out = []
    for first in (0, 1):
        inner = [(i, i + 1) for i in range(first, size - 1, 2)]
        pairs = [(number(i, k), number(j, k)) for i, j in inner for k in range(other)]
        alone = [i for i in range(size) if not any(i in pair for pair in inner)]
        if inner and other % 2 == 0:
            pairs += [(number(i, k), number(i, k + 1)) for i in alone for k in range(0, other, 2)]
        out.append(pairs + [(b, a) for a, b in pairs])
    return out


def swap_over(array, pairs):
    return lax.ppermute(array, ("gx", "gy"), pairs) if pairs else jnp.zeros_like(array)


def f32(*shape):
    return jax.ShapeDtypeStruct(shape, F32)


def s32(*shape):
    return jax.ShapeDtypeStruct(shape, jnp.int32)


def bf16(*shape):
    return jax.ShapeDtypeStruct(shape, BF16)


def call(kernel, name, out_shape, in_specs, scratch, moved, in_hbm_too=(), extra=0):
    single = not isinstance(out_shape, tuple)
    return pl.pallas_call(
        kernel, out_shape=out_shape, in_specs=in_specs,
        out_specs=VMEM if single else tuple(HBM if i in in_hbm_too else VMEM for i in range(len(out_shape))),
        scratch_shapes=scratch, name=name,
        compiler_params=pltpu.CompilerParams(vmem_limit_bytes=LIMIT + extra),
        cost_estimate=pl.CostEstimate(flops=1_000_000, bytes_accessed=moved, transcendentals=0),
    )


LIMIT = 6 * 1024 * 1024


def on_device(loads, dual_op, iface, precond, corner_map, coarse_inv, elem_stiff, elem_dofs, density, passive):
    nx, ny = lax.axis_size("gx"), lax.axis_size("gy")
    everyone = nx * ny
    unknowns = dual_op.shape[-1]
    modes = corner_map.shape[1]
    ex, ey = density.shape
    tiles = ex // 8
    x_even, x_odd = swaps(nx, ny, False)
    y_even, y_odd = swaps(nx, ny, True)

    def held(array):
        return pltpu.VMEM(array.shape, array.dtype)

    def in_hbm(array):
        return pltpu.with_memory_space_constraint(array, pltpu.HBM)

    def copies(n):
        return pltpu.SemaphoreType.DMA((n,))

    stiff = pltpu.SMEM(elem_stiff.shape, F32)
    one_table = pltpu.VMEM((1, CASES, 8, 8, LANES), F32)
    one_gathered = pltpu.VMEM((1, 8, CASES, 8, LANES), F32)
    table = pltpu.VMEM((2, CASES, 8, 8, LANES), F32)
    gathered = pltpu.VMEM((2, 8, CASES, 8, LANES), F32)

    params = (loads, precond, corner_map, elem_dofs, density, passive)
    send, pack, weight, spot = call(
        first_kernel, "first",
        (pltpu.HBM((everyone, CASES, modes), F32), s32(8, 8, LANES), f32(tiles + 1, 8, LANES), f32(2, 8, LANES)),
        [HBM] * 6, [pltpu.VMEM((everyone, CASES, modes), F32)] + [held(a) for a in params] + [copies(10)], 5_000_000,
        in_hbm_too=(0,), extra=4 * everyone * CASES * modes,
    )(*(in_hbm(a) for a in params))
    got = lax.all_to_all(send, ("gx", "gy"), 0, 0)

    side = f32(SIDE_C + modes, R)
    params = (loads, dual_op, iface, precond, corner_map)
    keep, mine_e, mine_o, index, inverse, chigh, clow = call(
        side_kernel, "sides",
        (f32(KEEP_S + 8, unknowns), side, side, s32(2, 8, R), s32(2, 8, unknowns), bf16(modes, unknowns),
         bf16(modes, unknowns)),
        [HBM] * 5, [held(a) for a in params] + [copies(5)], 8_000_000,
    )(*(in_hbm(a) for a in params))
    theirs_o = swap_over(mine_o, x_odd)
    theirs_e = swap_over(mine_e, x_even)

    field = f32(EARLY + 1, CASES, 8, LANES)
    spot_kp, kp, pp = call(
        early_kernel, "early", (f32(9, 8, LANES), f32(EARLY + 1, 8, CASES, 8, LANES), field),
        [VMEM] * 5 + [HBM],
        [one_table, one_gathered, one_gathered, pltpu.VMEM((EARLY + 1, 8, 8, LANES), jnp.int32),
         pltpu.VMEM((EARLY + 1, 8, LANES), F32), stiff, copies(1)], 18_000_000,
    )(keep, elem_dofs, pack, weight, spot, in_hbm(elem_stiff))
    got, spot_kp = lax.optimization_barrier((got, spot_kp))

    row = f32(2 * FIELDS, LANES)
    col = f32(FIELDS, LANES)
    send, t, row_e, row_o, col_e, col_o = call(
        second_kernel, "second",
        (pltpu.HBM((everyone, 2 * CASES, modes), F32), f32(CASES, unknowns), row, row, col, col),
        [VMEM] * 17 + [HBM] * 3,
        [pltpu.VMEM((everyone, 2 * CASES, modes), F32), one_table, one_gathered, pltpu.VMEM((FIELDS, 8, LANES), F32),
         held(precond), held(dual_op), stiff, copies(4)], 10_000_000, in_hbm_too=(0,),
        extra=8 * everyone * CASES * modes,
    )(got, keep, mine_e, mine_o, theirs_e, theirs_o, index, inverse, spot, spot_kp, coarse_inv, chigh, clow,
      pack, weight, kp, pp, in_hbm(precond), in_hbm(dual_op), in_hbm(elem_stiff))
    got = lax.all_to_all(send, ("gx", "gy"), 0, 0)

    ye, yo = swap_over(col_e, y_even), swap_over(col_o, y_odd)
    xo = swap_over(row_o, x_odd)
    xe = swap_over(row_e, x_even)

    late, pt, tt = call(
        field_kernel, "fields",
        (f32(tiles - EARLY, CASES, 8, LANES), f32(tiles, CASES, 8, LANES), f32(tiles, CASES, 8, LANES)),
        [VMEM] * 5 + [HBM], [table, gathered, gathered, stiff, copies(1)], 36_000_000,
    )(keep, t, elem_dofs, weight, kp, in_hbm(elem_stiff))

    adjoint, sens = call(
        last_kernel, "last", (f32(CASES, 1, unknowns), f32(ex, ey)), [VMEM] * 14, [], 4_000_000,
    )(got, coarse_inv, keep, t, pp, late, pt, tt, col_e, col_o, xe, xo, ye, yo)
    return adjoint, sens


def solution(mesh):
    placed = (
        P(None, "gy", "gx"),
        P("gy", "gx", None),
        P("gy", "gx", None),
        P("gy", "gx"),
        P("gy", None, "gx"),
        P(),
        P(),
        P(None, "gx", "gy"),
        P("gx", "gy"),
        P("gx", "gy"),
    )
    return jax.shard_map(
        on_device,
        mesh=mesh,
        in_specs=placed,
        out_specs=(P(None, "gy", "gx"), P("gx", "gy")),
        check_vma=False,
    )
```

```python
import jax
import jax.numpy as jnp
from jax import lax
from jax.experimental import pallas as pl
from jax.experimental.pallas import tpu as pltpu
from jax.sharding import PartitionSpec as P

R = 128
LANES = 128
CASES = 8

coupling = 0.3
radius_sq = 2.0
penalty = 3.0
diag = 1.0 + 4.0 * radius_sq

HI = lax.Precision.HIGHEST
F32 = jnp.float32
BF16 = jnp.bfloat16
VMEM = pl.BlockSpec(memory_space=pltpu.VMEM)
HBM = pl.BlockSpec(memory_space=pltpu.HBM)

SIDE_P, SIDE_Y, SIDE_M, SIDE_C = 0, 8, 16, 24
RZ, PE, PQ, QMQ, TLT, TE = range(6)
KEEP_P, KEEP_Y, KEEP_REST, KEEP_S = 0, 8, 16, 24
FIELDS = 3 * CASES
EARLY = 5
CORNER_PP, CORNER_PT, CORNER_TT = 8, 12, 16


def rows_dot(a, b):
    return lax.dot_general(a, b, (((1,), (1,)), ((), ())), precision=HI, preferred_element_type=F32)


def plain_dot(a, b):
    return lax.dot_general(a, b, (((1,), (0,)), ((), ())), precision=HI, preferred_element_type=F32)


def halves(x):
    high = x.astype(BF16)
    low = (x - high.astype(F32)).astype(BF16)
    return jnp.concatenate([high, low], axis=0)


def split(x):
    high = x.astype(BF16)
    return high, (x - high.astype(F32)).astype(BF16)


def split_dot(a, pair, dim):
    stack = halves(a)
    dims = (((1,), (dim,)), ((), ()))
    main = lax.dot_general(stack, pair[0], dims, preferred_element_type=F32)
    rest = lax.dot_general(stack, pair[1], dims, preferred_element_type=F32)
    return main[:8] + main[8:] + rest[:8]


def lane_sum(x):
    return jnp.sum(x, axis=1, keepdims=True)


def pattern(idx):
    return idx & (LANES - 1), (idx & 128) != 0, (idx & 256) != 0, (idx & 512) != 0


def pick(blocks, where):
    lane, bit0, bit1, bit2 = where
    got = [jnp.take_along_axis(b, lane, axis=1, mode="promise_in_bounds") for b in blocks]
    got = [jnp.where(bit0, got[2 * i + 1], got[2 * i]) for i in range(4)]
    got = [jnp.where(bit1, got[2 * i + 1], got[2 * i]) for i in range(2)]
    return jnp.where(bit2, got[1], got[0])


def blocks_of(row8):
    return [row8[:, LANES * h : LANES * (h + 1)] for h in range(8)]


def is_odd(axis):
    return lax.axis_index(axis) & 1 == 1


def sides_there(axis):
    at, size = lax.axis_index(axis), lax.axis_size(axis)
    return jnp.where(at > 0, 1.0, 0.0), jnp.where(at < size - 1, 1.0, 0.0)


def op_dot(vec, op_ref):
    out = lax.dot_general(halves(vec), op_ref[0], (((1,), (1,)), ((), ())), preferred_element_type=F32)
    return out[:CASES], out[CASES:]


def at_lanes(columns, first=0):
    lane = lax.broadcasted_iota(jnp.int32, (CASES, LANES), 1)
    block = jnp.zeros((CASES, LANES), F32)
    for j, column in enumerate(columns):
        block = jnp.where(lane == first + j, column, block)
    return block


def fetch(sems, pairs):
    copies = [pltpu.make_async_copy(a, b, sems.at[i]) for i, (a, b) in enumerate(pairs)]
    for copy in copies:
        copy.start()
    return copies


def to_row(g, block):
    tails = []
    for r in range(2):
        tail = block[4 * r : 4 * r + 1]
        for c in range(1, 4):
            tail = tail + pltpu.roll(block[4 * r + c : 4 * r + c + 1], 32 * c, 1)
        tails.append(tail)
    return jnp.concatenate([g[c : c + 1] for c in range(CASES)] + tails, axis=1)


def block_of(tails):
    rows = []
    for c in range(CASES):
        tail = tails[:, LANES * (c // 4) : LANES * (c // 4 + 1)]
        rows.append(pltpu.roll(tail, (LANES - 32 * (c % 4)) % LANES, 1))
    return jnp.concatenate(rows, axis=0)


def edge_tiles(first, second):
    ex, ey = first.shape
    lane = lax.broadcasted_iota(jnp.int32, (1, LANES), 1)
    turned = jnp.transpose(jnp.concatenate([first, second], axis=0))
    swapped = pltpu.roll(turned, LANES - ex, 1)
    out = []
    for array, low, high in ((first, turned, swapped), (second, swapped, turned)):
        cols = [jnp.where(lane < ex, low[j : j + 1], high[j + 1 : j + 2]) for j in (0, ey - 2)]
        out.append(jnp.concatenate([array[0:2], array[ex - 2 :]] + cols + [array[0:2]], axis=0))
    return out


def corner_lanes(low, high):
    lane = lax.broadcasted_iota(jnp.int32, low.shape, 1)
    out = jnp.where(lane == 0, low, jnp.where(lane == 1, pltpu.roll(low, 2, 1), 0))
    return jnp.where(lane == 2, pltpu.roll(high, 2, 1), jnp.where(lane == 3, pltpu.roll(high, 4, 1), out))


def corner_values(vec, where):
    return [pick(blocks_of(vec), pattern(jnp.broadcast_to(where[a : a + 1], (8, LANES)))) for a in range(8)]


def first_kernel(loads_hbm, pre_hbm, corner_hbm, dofs_hbm, density_hbm, passive_hbm,
                 send_hbm, pack_ref, weight_ref, spot_ref,
                 send_ref, loads_ref, pre_ref, corner_ref, dofs_ref, density_ref, passive_ref, sems):
    piece = corner_ref.shape[2] // 4
    parts = [pl.ds(piece * i, piece) for i in range(4)]
    copies = fetch(sems, [(loads_hbm, loads_ref), (pre_hbm, pre_ref)]
                   + [(corner_hbm.at[:, :, k], corner_ref.at[:, :, k]) for k in parts]
                   + [(dofs_hbm, dofs_ref), (density_hbm, density_ref), (passive_hbm, passive_ref)])
    copies[0].wait()
    copies[1].wait()
    p = pre_ref[...] * loads_ref[:, 0, :]
    part = None
    for i, k in enumerate(parts):
        copies[2 + i].wait()
        term = split_dot(p[:, piece * i : piece * (i + 1)], split(corner_ref[0, :, k]), 1)
        part = term if part is None else part + term
    for d in range(send_ref.shape[0]):
        send_ref[d] = part
    out = pltpu.make_async_copy(send_ref, send_hbm, sems.at[9])
    out.start()
    for copy in copies[6:]:
        copy.wait()
    for a in range(0, 8, 2):
        first, second = edge_tiles(dofs_ref[a].astype(F32), dofs_ref[a + 1].astype(F32))
        pack_ref[a] = first.astype(jnp.int32)
        pack_ref[a + 1] = second.astype(jnp.int32)
    rho = density_ref[...]
    weight = jnp.where(passive_ref[...] == 1, 0.0, -penalty * rho * rho)
    ex = weight.shape[0]
    for i in range(ex // 8):
        weight_ref[i] = weight[8 * i : 8 * i + 8]
    weight_ref[ex // 8] = edge_tiles(weight, weight)[0]
    spot_ref[0] = corner_lanes(dofs_ref[:, 0, :], dofs_ref[:, ex - 1, :]).astype(F32)
    spot_ref[1] = jnp.broadcast_to(corner_lanes(weight[0:1], weight[ex - 1 :]), (8, LANES))
    out.wait()


def stiff_row(stiff_ref, a, u):
    v = stiff_ref[a, 0] * u[0]
    for b in range(1, 8):
        v = v + stiff_ref[a, b] * u[b]
    return v


def side_indices(iface_ref):
    left = jnp.broadcast_to(iface_ref[0, :, :R], (8, R))
    right = jnp.broadcast_to(iface_ref[0, :, R : 2 * R], (8, R))
    x_odd = jnp.broadcast_to(is_odd("gx"), (8, R))
    return jnp.where(x_odd, left, right), jnp.where(x_odd, right, left)


def side_kernel(loads_hbm, op_hbm, iface_hbm, pre_hbm, corner_hbm,
                keep_ref, even_ref, odd_ref, index_ref, inverse_ref, chigh_ref, clow_ref,
                loads_ref, op_ref, iface_ref, pre_ref, corner_ref, sems):
    copies = fetch(sems, ((loads_hbm, loads_ref), (pre_hbm, pre_ref), (iface_hbm, iface_ref),
                          (corner_hbm, corner_ref), (op_hbm, op_ref)))
    for copy in copies[:4]:
        copy.wait()
    loads = loads_ref[:, 0, :]
    p = pre_ref[...] * loads
    keep_ref[KEEP_P : KEEP_P + 8] = p
    pre = jnp.broadcast_to(pre_ref[...], (8, pre_ref.shape[1]))
    chosen = []
    for idx, out in zip(side_indices(iface_ref), (even_ref, odd_ref)):
        where = pattern(idx)
        scale = pick(blocks_of(pre), where)
        chosen.append((where, scale, out))
        out[SIDE_P : SIDE_P + 8] = pick(blocks_of(p), where)
        out[SIDE_M : SIDE_M + 8] = scale
        for j in range(corner_ref.shape[1] // 8):
            rows = corner_ref[0, 8 * j : 8 * j + 8]
            out[SIDE_C + 8 * j : SIDE_C + 8 * j + 8] = scale * pick(blocks_of(rows), where)
    for side, idx in enumerate(side_indices(iface_ref)):
        index_ref[side] = idx
        column = jnp.transpose(jnp.broadcast_to(idx[0:1], (R, R)))
        number = lax.broadcasted_iota(jnp.int32, (R, LANES), 0) + 1
        for h in range(8):
            at = lax.broadcasted_iota(jnp.int32, (R, LANES), 1) + LANES * h
            found = jnp.sum(jnp.where(column == at, number, 0), axis=0, keepdims=True)
            inverse_ref[side, :, LANES * h : LANES * (h + 1)] = jnp.broadcast_to(found, (8, LANES))
    chigh_ref[...], clow_ref[...] = split(corner_ref[0])
    copies[4].wait()
    y, rest = op_dot(p, op_ref)
    keep_ref[KEEP_Y : KEEP_Y + 8] = y
    keep_ref[KEEP_REST : KEEP_REST + 8] = rest
    keep_ref[KEEP_S : KEEP_S + 8, :LANES] = at_lanes((lane_sum(loads * p), lane_sum(p * rest)))
    for where, scale, out in chosen:
        out[SIDE_Y : SIDE_Y + 8] = scale * pick(blocks_of(y), where)


def early_kernel(keep_ref, dofs_ref, pack_ref, weight_ref, spot_ref, stiff_hbm, spot_kp_ref,
                 kp_ref, pp_ref, table_ref, u_ref, other_ref, all_dofs_ref, all_weight_ref,
                 stiff_ref, sems):
    copies = fetch(sems, ((stiff_hbm, stiff_ref),))
    p = keep_ref[KEEP_P : KEEP_P + 8]
    make_tables(table_ref, p)
    for i in range(EARLY):
        for a in range(8):
            all_dofs_ref[i, a] = dofs_ref[a, 8 * i : 8 * i + 8]
        all_weight_ref[i] = weight_ref[i]
    for a in range(8):
        all_dofs_ref[EARLY, a] = pack_ref[a]
    all_weight_ref[EARLY] = weight_ref[weight_ref.shape[0] - 1]

    def gather(i, ref):
        gather_tile(lambda a: all_dofs_ref[i, a], table_ref, ref, 0)

    def fields(i, ref):
        scale = all_weight_ref[i]
        for c in range(CASES):
            u = [ref[0, a, c] for a in range(8)]
            pp = None
            for a in range(8):
                v = stiff_row(stiff_ref, a, u)
                kp_ref[i, a, c] = v
                pp = u[a] * v if pp is None else pp + u[a] * v
            pp_ref[i, c] = scale * pp

    staggered(EARLY + 1, gather, fields, (u_ref, other_ref), copies)
    spot_weight = spot_ref[1]
    u = corner_values(p, spot_ref[0].astype(jnp.int32))
    pp = None
    for a in range(8):
        v = stiff_row(stiff_ref, a, u)
        spot_kp_ref[a] = spot_weight * v
        pp = u[a] * v if pp is None else pp + u[a] * v
    lane = lax.broadcasted_iota(jnp.int32, (CASES, LANES), 1)
    spot_kp_ref[8] = pltpu.roll(jnp.where(lane < 4, spot_weight * pp, 0.0), CORNER_PP, 1)


def spread(values, inverse):
    out = []
    for h in range(8):
        at = inverse[:, LANES * h : LANES * (h + 1)]
        got = jnp.take_along_axis(values, jnp.maximum(at - 1, 0), axis=1, mode="promise_in_bounds")
        out.append(jnp.where(at > 0, got, 0.0))
    return jnp.concatenate(out, axis=1)


def second_kernel(got_ref, keep_ref, mine_e_ref, mine_o_ref, theirs_e_ref, theirs_o_ref, index_ref, inverse_ref,
                  spot_ref, spot_kp_ref, coarse_ref, chigh_ref, clow_ref, pack_ref, weight_ref, kp_ref, pp_ref,
                  pre_hbm, op_hbm, stiff_hbm,
                  send_hbm, t_ref, row_e_ref, row_o_ref, col_e_ref, col_o_ref,
                  send_ref, table_ref, u_ref, field_ref, pre_ref, op_ref, stiff_ref, sems):
    copies = fetch(sems, ((pre_hbm, pre_ref), (stiff_hbm, stiff_ref), (op_hbm, op_ref)))
    total = got_ref[0]
    for d in range(1, got_ref.shape[0]):
        total = total + got_ref[d]
    corner = chigh_ref[...], clow_ref[...]
    p = keep_ref[KEEP_P : KEEP_P + 8]
    base = keep_ref[KEEP_Y : KEEP_Y + 8]
    pairs = ((mine_e_ref, theirs_e_ref), (mine_o_ref, theirs_o_ref))
    below, above = sides_there("gx")
    x_odd = is_odd("gx")
    couplings = [-coupling * jnp.where(x_odd, a, b) for a, b in ((below, above), (above, below))]
    for side, (_, theirs) in enumerate(pairs):
        base = base + spread(couplings[side] * theirs[SIDE_P : SIDE_P + 8], inverse_ref[side])
    w = split_dot(total, split(coarse_ref[...]), 1)
    q = base + split_dot(w, corner, 0)
    copies[0].wait()
    t = pre_ref[...] * q
    t_ref[...] = t
    g = split_dot(t, corner, 1)
    tlt = None
    for side, (mine, theirs) in enumerate(pairs):
        t_mine = pick(blocks_of(t), pattern(index_ref[side]))
        t_theirs = theirs[SIDE_Y : SIDE_Y + 8] - coupling * theirs[SIDE_M : SIDE_M + 8] * mine[SIDE_P : SIDE_P + 8]
        t_theirs = t_theirs + split_dot(w, split(theirs[SIDE_C:]), 0)
        term = couplings[side] * lane_sum(t_mine * t_theirs)
        tlt = term if tlt is None else tlt + term
    copies[1].wait()
    u = corner_values(t, spot_ref[0].astype(jnp.int32))
    pt = tt = None
    for a in range(8):
        one, two = u[a] * spot_kp_ref[a], u[a] * stiff_row(stiff_ref, a, u)
        pt, tt = (one, two) if pt is None else (pt + one, tt + two)
    lane = lax.broadcasted_iota(jnp.int32, (CASES, LANES), 1)
    pt, tt = jnp.where(lane < 4, pt, 0.0), jnp.where(lane < 4, spot_ref[1] * tt, 0.0)
    rest = keep_ref[KEEP_REST : KEEP_REST + 8]
    block = keep_ref[KEEP_S : KEEP_S + 8, :LANES]
    block = block + spot_kp_ref[8] + pltpu.roll(pt, CORNER_PT, 1) + pltpu.roll(tt, CORNER_TT, 1)
    block = block + at_lanes((lane_sum(p * q), lane_sum(q * t), tlt, lane_sum(t * rest)), PQ)
    copies[2].wait()
    high, low = op_dot(t, op_ref)
    block = block + at_lanes((lane_sum(t * (high + low)),), TLT)
    row = to_row(g, block)
    for d in range(send_ref.shape[0]):
        send_ref[d] = row
    out = pltpu.make_async_copy(send_ref, send_hbm, sems.at[3])
    out.start()
    edge_fields(t, pack_ref, weight_ref, kp_ref, pp_ref, row_e_ref, row_o_ref, col_e_ref, col_o_ref,
                table_ref, u_ref, field_ref, stiff_ref)
    out.wait()


def make_tables(table_ref, *vectors):
    for i, vec in enumerate(vectors):
        for c in range(CASES):
            for h in range(8):
                row = vec[c : c + 1, LANES * h : LANES * (h + 1)]
                table_ref[i, c, h] = jnp.broadcast_to(row, (8, LANES))


def gather_tile(dofs, table_ref, u_ref, *which):
    for a in range(8):
        where = pattern(dofs(a))
        for c in range(CASES):
            for i in which:
                u_ref[i, a, c] = pick([table_ref[i, c, h] for h in range(8)], where)


def staggered(count, gather, fields, refs, ready=()):
    gather(0, refs[0])
    for copy in ready:
        copy.wait()
    pairs = (count - 1) // 2

    @pl.loop(0, pairs)
    def _(k):
        i = 2 * k
        gather(i + 1, refs[1])
        fields(i, refs[0])
        gather(i + 2, refs[0])
        fields(i + 1, refs[1])

    if count % 2 == 0:
        gather(count - 1, refs[1])
        fields(count - 2, refs[0])
        fields(count - 1, refs[1])
    else:
        fields(count - 1, refs[0])


def t_fields(t, kp, stiff_ref):
    pt = tt = None
    for a in range(8):
        w = stiff_ref[a, a] * t[a]
        for b in range(a + 1, 8):
            w = w + (stiff_ref[a, b] + stiff_ref[b, a]) * t[b]
        one, two = t[a] * kp[a], t[a] * w
        pt, tt = (one, two) if pt is None else (pt + one, tt + two)
    return pt, tt


def edge_fields(t, pack_ref, weight_ref, kp_ref, pp_ref, row_e_ref, row_o_ref, col_e_ref, col_o_ref,
                table_ref, u_ref, field_ref, stiff_ref):
    make_tables(table_ref, t)
    gather_tile(lambda a: pack_ref[a], table_ref, u_ref, 0)
    scale = weight_ref[weight_ref.shape[0] - 1]
    for c in range(CASES):
        pt, tt = t_fields([u_ref[0, a, c] for a in range(8)], [kp_ref[EARLY, a, c] for a in range(8)], stiff_ref)
        field_ref[c] = pp_ref[EARLY, c]
        field_ref[CASES + c] = scale * pt
        field_ref[2 * CASES + c] = scale * tt
    x_odd = jnp.broadcast_to(is_odd("gx"), (FIELDS, LANES))
    y_odd = jnp.broadcast_to(is_odd("gy"), (FIELDS, LANES))
    for i in range(2):
        low, high = field_ref[:, i, :], field_ref[:, 3 - i, :]
        row_e_ref[FIELDS * i : FIELDS * (i + 1)] = jnp.where(x_odd, low, high)
        row_o_ref[FIELDS * i : FIELDS * (i + 1)] = jnp.where(x_odd, high, low)
    low, high = field_ref[:, 4, :], field_ref[:, 5, :]
    col_e_ref[...] = jnp.where(y_odd, low, high)
    col_o_ref[...] = jnp.where(y_odd, high, low)


def field_kernel(keep_ref, t_ref, dofs_ref, weight_ref, kp_ref, stiff_hbm, pp_ref, pt_ref, tt_ref,
                 table_ref, u_ref, other_ref, stiff_ref, sems):
    copies = fetch(sems, ((stiff_hbm, stiff_ref),))
    make_tables(table_ref, t_ref[...], keep_ref[KEEP_P : KEEP_P + 8])

    def rows_of(tile):
        return pl.ds(pl.multiple_of(8 * tile, 8), 8)

    def t_at(ref, c):
        return [ref[0, a, c] for a in range(8)]

    def gather(tile, ref):
        gather_tile(lambda a: dofs_ref[a, rows_of(tile), :], table_ref, ref, 0)

    def fields(tile, ref):
        scale = weight_ref[tile]
        for c in range(CASES):
            pt, tt = t_fields(t_at(ref, c), [kp_ref[tile, a, c] for a in range(8)], stiff_ref)
            pt_ref[tile, c], tt_ref[tile, c] = scale * pt, scale * tt

    staggered(EARLY, gather, fields, (u_ref, other_ref), copies)

    def gather_both(i, ref):
        gather_tile(lambda a: dofs_ref[a, rows_of(i + EARLY), :], table_ref, ref, 0, 1)

    def fields_both(i, ref):
        scale = weight_ref[i + EARLY]
        for c in range(CASES):
            p = [ref[1, a, c] for a in range(8)]
            kp = [stiff_row(stiff_ref, a, p) for a in range(8)]
            pp = p[0] * kp[0]
            for a in range(1, 8):
                pp = pp + p[a] * kp[a]
            pt, tt = t_fields(t_at(ref, c), kp, stiff_ref)
            pp_ref[i, c], pt_ref[i + EARLY, c], tt_ref[i + EARLY, c] = scale * pp, scale * pt, scale * tt

    staggered(pt_ref.shape[0] - EARLY, gather_both, fields_both, (u_ref, other_ref))


def last_kernel(got_ref, coarse_ref, keep_ref, t_ref, early_ref, late_ref, pt_ref, tt_ref,
                mine_ye_ref, mine_yo_ref, xe_ref, xo_ref, ye_ref, yo_ref,
                adj_ref, out_ref):
    total = jnp.sum(got_ref[:, 0, :], axis=0, keepdims=True)
    g = jnp.concatenate([total[:, LANES * c : LANES * (c + 1)] for c in range(CASES)], axis=0)
    s = block_of(total[:, LANES * CASES :])
    rz, pq, qmq, tlt, pe, te = (s[:, j : j + 1] for j in (RZ, PQ, QMQ, TLT, PE, TE))
    tat = tlt + lane_sum(g * rows_dot(g, coarse_ref[...]))
    alpha = rz / pq
    rz_next = rz - 2.0 * alpha * pq + alpha * alpha * qmq
    grow = 1.0 + rz_next / rz
    pap = grow * grow * (pq + pe) - 2.0 * alpha * grow * (qmq + te) + alpha * alpha * tat
    alpha_next = rz_next / pap
    of_p, of_t = alpha + alpha_next * grow, -(alpha * alpha_next)
    adj_ref[:, 0, :] = of_p * keep_ref[KEEP_P : KEEP_P + 8] + of_t * t_ref[...]

    factors = [of_p * of_p, 2.0 * of_p * of_t, of_t * of_t]
    wide = [jnp.broadcast_to(f, (CASES, LANES)) for f in factors]
    splat = [[jnp.broadcast_to(f[c : c + 1], (8, LANES)) for c in range(CASES)] for f in wide]
    tiles = []
    for i in range(pt_ref.shape[0]):
        tile = None
        pp = early_ref.at[i] if i < EARLY else late_ref.at[i - EARLY]
        for ref, factor in zip((pp, pt_ref.at[i], tt_ref.at[i]), splat):
            for c in range(CASES):
                term = factor[c] * ref[c]
                tile = term if tile is None else tile + term
        tiles.append(tile)
    grad = jnp.concatenate(tiles, axis=0)
    column = jnp.concatenate(wide, axis=0)

    def combine(fields):
        return jnp.sum(column * fields, axis=0, keepdims=True)

    ex, ey = grad.shape
    x_odd, y_odd = is_odd("gx"), is_odd("gy")
    has = sides_there("gx") + sides_there("gy")

    def choose(flag, a, b):
        return jnp.where(jnp.broadcast_to(flag, a.shape), a, b)

    def two(a, b, flag):
        return choose(flag, a, b), choose(flag, b, a)

    def both(values, there):
        return [v * flag for v, flag in zip(values, there)]

    rows = [[combine(ref[FIELDS * i : FIELDS * (i + 1)]) for i in range(2)] for ref in (xe_ref, xo_ref)]
    g_below1, g_above1 = both(two(rows[0][0], rows[1][0], x_odd), has[:2])
    g_below2, g_above2 = both(two(rows[0][1], rows[1][1], x_odd), has[:2])
    before, after = both(two(combine(ye_ref[...]), combine(yo_ref[...]), y_odd), has[2:])
    col_low, col_high = two(combine(mine_ye_ref[...]), combine(mine_yo_ref[...]), y_odd)
    wide_lane = lax.broadcasted_iota(jnp.int32, (CASES, LANES), 1)
    of_lane = jnp.where(wide_lane < CORNER_PT, wide[0], jnp.where(wide_lane < CORNER_TT, wide[1], wide[2]))
    x, y = lax.axis_index("gx"), lax.axis_index("gy")
    nx, ny = lax.axis_size("gx"), lax.axis_size("gy")

    def corner_of(dx, dy, there, k):
        whose = jnp.clip(x + dx, 0, nx - 1) * ny + jnp.clip(y + dy, 0, ny - 1)
        row = jnp.sum(of_lane * block_of(got_ref[whose, :, LANES * CASES :]), axis=0, keepdims=True)
        parts = [row[:, at + k : at + k + 1] for at in (CORNER_PP, CORNER_PT, CORNER_TT)]
        return there * (parts[0] + parts[1] + parts[2]) / diag

    corner = [corner_of(-1, -1, has[0] * has[2], 3), corner_of(-1, 1, has[0] * has[3], 2),
              corner_of(1, -1, has[1] * has[2], 1), corner_of(1, 1, has[1] * has[3], 0)]
    lane = lax.broadcasted_iota(jnp.int32, (1, LANES), 1)

    def shifted(row, low, high, length):
        left = jnp.where(lane == 0, low, pltpu.roll(row, 1, 1))
        right = jnp.where(lane == length - 1, high, pltpu.roll(row, LANES - 1, 1))
        return left + right

    def upper(row):
        return pltpu.roll(row, LANES - ex, 1)

    g_before1, g_before2 = upper(before), before
    g_after1, g_after2 = after, upper(after)
    col_first, col_last = col_low, upper(col_high)
    s_below1, s_above1 = g_below1 / diag, g_above1 / diag
    s_before1, s_after1 = g_before1 / diag, g_after1 / diag

    def ring(g1, g2, inner, beside, there):
        return there * (g1 + radius_sq * (g2 / diag + inner / diag + beside)) / diag

    n_below = ring(g_below1, g_below2, grad[0:1], shifted(s_below1, corner[0], corner[1], ey), has[0])
    n_above = ring(g_above1, g_above2, grad[ex - 1 :], shifted(s_above1, corner[2], corner[3], ey), has[1])
    n_before = ring(g_before1, g_before2, col_first, shifted(s_before1, corner[0], corner[2], ex), has[2])
    n_after = ring(g_after1, g_after2, col_last, shifted(s_after1, corner[1], corner[3], ex), has[3])
    stack = jnp.concatenate([s_before1, s_after1, n_before, n_after, jnp.zeros((4, LANES), F32)], axis=0)
    columns = jnp.transpose(stack)[:ex]
    row_no = lax.broadcasted_iota(jnp.int32, (ex, ey), 0)
    col_no = lax.broadcasted_iota(jnp.int32, (ex, ey), 1)

    def sweep(s, below_row, above_row, before_col, after_col):
        down = jnp.where(row_no == 0, below_row, pltpu.roll(s, 1, 0))
        up = jnp.where(row_no == ex - 1, above_row, pltpu.roll(s, ex - 1, 0))
        left = jnp.where(col_no == 0, before_col, pltpu.roll(s, 1, 1))
        right = jnp.where(col_no == ey - 1, after_col, pltpu.roll(s, ey - 1, 1))
        return (grad + radius_sq * (up + down + right + left)) / diag

    s = sweep(grad / diag, s_below1, s_above1, columns[:, 0:1], columns[:, 1:2])
    out_ref[...] = sweep(s, n_below, n_above, columns[:, 2:3], columns[:, 3:4])


def swaps(nx, ny, along_y):
    def number(along, across):
        return across * ny + along if along_y else along * ny + across

    size, other = (ny, nx) if along_y else (nx, ny)
    out = []
    for first in (0, 1):
        inner = [(i, i + 1) for i in range(first, size - 1, 2)]
        pairs = [(number(i, k), number(j, k)) for i, j in inner for k in range(other)]
        alone = [i for i in range(size) if not any(i in pair for pair in inner)]
        if inner and other % 2 == 0:
            pairs += [(number(i, k), number(i, k + 1)) for i in alone for k in range(0, other, 2)]
        out.append(pairs + [(b, a) for a, b in pairs])
    return out


def swap_over(array, pairs):
    return lax.ppermute(array, ("gx", "gy"), pairs) if pairs else jnp.zeros_like(array)


def f32(*shape):
    return jax.ShapeDtypeStruct(shape, F32)


def s32(*shape):
    return jax.ShapeDtypeStruct(shape, jnp.int32)


def bf16(*shape):
    return jax.ShapeDtypeStruct(shape, BF16)


def call(kernel, name, out_shape, in_specs, scratch, moved, in_hbm_too=(), extra=0):
    single = not isinstance(out_shape, tuple)
    return pl.pallas_call(
        kernel, out_shape=out_shape, in_specs=in_specs,
        out_specs=VMEM if single else tuple(HBM if i in in_hbm_too else VMEM for i in range(len(out_shape))),
        scratch_shapes=scratch, name=name,
        compiler_params=pltpu.CompilerParams(vmem_limit_bytes=LIMIT + extra),
        cost_estimate=pl.CostEstimate(flops=1_000_000, bytes_accessed=moved, transcendentals=0),
    )


LIMIT = 6 * 1024 * 1024


def on_device(loads, dual_op, iface, precond, corner_map, coarse_inv, elem_stiff, elem_dofs, density, passive):
    nx, ny = lax.axis_size("gx"), lax.axis_size("gy")
    everyone = nx * ny
    unknowns = dual_op.shape[-1]
    modes = corner_map.shape[1]
    ex, ey = density.shape
    tiles = ex // 8
    x_even, x_odd = swaps(nx, ny, False)
    y_even, y_odd = swaps(nx, ny, True)

    def held(array):
        return pltpu.VMEM(array.shape, array.dtype)

    def in_hbm(array):
        return pltpu.with_memory_space_constraint(array, pltpu.HBM)

    def copies(n):
        return pltpu.SemaphoreType.DMA((n,))

    stiff = pltpu.SMEM(elem_stiff.shape, F32)
    one_table = pltpu.VMEM((1, CASES, 8, 8, LANES), F32)
    one_gathered = pltpu.VMEM((1, 8, CASES, 8, LANES), F32)
    table = pltpu.VMEM((2, CASES, 8, 8, LANES), F32)
    gathered = pltpu.VMEM((2, 8, CASES, 8, LANES), F32)

    params = (loads, precond, corner_map, elem_dofs, density, passive)
    send, pack, weight, spot = call(
        first_kernel, "first",
        (pltpu.HBM((everyone, CASES, modes), F32), s32(8, 8, LANES), f32(tiles + 1, 8, LANES), f32(2, 8, LANES)),
        [HBM] * 6, [pltpu.VMEM((everyone, CASES, modes), F32)] + [held(a) for a in params] + [copies(10)], 5_000_000,
        in_hbm_too=(0,), extra=4 * everyone * CASES * modes,
    )(*(in_hbm(a) for a in params))
    got = lax.all_to_all(send, ("gx", "gy"), 0, 0)

    side = f32(SIDE_C + modes, R)
    params = (loads, dual_op, iface, precond, corner_map)
    keep, mine_e, mine_o, index, inverse, chigh, clow = call(
        side_kernel, "sides",
        (f32(KEEP_S + 8, unknowns), side, side, s32(2, 8, R), s32(2, 8, unknowns), bf16(modes, unknowns),
         bf16(modes, unknowns)),
        [HBM] * 5, [held(a) for a in params] + [copies(5)], 8_000_000,
    )(*(in_hbm(a) for a in params))
    theirs_o = swap_over(mine_o, x_odd)
    theirs_e = swap_over(mine_e, x_even)

    field = f32(EARLY + 1, CASES, 8, LANES)
    spot_kp, kp, pp = call(
        early_kernel, "early", (f32(9, 8, LANES), f32(EARLY + 1, 8, CASES, 8, LANES), field),
        [VMEM] * 5 + [HBM],
        [one_table, one_gathered, one_gathered, pltpu.VMEM((EARLY + 1, 8, 8, LANES), jnp.int32),
         pltpu.VMEM((EARLY + 1, 8, LANES), F32), stiff, copies(1)], 18_000_000,
    )(keep, elem_dofs, pack, weight, spot, in_hbm(elem_stiff))
    got, spot_kp = lax.optimization_barrier((got, spot_kp))

    row = f32(2 * FIELDS, LANES)
    col = f32(FIELDS, LANES)
    send, t, row_e, row_o, col_e, col_o = call(
        second_kernel, "second",
        (pltpu.HBM((everyone, 1, (CASES + 2) * modes), F32), f32(CASES, unknowns), row, row, col, col),
        [VMEM] * 17 + [HBM] * 3,
        [pltpu.VMEM((everyone, 1, (CASES + 2) * modes), F32), one_table, one_gathered, pltpu.VMEM((FIELDS, 8, LANES), F32),
         held(precond), held(dual_op), stiff, copies(4)], 10_000_000, in_hbm_too=(0,),
        extra=8 * everyone * CASES * modes,
    )(got, keep, mine_e, mine_o, theirs_e, theirs_o, index, inverse, spot, spot_kp, coarse_inv, chigh, clow,
      pack, weight, kp, pp, in_hbm(precond), in_hbm(dual_op), in_hbm(elem_stiff))
    got = lax.all_to_all(send, ("gx", "gy"), 0, 0)

    ye, yo = swap_over(col_e, y_even), swap_over(col_o, y_odd)
    xo = swap_over(row_o, x_odd)
    xe = swap_over(row_e, x_even)

    late, pt, tt = call(
        field_kernel, "fields",
        (f32(tiles - EARLY, CASES, 8, LANES), f32(tiles, CASES, 8, LANES), f32(tiles, CASES, 8, LANES)),
        [VMEM] * 5 + [HBM], [table, gathered, gathered, stiff, copies(1)], 36_000_000,
    )(keep, t, elem_dofs, weight, kp, in_hbm(elem_stiff))

    adjoint, sens = call(
        last_kernel, "last", (f32(CASES, 1, unknowns), f32(ex, ey)), [VMEM] * 14, [], 4_000_000,
    )(got, coarse_inv, keep, t, pp, late, pt, tt, col_e, col_o, xe, xo, ye, yo)
    return adjoint, sens


def solution(mesh):
    placed = (
        P(None, "gy", "gx"),
        P("gy", "gx", None),
        P("gy", "gx", None),
        P("gy", "gx"),
        P("gy", None, "gx"),
        P(),
        P(),
        P(None, "gx", "gy"),
        P("gx", "gy"),
        P("gx", "gy"),
    )
    return jax.shard_map(
        on_device,
        mesh=mesh,
        in_specs=placed,
        out_specs=(P(None, "gy", "gx"), P("gx", "gy")),
        check_vma=False,
    )
```
